128 devices in a mesh: rep: 8 (over z, core), tensor: 16 (over y, x).
Axes of the slice: x: 4, y: 4, z: 4, core: 2. Of those that a mesh axis runs over, the one named last changes fastest.
Arguments:
- x_pre: bfloat16 [8192, 2560], P(('rep', 'tensor')), may hold values from -6 to 6
- x_dec: bfloat16 [16, 2560], replicated, may hold values from -6 to 6
- prefix_kv: bfloat16 [8, 4096, 32, 160], P('rep', None, 'tensor'), may hold values from -400 to 400
- cache_kv: bfloat16 [16, 4096, 32, 160], P(None, 'rep', 'tensor'), may hold values from -400 to 400
- dec_len: int32 [16], replicated, may hold values from 1 to 4096, as said below
- offsets: int32 [8], P('rep'), may hold values from 0 to 4096, as said below
- segments: int32 [8, 1024], P('rep'), may hold values from 0 to 3, never falling along the last dimension, each value on 1 to 512 neighbouring positions
- w_qkv: bfloat16 [2560, 7680], P(None, 'tensor'), may hold values from -0.125 to 0.125
- w_out: bfloat16 [2560, 2560], P('tensor'), may hold values from -0.125 to 0.125
- w_up: bfloat16 [2560, 10240], P(None, 'tensor'), may hold values from -0.125 to 0.125
- up_bias: float32 [10240], P('tensor'), may hold values from -3 to 3
- w_down: bfloat16 [10240, 2560], P('tensor'), may hold values from -0.0625 to 0.0625
- biases: float32 [2, 2560], replicated, may hold values from -3 to 3
- gains: float32 [2, 2560], replicated, may hold values from 0.1 to 1.9
- shifts: float32 [2, 2560], replicated, may hold values from -2.5 to 2.5
- w_next: bfloat16 [2560, 7680], P(None, 'tensor'), may hold values from -0.125 to 0.125
Outputs:
- layer_out: bfloat16 [8192, 2560], P(('rep', 'tensor'))
- next_qkv: bfloat16 [8192, 7680], P('rep', 'tensor')
- dec_out: bfloat16 [16, 2560], replicated
- dec_next_qkv: bfloat16 [16, 7680], P(None, 'tensor')
The draws below stay inside these ranges and needn't reach their ends.
Inputs may be any that keep to these rules, and one draw needn't show every extreme that they name: Request r's cache holds live entries at positions below dec_len[r]; in every draw one request's cache is full (4096) and one request has a single live position. `offsets`: in every draw one span has a full earlier cache (4096 positions) and one span has none.
All inputs are finite; a program needn't handle non-finite values.
Results may differ from the reference program's by a relative error of at most 0.025.
Values may be sent and summed in bfloat16 or wider, within the bound.
A program may use at most 192 MiB of HBM per device.

```python
import math
import jax
import jax.numpy as jnp
import numpy as np
from jax import lax

D = 2560
HEADS = 32
HD = 80
FF = 10240
PCH = 1024
PRE = 4096
DECODES = 16
GROUPS = 8
TOKENS = 8192
CACHE = 4096
N_TENSOR = 16


def loud_keys(key, shape, half_width, value_scale):
    key_base = jax.random.fold_in(key, 0)
    values = jax.random.truncated_normal(key_base, -4.0, 4.0, shape, jnp.float32)
    key_lanes = jnp.arange(shape[-1]) < half_width
    return jnp.where(key_lanes, values, value_scale * values)


def draw_prefix_kv(key, part):
    return loud_keys(jax.random.fold_in(key, 11), (GROUPS, PRE, HEADS, 2 * HD), HD, 1.0).astype(jnp.bfloat16)


def draw_cache_kv(key, part):
    return loud_keys(jax.random.fold_in(key, 23), (DECODES, CACHE, HEADS, 2 * HD), HD, 6.0).astype(jnp.bfloat16)


def draw_dec_len(key, part):
    key_top, key_div, key_order = jax.random.split(jax.random.fold_in(key, 37), 3)
    upper = jax.random.randint(key_top, (DECODES,), CACHE // 2, CACHE + 1)
    divider = jax.random.randint(key_div, (DECODES,), 1, 3)
    lengths = jnp.maximum(upper // divider, 1)
    order = jax.random.permutation(key_order, DECODES)
    lengths = lengths.at[order[0]].set(CACHE).at[order[1]].set(1)
    return lengths.astype(jnp.int32)


def draw_offsets(key, part):
    key_len, key_order = jax.random.split(jax.random.fold_in(key, 41))
    lengths = jax.random.randint(key_len, (GROUPS,), 0, PRE + 1)
    order = jax.random.permutation(key_order, GROUPS)
    lengths = lengths.at[order[0]].set(PRE).at[order[1]].set(0)
    return lengths.astype(jnp.int32)


def levels(key, shape, shards, smallest, top_value):
    def one(axis_at, parts):
        heights = jax.random.uniform(jax.random.fold_in(jax.random.fold_in(key, 6), axis_at), (parts,), jnp.float32, smallest / len(shards), top_value / len(shards))
        return jnp.repeat(jnp.exp(heights), shape[axis_at] // parts).reshape((-1,) + (1,) * (len(shape) - axis_at - 1))

    gain = one(*shards[0])
    for cut in shards[1:]:
        gain = gain * one(*cut)
    return gain


def split_up(amount, total, limit, skew):
    loads = [(1 << 20) // math.isqrt(standing ** skew) + 1 for standing in range(2, amount + 1)]
    surplus, given = total - limit - (amount - 1), [1] * (amount - 1)
    while surplus > 0:
        candidates = [i for i in range(amount - 1) if given[i] < limit]
        pool, budget = sum([loads[i] for i in candidates]), surplus
        for i in candidates:
            more = min(limit - given[i], max(1, budget * loads[i] // pool), surplus)
            given[i] = given[i] + more
            surplus = surplus - more
    return np.array([limit] + given)


def ragged(rng, count, total, limit, lean):
    if count == 2:
        one = jax.random.randint(rng, (), max(1, total - limit), min(limit, total - 1) + 1)
        return jnp.stack([one, total - one])
    sizes = jnp.asarray(split_up(count, total, limit, lean), jnp.int32)
    couples = (count - 1) // 2
    donor, sink = sizes[1:1 + 2 * couples:2], sizes[2:2 + 2 * couples:2]
    margin = jnp.minimum(donor - 1, limit - sink)
    passed = jax.random.randint(jax.random.fold_in(rng, 1), (couples,), 0, 1 << 20) % (margin + 1)
    sizes = sizes.at[1:1 + 2 * couples:2].set(donor - passed).at[2:2 + 2 * couples:2].set(sink + passed)
    return sizes[jax.random.permutation(jax.random.fold_in(rng, 2), count)]


def normal_values(stream_key, shape, width, most, cuts=(), dtype=jnp.bfloat16):
    entries = width * jax.random.normal(stream_key, shape, jnp.float32)
    if cuts:
        entries = entries * levels(stream_key, shape, cuts, -0.22, 0.18)
    return jnp.clip(entries, -most, most).astype(dtype)


def setup_inputs(seed: int = 0) -> dict:
    key_of = jax.random.split(jax.random.key(seed), 17)
    x_pre = normal_values(key_of[0], (TOKENS, D), 1.0, 6.0, ((0, 128),))
    x_dec = normal_values(key_of[1], (DECODES, D), 1.0, 6.0)
    prefix_kv = draw_prefix_kv(jax.random.fold_in(key_of[16], 71), 0)
    cache_kv = draw_cache_kv(jax.random.fold_in(key_of[16], 71), 0)
    dec_len = draw_dec_len(jax.random.fold_in(key_of[16], 71), 0)
    offsets = draw_offsets(jax.random.fold_in(key_of[16], 71), 0)
    segments = jax.vmap(lambda own: jnp.searchsorted(jnp.cumsum(ragged(own, 4, PCH, PCH // 2, 1)), jnp.arange(PCH), side="right"))(jax.random.split(key_of[6], GROUPS)).reshape((GROUPS, PCH)).astype(jnp.int32)
    w_qkv = normal_values(key_of[7], (D, 3 * HEADS * HD), D ** -0.5, 0.125, ((1, 16),))
    w_out = normal_values(key_of[8], (HEADS * HD, D), (HEADS * HD) ** -0.5, 0.125, ((0, 16),))
    w_up = normal_values(key_of[9], (D, FF), D ** -0.5, 0.125, ((1, 16),))
    up_bias = normal_values(key_of[10], (FF,), 0.5, 3.0, ((0, 16),), jnp.float32)
    w_down = normal_values(key_of[11], (FF, D), FF ** -0.5, 0.0625, ((0, 16),))
    biases = normal_values(key_of[12], (2, D), 0.5, 3.0, (), jnp.float32)
    gains = jnp.clip(1.0 + 0.18 * jax.random.normal(key_of[13], (2, D), jnp.float32), 0.1, 1.9)
    shifts = normal_values(key_of[14], (2, D), 0.4, 2.5, (), jnp.float32)
    w_next = normal_values(key_of[15], (D, 3 * HEADS * HD), D ** -0.5, 0.125, ((1, 16),))
    return dict(x_pre=x_pre, x_dec=x_dec, prefix_kv=prefix_kv, cache_kv=cache_kv, dec_len=dec_len, offsets=offsets, segments=segments, w_qkv=w_qkv, w_out=w_out, w_up=w_up, up_bias=up_bias, w_down=w_down, biases=biases, gains=gains, shifts=shifts, w_next=w_next)


NEG = -1e+30

def layer_norm(values, gain_row, shift_row):
    average = lax.optimization_barrier(jnp.mean(values, axis=-1, keepdims=True))
    centred = values - average
    spread = lax.optimization_barrier(jnp.mean(centred * centred, axis=-1, keepdims=True))
    return centred * lax.rsqrt(spread + 1e-05) * gain_row + shift_row

def split_sum(rows, weight):
    width_part = rows.shape[1] // N_TENSOR
    left_side = rows.reshape(rows.shape[0], N_TENSOR, width_part).astype(jnp.float32)
    right_side = weight.reshape(N_TENSOR, width_part, weight.shape[1]).astype(jnp.float32)
    partial_value = jnp.einsum('rtk,tkd->trd', left_side, right_side)
    rounded = lax.optimization_barrier(partial_value.astype(jnp.bfloat16))
    return lax.optimization_barrier(jnp.sum(rounded.astype(jnp.float32), axis=0))

def visible(seg_query, query_pos, seg_all, offset, prefix_len):
    prefix_pos = jnp.arange(prefix_len)
    from_prefix = (prefix_pos[None, :] < offset) & (seg_query[:, None] == 0)
    span_pos = jnp.arange(seg_all.shape[0])
    from_span = (seg_all[None, :] == seg_query[:, None]) & (span_pos[None, :] <= query_pos[:, None])
    return jnp.concatenate([from_prefix, from_span], axis=1)

def masked_weights(scores, mask):
    scores = jnp.where(mask, scores, NEG)
    highest = lax.optimization_barrier(jnp.max(scores, axis=-1, keepdims=True))
    weights = jnp.where(mask, jnp.exp(scores - highest), 0.0)
    return (weights / lax.optimization_barrier(jnp.sum(weights, axis=-1, keepdims=True))).astype(jnp.bfloat16)

def reference(x_pre, x_dec, prefix_kv, cache_kv, dec_len, offsets, segments, w_qkv, w_out, w_up, up_bias, w_down, biases, gains, shifts, w_next):
    scale = HD ** (-0.5)

    def dense_tail(attn, x_rows):
        h_first = layer_norm(x_rows.astype(jnp.float32) + split_sum(attn, w_out) + biases[0], gains[0], shifts[0]).astype(jnp.bfloat16)
        hidden = jax.nn.gelu(jnp.dot(h_first, w_up, preferred_element_type=jnp.float32) + up_bias, approximate=False).astype(jnp.bfloat16)
        h_second = layer_norm(h_first.astype(jnp.float32) + split_sum(hidden, w_down) + biases[1], gains[1], shifts[1]).astype(jnp.bfloat16)
        return (h_second, jnp.dot(h_second, w_next, preferred_element_type=jnp.float32).astype(jnp.bfloat16))

    def span_layer(span_args):
        rows, prefix, offset, seg = span_args
        qkv = jnp.dot(rows, w_qkv, preferred_element_type=jnp.float32).astype(jnp.bfloat16).reshape(PCH, HEADS, 3, HD)
        keys = jnp.concatenate([prefix[:, :, :HD], qkv[:, :, 1]], axis=0)
        values = jnp.concatenate([prefix[:, :, HD:], qkv[:, :, 2]], axis=0)
        mask = visible(seg, jnp.arange(PCH), seg, offset, PRE)

        def one_head(head_args):
            query_h, key_h, value_h = head_args
            scores = jnp.dot(query_h, key_h.T, preferred_element_type=jnp.float32) * scale
            weights = masked_weights(scores, mask)
            return jnp.dot(weights, value_h, preferred_element_type=jnp.float32).astype(jnp.bfloat16)
        heads_out = lax.map(one_head, (qkv[:, :, 0].transpose(1, 0, 2), keys.transpose(1, 0, 2), values.transpose(1, 0, 2)))
        attn = heads_out.transpose(1, 0, 2).reshape(PCH, HEADS * HD)
        return dense_tail(attn, rows)
    span_out, span_next = lax.map(span_layer, (x_pre.reshape(GROUPS, PCH, D), prefix_kv, offsets, segments))
    dec_qkv = jnp.dot(x_dec, w_qkv, preferred_element_type=jnp.float32).astype(jnp.bfloat16).reshape(DECODES, HEADS, 3, HD)

    def one_request(request_args):
        query_r, cache_r, length = request_args
        query_f = query_r[:, 0].astype(jnp.float32)
        scores = jnp.einsum('hd,phd->hp', query_f, cache_r[:, :, :HD].astype(jnp.float32)) * scale
        valid = jnp.arange(CACHE) < length
        scores = jnp.where(valid[None, :], scores, NEG)
        own_score = lax.optimization_barrier(jnp.sum(query_f * query_r[:, 1].astype(jnp.float32), axis=-1)) * scale
        highest = jnp.maximum(lax.optimization_barrier(jnp.max(scores, axis=-1)), own_score)
        weights = jnp.where(valid[None, :], jnp.exp(scores - highest[:, None]), 0.0)
        own_weight = jnp.exp(own_score - highest)
        total = lax.optimization_barrier(jnp.sum(weights, axis=-1)) + own_weight
        mixed = jnp.einsum('hp,phd->hd', weights, cache_r[:, :, HD:].astype(jnp.float32)) + own_weight[:, None] * query_r[:, 2].astype(jnp.float32)
        return (mixed / total[:, None]).astype(jnp.bfloat16)
    dec_heads = lax.map(one_request, (dec_qkv, cache_kv, dec_len))
    dec_out, dec_next = dense_tail(dec_heads.reshape(DECODES, HEADS * HD), x_dec)
    return (span_out.reshape(TOKENS, D), span_next.reshape(TOKENS, 3 * HEADS * HD), dec_out, dec_next)
```

```python
import functools

import jax
import jax.numpy as jnp
from jax import lax
from jax.experimental import pallas as pl
from jax.experimental.pallas import tpu as pltpu
from jax.sharding import PartitionSpec as P

MESH = pl.DeviceIdType.MESH
NEG = -1e30
LOG2E = 1.4426950408889634
SIDE = 4
ROWS = 64
VMEM = pltpu.VMEM
NT = (((1,), (1,)), ((), ()))


def place():
    t = lax.axis_index("tensor")
    core = lax.rem(lax.axis_index("rep"), 2)
    y, x = lax.div(t, SIDE), lax.rem(t, SIDE)
    major = y * (1 - core) + x * core
    minor = x * (1 - core) + y * core
    step_major, step_minor = SIDE - (SIDE - 1) * core, 1 + (SIDE - 1) * core

    def device(i, j):
        return lax.rem(i, SIDE) * step_major + lax.rem(j, SIDE) * step_minor

    return y, x, major, minor, device


class Copies:
    def __init__(self, send, recv):
        self.send, self.recv, self.used, self.all = send, recv, 0, []

    def start(self, src, dst, where):
        copy = pltpu.make_async_remote_copy(
            src_ref=src,
            dst_ref=dst,
            send_sem=self.send.at[self.used],
            recv_sem=self.recv.at[self.used],
            device_id=where,
            device_id_type=MESH,
        )
        copy.start()
        self.used += 1
        self.all.append(copy)
        return copy

    def drain(self):
        for copy in self.all:
            copy.wait_send()


def tensor(t):
    return {"tensor": t}


def greet(tensor_peers, rep_peers=()):
    barrier = pltpu.get_barrier_semaphore()
    for t in tensor_peers:
        pl.semaphore_signal(barrier, inc=1, device_id=tensor(t), device_id_type=MESH)
    for r in rep_peers:
        pl.semaphore_signal(barrier, inc=1, device_id={"rep": r}, device_id_type=MESH)
    pl.semaphore_wait(barrier, len(tensor_peers) + len(rep_peers))


class Gather:
    def __init__(self, copies, at):
        y, x, self.a, self.b, self.device = place()
        self.copies, self.at = copies, at

    def go(self, i, j, ti, tj):
        return self.copies.start(self.at(i, j), self.at(i, j), tensor(self.device(ti, tj)))

    def begin(self):
        a, b = self.a, self.b
        self.right = self.go(a, b, a, b + 1)
        self.left = self.go(a, b, a, b + 3)
        self.up = [self.go(a, b, a + 1, b)]
        self.down = [self.go(a, b, a + 3, b)]

    def spread(self, j):
        a, b = self.a, self.b
        self.up.append(self.go(a, j, a + 1, b))
        self.down.append(self.go(a, j, a + 3, b))

    def half(self, i, j, part):
        return self.at(i, j).at[pl.ds(part * (ROWS // 2), ROWS // 2)]

    def first(self):
        a, b = self.a, self.b
        self.right.wait_recv()
        one = self.half(a, b + 3, 0)
        far_one = self.copies.start(one, one, tensor(self.device(a, b + 1)))
        self.spread(b + 3)
        self.left.wait_recv()
        two = self.half(a, b + 1, 1)
        far_two = self.copies.start(two, two, tensor(self.device(a, b + 3)))
        self.spread(b + 1)
        far_one.wait_recv()
        far_two.wait_recv()
        self.spread(b + 2)

    def middle(self):
        a, b = self.a, self.b
        self.up[0].wait_recv()
        self.far = [self.go(a + 3, b, a + 1, b)]
        self.down[1].wait_recv()
        self.far.append(self.go(a + 1, b + 3, a + 3, b))
        self.down[2].wait_recv()
        self.far.append(self.go(a + 1, b + 1, a + 3, b))
        self.up[3].wait_recv()
        self.far.append(self.go(a + 3, b + 2, a + 1, b))
        self.up[1].wait_recv()
        self.up[2].wait_recv()
        self.down[0].wait_recv()
        self.down[3].wait_recv()

    def last(self):
        for copy in self.far:
            copy.wait_recv()


class Scatter:
    def __init__(self, copies, parts, far, near, row, row_far, row_near):
        y, x, self.a, self.b, self.device = place()
        self.copies, self.parts, self.far, self.near = copies, parts, far, near
        self.row, self.row_far, self.row_near = row, row_far, row_near

    def pair(self, i, half):
        return self.parts.at[lax.rem(i, SIDE), pl.ds(2 * half, 2)]

    def send_far(self):
        a, b = self.a, self.b
        self.up_far = self.copies.start(
            self.pair(a + 2, 0), self.far.at[0], tensor(self.device(a + 1, b))
        )
        self.down_far = self.copies.start(
            self.pair(a + 2, 1), self.far.at[1], tensor(self.device(a + 3, b))
        )

    def send_near(self):
        a, b = self.a, self.b
        self.up_near = self.copies.start(
            self.pair(a + 1, 1), self.near.at[0, pl.ds(2, 2)], tensor(self.device(a + 1, b))
        )
        self.down_near = self.copies.start(
            self.pair(a + 3, 0), self.near.at[1, pl.ds(0, 2)], tensor(self.device(a + 3, b))
        )

    def pass_on(self):
        a, b = self.a, self.b
        self.up_far.wait_recv()
        self.pair(a + 1, 0)[...] = (
            self.pair(a + 1, 0)[...].astype(jnp.float32) + self.far[0].astype(jnp.float32)
        ).astype(jnp.bfloat16)
        self.up_sum = self.copies.start(
            self.pair(a + 1, 0), self.near.at[0, pl.ds(0, 2)], tensor(self.device(a + 1, b))
        )
        self.down_far.wait_recv()
        self.pair(a + 3, 1)[...] = (
            self.pair(a + 3, 1)[...].astype(jnp.float32) + self.far[1].astype(jnp.float32)
        ).astype(jnp.bfloat16)
        self.down_sum = self.copies.start(
            self.pair(a + 3, 1), self.near.at[1, pl.ds(2, 2)], tensor(self.device(a + 3, b))
        )

    def total(self, j):
        at = lax.rem(j, SIDE)
        return (
            self.parts[lax.rem(self.a, SIDE), at].astype(jnp.float32)
            + self.near[0, at].astype(jnp.float32)
            + self.near[1, at].astype(jnp.float32)
        )

    def finish(self):
        a, b = self.a, self.b
        half = ROWS // 2
        for copy in (self.up_near, self.down_near, self.up_sum, self.down_sum):
            copy.wait_recv()
        right, left = tensor(self.device(a, b + 1)), tensor(self.device(a, b + 3))
        top, low = pl.ds(0, half), pl.ds(half, half)

        def row(j):
            return self.row.at[lax.rem(j, SIDE)]

        row(b + 2)[...] = self.total(b + 2).astype(jnp.bfloat16)
        right_far = self.copies.start(row(b + 2).at[top], self.row_far.at[0], right)
        left_far = self.copies.start(row(b + 2).at[low], self.row_far.at[1], left)
        row(b + 1)[...] = self.total(b + 1).astype(jnp.bfloat16)
        right_near = self.copies.start(row(b + 1).at[low], self.row_near.at[0, low], right)
        row(b + 3)[...] = self.total(b + 3).astype(jnp.bfloat16)
        left_near = self.copies.start(row(b + 3).at[top], self.row_near.at[1, top], left)
        own = self.total(b)
        right_far.wait_recv()
        row(b + 1).at[top][...] = (
            row(b + 1).at[top][...].astype(jnp.float32) + self.row_far[0].astype(jnp.float32)
        ).astype(jnp.bfloat16)
        right_sum = self.copies.start(row(b + 1).at[top], self.row_near.at[0, top], right)
        left_far.wait_recv()
        row(b + 3).at[low][...] = (
            row(b + 3).at[low][...].astype(jnp.float32) + self.row_far[1].astype(jnp.float32)
        ).astype(jnp.bfloat16)
        left_sum = self.copies.start(row(b + 3).at[low], self.row_near.at[1, low], left)
        for copy in (right_near, left_near, right_sum, left_sum):
            copy.wait_recv()
        return (
            own + self.row_near[0].astype(jnp.float32) + self.row_near[1].astype(jnp.float32)
        )


class SmallSum:
    def __init__(self, copies, over_x, over_y):
        t = lax.axis_index("tensor")
        self.y, self.x = lax.div(t, SIDE), lax.rem(t, SIDE)
        self.copies, self.over_x, self.over_y = copies, over_x, over_y

    def begin(self, value):
        self.over_x[self.x] = value.astype(jnp.bfloat16)
        mine = self.over_x.at[self.x]
        self.sent = [
            self.copies.start(
                mine, mine, tensor(SIDE * self.y + lax.rem(self.x + k, SIDE))
            )
            for k in (1, 2, 3)
        ]

    def middle(self):
        for copy in self.sent:
            copy.wait_recv()
        self.over_y[self.y] = sum(
            self.over_x[k].astype(jnp.float32) for k in range(SIDE)
        ).astype(jnp.bfloat16)
        mine = self.over_y.at[self.y]
        self.sent = [
            self.copies.start(
                mine, mine, tensor(SIDE * lax.rem(self.y + k, SIDE) + self.x)
            )
            for k in (1, 2, 3)
        ]

    def finish(self):
        for copy in self.sent:
            copy.wait_recv()
        return sum(self.over_y[k].astype(jnp.float32) for k in range(SIDE))


def layer_norm(values, gain_row, shift_row):
    average = jnp.mean(values, axis=-1, keepdims=True)
    centred = values - average
    spread = jnp.mean(centred * centred, axis=-1, keepdims=True)
    return centred * lax.rsqrt(spread + 1e-05) * gain_row + shift_row


def project_kernel(
    reps,
    scale,
    x_ref,
    dec_ref,
    len_ref,
    w_hbm,
    cache_hbm,
    out_ref,
    attn_ref,
    rows,
    w_ref,
    cache_ref,
    states,
    local_sem,
    send_sem,
    recv_sem,
):
    load_w = pltpu.make_async_copy(w_hbm, w_ref, local_sem.at[0])
    load_w.start()
    load_cache = pltpu.make_async_copy(cache_hbm, cache_ref, local_sem.at[1])
    load_cache.start()
    y, x, a, b, device = place()
    rep = lax.axis_index("rep")
    copies = Copies(send_sem, recv_sem)
    rows[device(a, b)] = x_ref[...]
    greet(
        [device(a, b + 1), device(a, b + 3), device(a + 1, b), device(a + 3, b)],
        [lax.rem(rep + k, reps) for k in range(1, reps)],
    )
    gather = Gather(copies, lambda i, j: rows.at[device(i, j)])
    gather.begin()
    load_w.wait()
    dec = (
        lax.dot_general(w_ref[...], dec_ref[...], NT, preferred_element_type=jnp.float32)
        .astype(jnp.bfloat16)
        .astype(jnp.float32)
    )
    gather.first()
    load_cache.wait()
    hd = cache_ref.shape[2] // 2
    heads = cache_ref.shape[1]
    span = cache_ref.shape[3]
    lanes = dec.shape[1]
    lane = lax.broadcasted_iota(jnp.int32, (1, lanes), 1)
    position = rep * span + lax.broadcasted_iota(jnp.int32, (1, span), 1)

    def request(r, state):
        pick = lane == r
        column = jnp.sum(jnp.where(pick, dec, 0.0), axis=1, keepdims=True)
        valid = position < len_ref[r]
        out = []
        for h in range(heads):
            query = column[3 * hd * h : 3 * hd * h + hd]
            key = cache_ref[r, h, :hd].astype(jnp.float32)
            value = cache_ref[r, h, hd:].astype(jnp.float32)
            score = jnp.sum(key * query, axis=0, keepdims=True) * scale
            score = jnp.where(valid, score, NEG)
            high = jnp.max(score, axis=1, keepdims=True)
            weight = jnp.where(valid, jnp.exp(score - high), 0.0)
            total = jnp.sum(weight, axis=1, keepdims=True)
            mixed = jnp.sum(value * weight, axis=1, keepdims=True)
            highs, totals, mixes = state[h]
            out.append(
                (
                    jnp.where(pick, high, highs),
                    jnp.where(pick, total, totals),
                    jnp.where(pick, mixed, mixes),
                )
            )
        return tuple(out)

    empty = tuple(
        (
            jnp.full((1, lanes), NEG, jnp.float32),
            jnp.zeros((1, lanes), jnp.float32),
            jnp.zeros((hd, lanes), jnp.float32),
        )
        for _ in range(heads)
    )
    state = lax.fori_loop(0, cache_ref.shape[0], request, empty)
    for h in range(heads):
        states[rep, h, :hd] = state[h][2]
        states[rep, h, hd : hd + 8] = jnp.broadcast_to(state[h][0], (8, lanes))
        states[rep, h, hd + 8 : hd + 16] = jnp.broadcast_to(state[h][1], (8, lanes))
    sent = [
        copies.start(states.at[rep], states.at[rep], {"rep": lax.rem(rep + k, reps)})
        for k in range(1, reps)
    ]
    gather.middle()
    for copy in sent:
        copy.wait_recv()
    for h in range(heads):
        base = 3 * hd * h
        query, key, value = (dec[base + hd * k : base + hd * (k + 1)] for k in range(3))
        own = jnp.sum(query * key, axis=0, keepdims=True) * scale
        highest = own
        for k in range(reps):
            highest = jnp.maximum(highest, states[k, h, hd : hd + 1])
        own_weight = jnp.exp(own - highest)
        total, mixed = own_weight, own_weight * value
        for k in range(reps):
            factor = jnp.exp(states[k, h, hd : hd + 1] - highest)
            total = total + factor * states[k, h, hd + 8 : hd + 9]
            mixed = mixed + factor * states[k, h, :hd]
        attn_ref[hd * h : hd * (h + 1)] = (mixed / total).astype(attn_ref.dtype)
    gather.last()

    @pl.loop(0, SIDE)
    def _(i):
        block = rows[pl.ds(SIDE * i, SIDE)].reshape(SIDE * ROWS, rows.shape[2])
        out_ref[:, pl.ds(pl.multiple_of(i * SIDE * ROWS, SIDE * ROWS), SIDE * ROWS)] = (
            lax.dot_general(w_ref[...], block, NT, preferred_element_type=jnp.float32).astype(
                out_ref.dtype
            )
        )

    copies.drain()


def attend_kernel(
    scale, offset_ref, first_ref, qkv_ref, kv_ref, seg_row, seg_col, out_ref, q_ref, m_ref, l_ref, acc_ref
):
    head = pl.program_id(0)
    hd = q_ref.shape[1]
    span = seg_row.shape[1]
    block, key_block = 256, 1024
    factor = scale * LOG2E
    q_ref[...] = qkv_ref[0, 0].astype(jnp.float32).T.astype(jnp.bfloat16)
    offset = offset_ref[0]

    def absorb(score, values):
        high = jnp.maximum(m_ref[...], jnp.max(score, axis=1, keepdims=True))
        decay = jnp.exp2((m_ref[...] - high) * factor)
        weight = jnp.exp2((score - high) * factor)
        m_ref[...] = high
        l_ref[...] = l_ref[...] * decay + jnp.sum(weight, axis=1, keepdims=True)
        acc_ref[...] = acc_ref[...] * decay + lax.dot_general(
            weight.astype(jnp.bfloat16), values, NT, preferred_element_type=jnp.float32
        )

    for i in range(span // block):
        rows = slice(i * block, (i + 1) * block)
        m_ref[...] = jnp.full(m_ref.shape, NEG, jnp.float32)
        l_ref[...] = jnp.zeros(l_ref.shape, jnp.float32)
        acc_ref[...] = jnp.zeros(acc_ref.shape, jnp.float32)
        seg_q = seg_col[rows]
        if (i * block) < span // 2:

            @pl.when((first_ref[i] == 0) & (offset > 0))
            def _():
                @pl.loop(0, lax.div(offset + (key_block - 1), key_block))
                def _(j):
                    at = pl.multiple_of(j * key_block, key_block)
                    score = jnp.dot(
                        q_ref[rows],
                        kv_ref[0, :hd, pl.ds(at, key_block)],
                        preferred_element_type=jnp.float32,
                    )
                    where = at + lax.broadcasted_iota(jnp.int32, (1, key_block), 1)
                    absorb(
                        jnp.where(where < offset, score, NEG),
                        kv_ref[0, hd:, pl.ds(at, key_block)],
                    )

                keep = seg_q == 0
                m_ref[...] = jnp.where(keep, m_ref[...], NEG)
                l_ref[...] = jnp.where(keep, l_ref[...], 0.0)
                acc_ref[...] = jnp.where(keep, acc_ref[...], 0.0)

        low = max(0, (i - span // 2 // block) * block)
        high = (i + 1) * block
        score = jnp.dot(
            q_ref[rows], qkv_ref[0, 1, :, low:high], preferred_element_type=jnp.float32
        )
        shape = (block, high - low)
        query_at = i * block + lax.broadcasted_iota(jnp.int32, shape, 0)
        key_at = low + lax.broadcasted_iota(jnp.int32, shape, 1)
        seen = (seg_row[:, low:high] == seg_q) & (key_at <= query_at)
        absorb(jnp.where(seen, score, NEG), qkv_ref[0, 2, :, low:high])
        result = (acc_ref[...] / l_ref[...]).astype(out_ref.dtype)
        for h in range(out_ref.shape[1] // hd):

            @pl.when(head == h)
            def _():
                out_ref[rows, h * hd : (h + 1) * hd] = result


def tail_kernel(
    attn_ref,
    dec_attn_ref,
    x_ref,
    x_dec_ref,
    w_out_ref,
    up_bias_ref,
    biases_ref,
    gains_ref,
    shifts_ref,
    w_up_hbm,
    w_down_hbm,
    w_next_hbm,
    out_ref,
    next_ref,
    dec_out_ref,
    dec_next_ref,
    w_up_ref,
    w_down_ref,
    w_next_ref,
    slabs,
    rows,
    parts,
    more,
    far,
    near,
    row,
    row_far,
    row_near,
    over_x,
    over_y,
    local_sem,
    send_sem,
    recv_sem,
):
    loads = []
    for k, (source, target) in enumerate(
        ((w_up_hbm, w_up_ref), (w_down_hbm, w_down_ref), (w_next_hbm, w_next_ref))
    ):
        loads.append(pltpu.make_async_copy(source, target, local_sem.at[k]))
        loads[-1].start()
    y, x, a, b, device = place()
    copies = Copies(send_sem, recv_sem)
    greet(
        [SIDE * y + lax.rem(x + k, SIDE) for k in (1, 2, 3)]
        + [SIDE * lax.rem(y + k, SIDE) + x for k in (1, 2, 3)]
    )
    width = x_ref.shape[1]
    chunk = (SIDE, ROWS, width)

    dec_sum = SmallSum(copies, over_x.at[0], over_y.at[0])
    dec_sum.begin(
        jnp.dot(dec_attn_ref[...], w_out_ref[...], preferred_element_type=jnp.float32)
    )

    def out_share(i):
        left = jnp.concatenate(
            [
                attn_ref[pl.ds(pl.multiple_of(device(i, j) * ROWS, ROWS), ROWS)]
                for j in range(SIDE)
            ],
            axis=0,
        )
        parts[lax.rem(i, SIDE)] = (
            jnp.dot(left, w_out_ref[...], preferred_element_type=jnp.float32)
            .astype(jnp.bfloat16)
            .reshape(chunk)
        )

    scatter = Scatter(copies, parts, far.at[0], near.at[0], row.at[0], row_far.at[0], row_near.at[0])
    out_share(a + 2)
    scatter.send_far()
    out_share(a + 1)
    out_share(a + 3)
    scatter.send_near()
    out_share(a)
    dec_sum.middle()
    scatter.pass_on()
    dec_first = layer_norm(
        x_dec_ref[...].astype(jnp.float32) + dec_sum.finish() + biases_ref[0:1],
        gains_ref[0:1],
        shifts_ref[0:1],
    ).astype(jnp.bfloat16)
    attn_sum = scatter.finish()
    first = layer_norm(
        x_ref[...].astype(jnp.float32) + attn_sum + biases_ref[0:1], gains_ref[0:1], shifts_ref[0:1]
    ).astype(jnp.bfloat16)

    def slab(i, j):
        return slabs.at[lax.rem(i, SIDE), lax.rem(j, SIDE)]

    slab(a, b)[...] = first
    gather = Gather(copies, slab)
    gather.begin()
    loads[0].wait()
    loads[1].wait()

    def mlp(value):
        inner = jnp.dot(value, w_up_ref[...], preferred_element_type=jnp.float32) + up_bias_ref[...]
        hidden = (0.5 * inner * (1.0 + lax.erf(inner * 0.7071067811865476))).astype(jnp.bfloat16)
        return jnp.dot(hidden, w_down_ref[...], preferred_element_type=jnp.float32)

    dec_sum = SmallSum(copies, over_x.at[1], over_y.at[1])
    dec_sum.begin(mlp(dec_first))

    def mlp_share(i):
        at = lax.rem(i, SIDE)
        more[at] = (
            mlp(slabs[at].reshape(SIDE * ROWS, width)).astype(jnp.bfloat16).reshape(chunk)
        )

    scatter = Scatter(copies, more, far.at[1], near.at[1], row.at[1], row_far.at[1], row_near.at[1])
    gather.first()
    mlp_share(a)
    gather.middle()
    mlp_share(a + 1)
    mlp_share(a + 3)
    scatter.send_near()
    dec_sum.middle()
    gather.last()
    mlp_share(a + 2)
    scatter.send_far()
    dec_out = layer_norm(
        dec_first.astype(jnp.float32) + dec_sum.finish() + biases_ref[1:2],
        gains_ref[1:2],
        shifts_ref[1:2],
    ).astype(jnp.bfloat16)
    dec_out_ref[...] = dec_out
    loads[2].wait()
    dec_next_ref[...] = lax.dot_general(
        dec_out, w_next_ref[...], NT, preferred_element_type=jnp.float32
    ).astype(jnp.bfloat16)
    scatter.pass_on()
    mlp_sum = scatter.finish()
    second = layer_norm(
        first.astype(jnp.float32) + mlp_sum + biases_ref[1:2], gains_ref[1:2], shifts_ref[1:2]
    ).astype(jnp.bfloat16)
    out_ref[...] = second
    rows[device(a, b)] = second
    gather = Gather(copies, lambda i, j: rows.at[device(i, j)])
    gather.begin()
    gather.first()
    gather.middle()
    gather.last()

    @pl.loop(0, SIDE)
    def _(i):
        block = rows[pl.ds(SIDE * i, SIDE)].reshape(SIDE * ROWS, width)
        next_ref[:, pl.ds(pl.multiple_of(i * SIDE * ROWS, SIDE * ROWS), SIDE * ROWS)] = (
            lax.dot_general(
                w_next_ref[...], block, NT, preferred_element_type=jnp.float32
            ).astype(next_ref.dtype)
        )

    copies.drain()


def per_device(
    reps,
    x_pre,
    x_dec,
    prefix_kv,
    cache_kv,
    dec_len,
    offsets,
    segments,
    w_qkv,
    w_out,
    w_up,
    up_bias,
    w_down,
    biases,
    gains,
    shifts,
    w_next,
):
    heads = prefix_kv.shape[2]
    hd = prefix_kv.shape[3] // 2
    span = segments.shape[1]
    width = x_pre.shape[1]
    decodes = x_dec.shape[0]
    columns = w_qkv.shape[1]
    units = w_up.shape[1]
    scale = hd ** (-0.5)
    bf16, f32 = jnp.bfloat16, jnp.float32
    shape = jax.ShapeDtypeStruct
    whole = pl.BlockSpec(memory_space=VMEM)
    scalars = pl.BlockSpec(memory_space=pltpu.SMEM)
    anywhere = pl.BlockSpec(memory_space=pl.ANY)
    group = SIDE * SIDE

    cache_t = cache_kv.transpose(0, 2, 3, 1)
    n_copies = 16 + reps - 1
    qkv_t, dec_attn_t = pl.pallas_call(
        functools.partial(project_kernel, reps, scale),
        out_shape=(shape((columns, span), bf16), shape((heads * hd, 128), bf16)),
        in_specs=[whole, whole, scalars, anywhere, anywhere],
        out_specs=(whole, whole),
        scratch_shapes=[
            VMEM((group, ROWS, width), bf16),
            VMEM((columns, width), bf16),
            VMEM(cache_t.shape, bf16),
            VMEM((reps, heads, hd + 16, 128), f32),
            pltpu.SemaphoreType.DMA((2,)),
            pltpu.SemaphoreType.DMA((n_copies,)),
            pltpu.SemaphoreType.DMA((n_copies,)),
        ],
        compiler_params=pltpu.CompilerParams(
            collective_id=0, has_side_effects=True, vmem_limit_bytes=48 << 20
        ),
        name="project",
    )(x_pre, jnp.pad(x_dec, ((0, 128 - decodes), (0, 0))), dec_len, w_qkv.T, cache_t)

    attn = pl.pallas_call(
        functools.partial(attend_kernel, scale),
        grid=(heads,),
        out_shape=shape((span, heads * hd), bf16),
        in_specs=[
            scalars,
            scalars,
            pl.BlockSpec((1, 3, hd, span), lambda h: (h, 0, 0, 0)),
            pl.BlockSpec((1, 2 * hd, prefix_kv.shape[1]), lambda h: (h, 0, 0)),
            pl.BlockSpec((1, span), lambda h: (0, 0)),
            pl.BlockSpec((span, 1), lambda h: (0, 0)),
        ],
        out_specs=pl.BlockSpec((span, heads * hd), lambda h: (0, 0)),
        scratch_shapes=[
            VMEM((span, hd), bf16),
            VMEM((256, 1), f32),
            VMEM((256, 1), f32),
            VMEM((256, hd), f32),
        ],
        compiler_params=pltpu.CompilerParams(
            dimension_semantics=("arbitrary",), vmem_limit_bytes=48 << 20
        ),
        name="attend",
    )(
        offsets,
        segments[0, :: 256],
        qkv_t.reshape(heads, 3, hd, span),
        prefix_kv[0].transpose(1, 2, 0),
        segments,
        segments.reshape(span, 1),
    )

    n_copies = 2 * (16 + 12 + 6)
    layer_out, next_t, dec_out, dec_next = pl.pallas_call(
        tail_kernel,
        out_shape=(
            shape((ROWS, width), bf16),
            shape((columns, span), bf16),
            shape((decodes, width), bf16),
            shape((decodes, columns), bf16),
        ),
        in_specs=[whole] * 9 + [anywhere] * 3,
        out_specs=(whole,) * 4,
        scratch_shapes=[
            VMEM((width, units), bf16),
            VMEM((units, width), bf16),
            VMEM((columns, width), bf16),
            VMEM((SIDE, SIDE, ROWS, width), bf16),
            VMEM((group, ROWS, width), bf16),
            VMEM((SIDE, SIDE, ROWS, width), bf16),
            VMEM((SIDE, SIDE, ROWS, width), bf16),
            VMEM((2, 2, 2, ROWS, width), bf16),
            VMEM((2, 2, SIDE, ROWS, width), bf16),
            VMEM((2, SIDE, ROWS, width), bf16),
            VMEM((2, 2, ROWS // 2, width), bf16),
            VMEM((2, 2, ROWS, width), bf16),
            VMEM((2, SIDE, decodes, width), bf16),
            VMEM((2, SIDE, decodes, width), bf16),
            pltpu.SemaphoreType.DMA((3,)),
            pltpu.SemaphoreType.DMA((n_copies,)),
            pltpu.SemaphoreType.DMA((n_copies,)),
        ],
        compiler_params=pltpu.CompilerParams(
            collective_id=1, has_side_effects=True, vmem_limit_bytes=60 << 20
        ),
        name="tail",
    )(
        attn,
        dec_attn_t[:, :decodes].T,
        x_pre,
        x_dec,
        w_out,
        up_bias.reshape(1, units),
        biases,
        gains,
        shifts,
        w_up,
        w_down,
        w_next.T,
    )
    return layer_out, next_t.T, dec_out, dec_next


def solution(mesh):
    placed = (
        P(("rep", "tensor"), None),
        P(),
        P("rep", None, "tensor", None),
        P(None, "rep", "tensor", None),
        P(),
        P("rep"),
        P("rep", None),
        P(None, "tensor"),
        P("tensor", None),
        P(None, "tensor"),
        P("tensor"),
        P("tensor", None),
        P(),
        P(),
        P(),
        P(None, "tensor"),
    )
    return jax.shard_map(
        functools.partial(per_device, mesh.shape["rep"]),
        mesh=mesh,
        in_specs=placed,
        out_specs=(P(("rep", "tensor"), None), P("rep", "tensor"), P(), P(None, "tensor")),
        check_vma=False,
    )
```

```python
import functools

import jax
import jax.numpy as jnp
from jax import lax
from jax.experimental import pallas as pl
from jax.experimental.pallas import tpu as pltpu
from jax.sharding import PartitionSpec as P

MESH = pl.DeviceIdType.MESH
NEG = -1e30
LOG2E = 1.4426950408889634
SIDE = 4
ROWS = 64
VMEM = pltpu.VMEM
NT = (((1,), (1,)), ((), ()))


def place():
    t = lax.axis_index("tensor")
    core = lax.rem(lax.axis_index("rep"), 2)
    y, x = lax.div(t, SIDE), lax.rem(t, SIDE)
    major = y * (1 - core) + x * core
    minor = x * (1 - core) + y * core
    step_major, step_minor = SIDE - (SIDE - 1) * core, 1 + (SIDE - 1) * core

    def device(i, j):
        return lax.rem(i, SIDE) * step_major + lax.rem(j, SIDE) * step_minor

    return y, x, major, minor, device


class Copies:
    def __init__(self, send, recv):
        self.send, self.recv, self.used, self.all = send, recv, 0, []

    def start(self, src, dst, where):
        copy = pltpu.make_async_remote_copy(
            src_ref=src,
            dst_ref=dst,
            send_sem=self.send.at[self.used],
            recv_sem=self.recv.at[self.used],
            device_id=where,
            device_id_type=MESH,
        )
        copy.start()
        self.used += 1
        self.all.append(copy)
        return copy

    def drain(self):
        for copy in self.all:
            copy.wait_send()


def tensor(t):
    return {"tensor": t}


def greet(tensor_peers, rep_peers=()):
    barrier = pltpu.get_barrier_semaphore()
    for t in tensor_peers:
        pl.semaphore_signal(barrier, inc=1, device_id=tensor(t), device_id_type=MESH)
    for r in rep_peers:
        pl.semaphore_signal(barrier, inc=1, device_id={"rep": r}, device_id_type=MESH)
    pl.semaphore_wait(barrier, len(tensor_peers) + len(rep_peers))


class Gather:
    def __init__(self, copies, at, own=None):
        y, x, self.a, self.b, self.device = place()
        self.copies, self.at, self.own = copies, at, own

    def go(self, i, j, ti, tj):
        return self.copies.start(self.at(i, j), self.at(i, j), tensor(self.device(ti, tj)))

    def begin(self):
        a, b = self.a, self.b
        own = self.at(a, b) if self.own is None else self.own
        self.right, self.left, up, down = (
            self.copies.start(own, self.at(a, b), tensor(self.device(i, j)))
            for i, j in ((a, b + 1), (a, b + 3), (a + 1, b), (a + 3, b))
        )
        self.up, self.down = [up], [down]

    def spread(self, j):
        a, b = self.a, self.b
        self.up.append(self.go(a, j, a + 1, b))
        self.down.append(self.go(a, j, a + 3, b))

    def half(self, i, j, part):
        return self.at(i, j).at[pl.ds(part * (ROWS // 2), ROWS // 2)]

    def first(self):
        a, b = self.a, self.b
        self.right.wait_recv()
        one = self.half(a, b + 3, 0)
        far_one = self.copies.start(one, one, tensor(self.device(a, b + 1)))
        self.spread(b + 3)
        self.left.wait_recv()
        two = self.half(a, b + 1, 1)
        far_two = self.copies.start(two, two, tensor(self.device(a, b + 3)))
        self.spread(b + 1)
        far_one.wait_recv()
        far_two.wait_recv()
        self.spread(b + 2)

    def middle(self):
        a, b = self.a, self.b
        self.up[0].wait_recv()
        self.far = [self.go(a + 3, b, a + 1, b)]
        self.down[1].wait_recv()
        self.far.append(self.go(a + 1, b + 3, a + 3, b))
        self.down[2].wait_recv()
        self.far.append(self.go(a + 1, b + 1, a + 3, b))
        self.up[3].wait_recv()
        self.far.append(self.go(a + 3, b + 2, a + 1, b))
        self.up[1].wait_recv()
        self.up[2].wait_recv()
        self.down[0].wait_recv()
        self.down[3].wait_recv()

    def last(self):
        for copy in self.far:
            copy.wait_recv()


class RingSum:
    def __init__(self, copies, row, far, near, index, to):
        self.copies, self.slabs, self.far, self.near = copies, row, far, near
        self.c, self.next, self.prev = index, to(index + 1), to(index + 3)
        half = ROWS // 2
        self.top, self.low = pl.ds(0, half), pl.ds(half, half)

    def row(self, k):
        return self.slabs.at[lax.rem(self.c + k, SIDE)]

    def send_far(self):
        self.next_far = self.copies.start(self.row(2).at[self.top], self.far.at[0], self.next)
        self.prev_far = self.copies.start(self.row(2).at[self.low], self.far.at[1], self.prev)

    def send_next(self):
        self.next_near = self.copies.start(
            self.row(1).at[self.low], self.near.at[0, self.low], self.next
        )

    def send_prev(self):
        self.prev_near = self.copies.start(
            self.row(3).at[self.top], self.near.at[1, self.top], self.prev
        )

    def pass_on(self):
        self.next_far.wait_recv()
        add_into(self.row(1).at[self.top], self.far[0])
        self.next_sum = self.copies.start(
            self.row(1).at[self.top], self.near.at[0, self.top], self.next
        )
        self.prev_far.wait_recv()
        add_into(self.row(3).at[self.low], self.far[1])
        self.prev_sum = self.copies.start(
            self.row(3).at[self.low], self.near.at[1, self.low], self.prev
        )

    def finish(self, own):
        for copy in (self.next_near, self.prev_near, self.next_sum, self.prev_sum):
            copy.wait_recv()
        return own + self.near[0].astype(jnp.float32) + self.near[1].astype(jnp.float32)


def add_into(ref, value):
    ref[...] = (ref[...].astype(jnp.float32) + value.astype(jnp.float32)).astype(ref.dtype)


class Scatter:
    def __init__(self, copies, parts, far, near, row, row_far, row_near):
        y, x, a, b, self.device = place()
        self.a, self.b = a, b
        self.copies, self.parts, self.far, self.near = copies, parts, far, near
        self.ring = RingSum(
            copies, row, row_far, row_near, b, lambda j: tensor(self.device(a, j))
        )
        self.above, self.below = tensor(self.device(a + 1, b)), tensor(self.device(a + 3, b))
        self.ups, self.downs = (b + 2, b + 1), (b + 3, b)

    def part(self, i, j):
        return self.parts.at[lax.rem(i, SIDE), lax.rem(j, SIDE)]

    def landing(self, side, j):
        return self.near.at[side, lax.rem(j, SIDE)]

    def send_far(self):
        self.far_up, self.far_down = [], []
        for k in range(2):
            self.far_up.append(
                self.copies.start(self.part(self.a + 2, self.ups[k]), self.far.at[0, k], self.above)
            )
            self.far_down.append(
                self.copies.start(
                    self.part(self.a + 2, self.downs[k]), self.far.at[1, k], self.below
                )
            )

    def send_near(self):
        self.near_up, self.near_down = [], []
        for k in range(2):
            self.near_up.append(
                self.copies.start(
                    self.part(self.a + 1, self.downs[k]),
                    self.landing(0, self.downs[k]),
                    self.above,
                )
            )
            self.near_down.append(
                self.copies.start(
                    self.part(self.a + 3, self.ups[k]), self.landing(1, self.ups[k]), self.below
                )
            )

    def pass_on(self):
        self.sum_up, self.sum_down = [], []
        for k in range(2):
            self.far_up[k].wait_recv()
            add_into(self.part(self.a + 1, self.ups[k]), self.far[0, k])
            self.sum_up.append(
                self.copies.start(
                    self.part(self.a + 1, self.ups[k]), self.landing(0, self.ups[k]), self.above
                )
            )
            self.far_down[k].wait_recv()
            add_into(self.part(self.a + 3, self.downs[k]), self.far[1, k])
            self.sum_down.append(
                self.copies.start(
                    self.part(self.a + 3, self.downs[k]),
                    self.landing(1, self.downs[k]),
                    self.below,
                )
            )

    def total(self, j):
        at = lax.rem(j, SIDE)
        return (
            self.parts[self.a, at].astype(jnp.float32)
            + self.near[0, at].astype(jnp.float32)
            + self.near[1, at].astype(jnp.float32)
        )

    def finish(self):
        ring, b = self.ring, self.b
        self.sum_up[0].wait_recv()
        self.near_down[0].wait_recv()
        ring.row(2)[...] = self.total(b + 2).astype(jnp.bfloat16)
        ring.send_far()
        self.near_up[0].wait_recv()
        self.sum_down[0].wait_recv()
        ring.row(3)[...] = self.total(b + 3).astype(jnp.bfloat16)
        ring.send_prev()
        self.sum_up[1].wait_recv()
        self.near_down[1].wait_recv()
        ring.row(1)[...] = self.total(b + 1).astype(jnp.bfloat16)
        ring.send_next()
        ring.pass_on()
        self.near_up[1].wait_recv()
        self.sum_down[1].wait_recv()
        return ring.finish(self.total(b))


class SmallSum:
    def __init__(self, copies, over_x, over_y):
        t = lax.axis_index("tensor")
        self.y, self.x = lax.div(t, SIDE), lax.rem(t, SIDE)
        self.copies, self.over_x, self.over_y = copies, over_x, over_y

    def begin(self, value):
        self.over_x[self.x] = value.astype(jnp.bfloat16)
        mine = self.over_x.at[self.x]
        self.sent = [
            self.copies.start(
                mine, mine, tensor(SIDE * self.y + lax.rem(self.x + k, SIDE))
            )
            for k in (1, 2, 3)
        ]

    def middle(self):
        for copy in self.sent:
            copy.wait_recv()
        self.over_y[self.y] = sum(
            self.over_x[k].astype(jnp.float32) for k in range(SIDE)
        ).astype(jnp.bfloat16)
        mine = self.over_y.at[self.y]
        self.sent = [
            self.copies.start(
                mine, mine, tensor(SIDE * lax.rem(self.y + k, SIDE) + self.x)
            )
            for k in (1, 2, 3)
        ]

    def finish(self):
        for copy in self.sent:
            copy.wait_recv()
        return sum(self.over_y[k].astype(jnp.float32) for k in range(SIDE))


def layer_norm(values, gain_row, shift_row):
    average = jnp.mean(values, axis=-1, keepdims=True)
    centred = values - average
    spread = jnp.mean(centred * centred, axis=-1, keepdims=True)
    return centred * lax.rsqrt(spread + 1e-05) * gain_row + shift_row


def project_kernel(
    reps,
    scale,
    len_ref,
    dec_ref,
    x_hbm,
    w_hbm,
    cache_hbm,
    w_out_hbm,
    out_ref,
    attn_ref,
    w_row_hbm,
    rows,
    dec_rows,
    w_ref,
    cache_ref,
    states,
    local_sem,
    send_sem,
    recv_sem,
):
    y, x, a, b, device = place()
    load_x = pltpu.make_async_copy(x_hbm, rows.at[device(a, b)], local_sem.at[2])
    load_x.start()
    load_w = pltpu.make_async_copy(w_hbm, w_ref, local_sem.at[0])
    load_w.start()
    load_cache = pltpu.make_async_copy(cache_hbm, cache_ref, local_sem.at[1])
    load_cache.start()
    keep_w = pltpu.make_async_copy(w_out_hbm, w_row_hbm.at[b], local_sem.at[3])
    keep_w.start()
    rep = lax.axis_index("rep")
    copies = Copies(send_sem, recv_sem)
    greet(
        [device(a, b + k) for k in (1, 2, 3)] + [device(a + 1, b), device(a + 3, b)],
        [lax.rem(rep + k, reps) for k in range(1, reps)],
    )
    gather = Gather(copies, lambda i, j: rows.at[device(i, j)])
    load_x.wait()
    gather.begin()
    planes = reps // 2
    quarter = w_out_hbm.shape[1] // planes
    mine = pl.ds(pl.multiple_of(lax.div(rep, 2) * quarter, 128), quarter)
    shards = [
        copies.start(
            w_out_hbm.at[:, mine], w_row_hbm.at[b, :, mine], tensor(device(a, b + k))
        )
        for k in (1, 3, 2)
    ]
    dec_rows[...] = jnp.zeros_like(dec_rows)
    dec_rows[: dec_ref.shape[0]] = dec_ref[...]
    load_w.wait()
    dec = (
        lax.dot_general(w_ref[...], dec_rows[...], NT, preferred_element_type=jnp.float32)
        .astype(jnp.bfloat16)
        .astype(jnp.float32)
    )
    gather.first()
    spread = []
    for k, shard in zip((1, 3, 2), shards):
        shard.wait_recv()
        piece = w_row_hbm.at[lax.rem(b - k + SIDE, SIDE), :, mine]
        spread += [
            copies.start(piece, piece, {"rep": lax.rem(rep + 2 * p, reps)})
            for p in range(1, planes)
        ]
    load_cache.wait()
    hd = cache_ref.shape[2] // 2
    heads = cache_ref.shape[1]
    span = cache_ref.shape[3]
    lanes = dec.shape[1]
    lane = lax.broadcasted_iota(jnp.int32, (1, lanes), 1)
    position = rep * span + lax.broadcasted_iota(jnp.int32, (1, span), 1)

    def request(r, state):
        pick = lane == r
        column = jnp.sum(jnp.where(pick, dec, 0.0), axis=1, keepdims=True)
        valid = position < len_ref[r]
        out = []
        for h in range(heads):
            query = column[3 * hd * h : 3 * hd * h + hd]
            key = cache_ref[r, h, :hd].astype(jnp.float32)
            value = cache_ref[r, h, hd:].astype(jnp.float32)
            score = jnp.sum(key * query, axis=0, keepdims=True) * scale
            score = jnp.where(valid, score, NEG)
            high = jnp.max(score, axis=1, keepdims=True)
            weight = jnp.where(valid, jnp.exp(score - high), 0.0)
            total = jnp.sum(weight, axis=1, keepdims=True)
            mixed = jnp.sum(value * weight, axis=1, keepdims=True)
            highs, totals, mixes = state[h]
            out.append(
                (
                    jnp.where(pick, high, highs),
                    jnp.where(pick, total, totals),
                    jnp.where(pick, mixed, mixes),
                )
            )
        return tuple(out)

    empty = tuple(
        (
            jnp.full((1, lanes), NEG, jnp.float32),
            jnp.zeros((1, lanes), jnp.float32),
            jnp.zeros((hd, lanes), jnp.float32),
        )
        for _ in range(heads)
    )
    state = lax.fori_loop(0, cache_ref.shape[0], request, empty)
    for h in range(heads):
        states[rep, h, :hd] = state[h][2]
        states[rep, h, hd : hd + 8] = jnp.broadcast_to(state[h][0], (8, lanes))
        states[rep, h, hd + 8 : hd + 16] = jnp.broadcast_to(state[h][1], (8, lanes))
    sent = [
        copies.start(states.at[rep], states.at[rep], {"rep": lax.rem(rep + k, reps)})
        for k in range(1, reps)
    ]
    gather.middle()
    for copy in sent:
        copy.wait_recv()
    for h in range(heads):
        base = 3 * hd * h
        query, key, value = (dec[base + hd * k : base + hd * (k + 1)] for k in range(3))
        own = jnp.sum(query * key, axis=0, keepdims=True) * scale
        highest = own
        for k in range(reps):
            highest = jnp.maximum(highest, states[k, h, hd : hd + 1])
        own_weight = jnp.exp(own - highest)
        total, mixed = own_weight, own_weight * value
        for k in range(reps):
            factor = jnp.exp(states[k, h, hd : hd + 1] - highest)
            total = total + factor * states[k, h, hd + 8 : hd + 9]
            mixed = mixed + factor * states[k, h, :hd]
        attn_ref[:, hd * h : hd * (h + 1)] = (mixed / total).T[: attn_ref.shape[0]].astype(
            attn_ref.dtype
        )
    gather.last()

    @pl.loop(0, SIDE)
    def _(i):
        block = rows[pl.ds(SIDE * i, SIDE)].reshape(SIDE * ROWS, rows.shape[2])
        out_ref[:, pl.ds(pl.multiple_of(i * SIDE * ROWS, SIDE * ROWS), SIDE * ROWS)] = (
            lax.dot_general(w_ref[...], block, NT, preferred_element_type=jnp.float32).astype(
                out_ref.dtype
            )
        )

    for copy in spread:
        copy.wait_recv()
    keep_w.wait()
    copies.drain()


def attend_kernel(
    scale, offset_ref, seg_ref, qkv_ref, kv_ref, seg_row, out_ref, q_ref, m_ref, l_ref, acc_ref
):
    head = pl.program_id(0)
    hd = q_ref.shape[1]
    span = seg_row.shape[1]
    block, key_block = 256, 1024
    factor = scale * LOG2E
    q_ref[...] = qkv_ref[0, 0].astype(jnp.float32).T.astype(jnp.bfloat16)
    offset = offset_ref[0]
    seg_keys = seg_row[...].astype(jnp.float32)
    seg_rows = jnp.broadcast_to(seg_keys, (8, span)).T[:, :1]

    def absorb(score, values):
        high = jnp.maximum(m_ref[...], jnp.max(score, axis=1, keepdims=True))
        decay = jnp.exp2((m_ref[...] - high) * factor)
        weight = jnp.exp2((score - high) * factor)
        m_ref[...] = high
        l_ref[...] = l_ref[...] * decay + jnp.sum(weight, axis=1, keepdims=True)
        acc_ref[...] = acc_ref[...] * decay + lax.dot_general(
            weight.astype(jnp.bfloat16), values, NT, preferred_element_type=jnp.float32
        )

    for i in range(span // block):
        rows = slice(i * block, (i + 1) * block)
        m_ref[...] = jnp.full(m_ref.shape, NEG, jnp.float32)
        l_ref[...] = jnp.zeros(l_ref.shape, jnp.float32)
        acc_ref[...] = jnp.zeros(acc_ref.shape, jnp.float32)
        seg_q = seg_rows[rows]
        if (i * block) < span // 2:

            @pl.when((seg_ref[0, i * block] == 0) & (offset > 0))
            def _():
                @pl.loop(0, lax.div(offset + (key_block - 1), key_block))
                def _(j):
                    at = pl.multiple_of(j * key_block, key_block)
                    score = jnp.dot(
                        q_ref[rows],
                        kv_ref[0, :hd, pl.ds(at, key_block)],
                        preferred_element_type=jnp.float32,
                    )
                    where = at + lax.broadcasted_iota(jnp.int32, (1, key_block), 1)
                    absorb(
                        jnp.where(where < offset, score, NEG),
                        kv_ref[0, hd:, pl.ds(at, key_block)],
                    )

                keep = seg_q == 0
                m_ref[...] = jnp.where(keep, m_ref[...], NEG)
                l_ref[...] = jnp.where(keep, l_ref[...], 0.0)
                acc_ref[...] = jnp.where(keep, acc_ref[...], 0.0)

        low = max(0, (i - span // 2 // block) * block)
        high = (i + 1) * block
        score = jnp.dot(
            q_ref[rows], qkv_ref[0, 1, :, low:high], preferred_element_type=jnp.float32
        )
        shape = (block, high - low)
        query_at = i * block + lax.broadcasted_iota(jnp.int32, shape, 0)
        key_at = low + lax.broadcasted_iota(jnp.int32, shape, 1)
        seen = (seg_keys[:, low:high] == seg_q) & (key_at <= query_at)
        absorb(jnp.where(seen, score, NEG), qkv_ref[0, 2, :, low:high])
        result = (acc_ref[...] / l_ref[...]).astype(out_ref.dtype)
        for h in range(out_ref.shape[1] // hd):

            @pl.when(head == h)
            def _():
                out_ref[rows, h * hd : (h + 1) * hd] = result


def tail_kernel(
    dec_attn_ref,
    x_dec_ref,
    up_bias_ref,
    biases_ref,
    gains_ref,
    shifts_ref,
    attn_hbm,
    x_hbm,
    w_row_hbm,
    w_up_hbm,
    w_down_hbm,
    rows,
    out_ref,
    dec_out_ref,
    x_ref,
    w_row_ref,
    w_up_ref,
    w_down_ref,
    heads_ref,
    slabs,
    parts,
    far,
    near,
    row,
    row_far,
    row_near,
    over_x,
    over_y,
    local_sem,
    send_sem,
    recv_sem,
):
    loads = []
    for k, (source, target) in enumerate(
        ((w_row_hbm, w_row_ref), (x_hbm, x_ref), (w_up_hbm, w_up_ref), (w_down_hbm, w_down_ref))
    ):
        loads.append(pltpu.make_async_copy(source, target, local_sem.at[k]))
        loads[-1].start()
    y, x, a, b, device = place()
    copies = Copies(send_sem, recv_sem)

    def tokens(i, j):
        at = pl.multiple_of(device(i, j) * ROWS, ROWS)
        return attn_hbm.at[pl.ds(at, ROWS)]

    for i in range(SIDE):
        loads.append(
            pltpu.make_async_copy(tokens(i, b), heads_ref.at[b, i], local_sem.at[4 + i])
        )
        loads[-1].start()
    greet(
        [SIDE * y + lax.rem(x + k, SIDE) for k in (1, 2, 3)]
        + [SIDE * lax.rem(y + k, SIDE) + x for k in (1, 2, 3)]
    )
    width = x_ref.shape[1]
    chunk = (SIDE, ROWS, width)

    swaps = [
        copies.start(tokens(i, b + k), heads_ref.at[b, i], tensor(device(a, b + k)))
        for k in (2, 1, 3)
        for i in range(SIDE)
    ]
    loads[0].wait()
    dec_sum = SmallSum(copies, over_x.at[0], over_y.at[0])
    dec_sum.begin(
        jnp.dot(dec_attn_ref[...], w_row_ref[b], preferred_element_type=jnp.float32)
    )
    for load in loads[4:]:
        load.wait()
    for swap in swaps:
        swap.wait_recv()
    ring = RingSum(
        copies, row.at[0], row_far.at[0], row_near.at[0], a, lambda i: tensor(device(i, b))
    )

    def out_share(k):
        left = heads_ref[:, lax.rem(a + k, SIDE)]
        total = sum(
            jnp.dot(left[j], w_row_ref[j], preferred_element_type=jnp.float32)
            for j in range(SIDE)
        )
        return total

    ring.row(2)[...] = out_share(2).astype(jnp.bfloat16)
    ring.send_far()
    ring.row(1)[...] = out_share(1).astype(jnp.bfloat16)
    ring.send_next()
    ring.row(3)[...] = out_share(3).astype(jnp.bfloat16)
    ring.send_prev()
    ring.pass_on()
    dec_sum.middle()
    own = out_share(0)
    dec_first = layer_norm(
        x_dec_ref[...].astype(jnp.float32) + dec_sum.finish() + biases_ref[0:1],
        gains_ref[0:1],
        shifts_ref[0:1],
    ).astype(jnp.bfloat16)
    loads[1].wait()
    attn_sum = ring.finish(own)
    first = layer_norm(
        x_ref[...].astype(jnp.float32) + attn_sum + biases_ref[0:1], gains_ref[0:1], shifts_ref[0:1]
    ).astype(jnp.bfloat16)

    def slab(i, j):
        return slabs.at[lax.rem(i, SIDE), lax.rem(j, SIDE)]

    slab(a, b)[...] = first
    gather = Gather(copies, slab)
    gather.begin()
    loads[2].wait()
    loads[3].wait()

    def mlp(value):
        inner = jnp.dot(value, w_up_ref[...], preferred_element_type=jnp.float32)
        inner = inner + up_bias_ref[...][None, :]
        hidden = (0.5 * inner * (1.0 + lax.erf(inner * 0.7071067811865476))).astype(jnp.bfloat16)
        return jnp.dot(hidden, w_down_ref[...], preferred_element_type=jnp.float32)

    dec_sum = SmallSum(copies, over_x.at[1], over_y.at[1])
    dec_sum.begin(mlp(dec_first))

    def mlp_share(i):
        at = lax.rem(i, SIDE)
        parts[at] = (
            mlp(slabs[at].reshape(SIDE * ROWS, width)).astype(jnp.bfloat16).reshape(chunk)
        )

    scatter = Scatter(copies, parts, far, near, row.at[1], row_far.at[1], row_near.at[1])
    gather.first()
    mlp_share(a)
    gather.middle()
    mlp_share(a + 1)
    mlp_share(a + 3)
    scatter.send_near()
    dec_sum.middle()
    gather.last()
    mlp_share(a + 2)
    scatter.send_far()
    dec_out = layer_norm(
        dec_first.astype(jnp.float32) + dec_sum.finish() + biases_ref[1:2],
        gains_ref[1:2],
        shifts_ref[1:2],
    ).astype(jnp.bfloat16)
    dec_out_ref[...] = dec_out
    scatter.pass_on()
    mlp_sum = scatter.finish()
    second = layer_norm(
        first.astype(jnp.float32) + mlp_sum + biases_ref[1:2], gains_ref[1:2], shifts_ref[1:2]
    ).astype(jnp.bfloat16)
    out_ref[...] = second
    keep = pltpu.make_async_copy(out_ref, rows.at[device(a, b)], local_sem.at[0])
    keep.start()
    gather = Gather(copies, lambda i, j: rows.at[device(i, j)], out_ref)
    gather.begin()
    gather.first()
    gather.middle()
    gather.last()
    keep.wait()
    copies.drain()


def next_kernel(rows_ref, own_ref, dec_ref, w_ref, next_ref, out_ref, dec_out_ref, dec_next_ref):
    block = rows_ref[...].reshape(SIDE * ROWS, rows_ref.shape[2])
    next_ref[...] = lax.dot_general(
        w_ref[...], block, NT, preferred_element_type=jnp.float32
    ).astype(next_ref.dtype)

    @pl.when(pl.program_id(0) == 0)
    def _():
        out_ref[...] = own_ref[...]
        dec_out_ref[...] = dec_ref[...]
        dec_next_ref[...] = lax.dot_general(
            dec_ref[...], w_ref[...], NT, preferred_element_type=jnp.float32
        ).astype(dec_next_ref.dtype)


def per_device(
    reps,
    x_pre,
    x_dec,
    prefix_kv,
    cache_kv,
    dec_len,
    offsets,
    segments,
    w_qkv,
    w_out,
    w_up,
    up_bias,
    w_down,
    biases,
    gains,
    shifts,
    w_next,
):
    heads = prefix_kv.shape[2]
    hd = prefix_kv.shape[3] // 2
    span = segments.shape[1]
    width = x_pre.shape[1]
    decodes = x_dec.shape[0]
    columns = w_qkv.shape[1]
    units = w_up.shape[1]
    scale = hd ** (-0.5)
    bf16, f32 = jnp.bfloat16, jnp.float32
    shape = jax.ShapeDtypeStruct
    whole = pl.BlockSpec(memory_space=VMEM)
    scalars = pl.BlockSpec(memory_space=pltpu.SMEM)
    anywhere = pl.BlockSpec(memory_space=pltpu.HBM)
    group = SIDE * SIDE

    cache_t = cache_kv.transpose(0, 2, 3, 1)
    planes = reps // 2
    n_copies = 16 + reps - 1 + (SIDE - 1) * planes
    qkv_t, dec_attn, w_row = pl.pallas_call(
        functools.partial(project_kernel, reps, scale),
        out_shape=(
            shape((columns, span), bf16),
            shape((decodes, heads * hd), bf16),
            shape((SIDE,) + w_out.shape, bf16),
        ),
        in_specs=[scalars, whole] + [anywhere] * 4,
        out_specs=(whole, whole, anywhere),
        scratch_shapes=[
            VMEM((group, ROWS, width), bf16),
            VMEM((128, width), bf16),
            VMEM((columns, width), bf16),
            VMEM(cache_t.shape, bf16),
            VMEM((reps, heads, hd + 16, 128), f32),
            pltpu.SemaphoreType.DMA((4,)),
            pltpu.SemaphoreType.DMA((n_copies,)),
            pltpu.SemaphoreType.DMA((n_copies,)),
        ],
        compiler_params=pltpu.CompilerParams(
            collective_id=0, has_side_effects=True, vmem_limit_bytes=62 << 20
        ),
        name="project",
    )(dec_len, x_dec, x_pre, w_qkv.T, cache_t, w_out)

    attn = pl.pallas_call(
        functools.partial(attend_kernel, scale),
        grid=(heads,),
        out_shape=shape((span, heads * hd), bf16),
        in_specs=[
            scalars,
            scalars,
            pl.BlockSpec((1, 3, hd, span), lambda h: (h, 0, 0, 0)),
            pl.BlockSpec((1, 2 * hd, prefix_kv.shape[1]), lambda h: (h, 0, 0)),
            pl.BlockSpec((1, span), lambda h: (0, 0)),
        ],
        out_specs=pl.BlockSpec((span, heads * hd), lambda h: (0, 0)),
        scratch_shapes=[
            VMEM((span, hd), bf16),
            VMEM((256, 1), f32),
            VMEM((256, 1), f32),
            VMEM((256, hd), f32),
        ],
        compiler_params=pltpu.CompilerParams(
            dimension_semantics=("arbitrary",), vmem_limit_bytes=48 << 20
        ),
        name="attend",
    )(
        offsets,
        segments,
        qkv_t.reshape(heads, 3, hd, span),
        prefix_kv[0].transpose(1, 2, 0),
        segments,
    )

    n_copies = 2 * (16 + 6) + 12 + 12 + 6 + 6
    rows, own, dec_own = pl.pallas_call(
        tail_kernel,
        out_shape=(
            shape((group, ROWS, width), bf16),
            shape((ROWS, width), bf16),
            shape((decodes, width), bf16),
        ),
        in_specs=[whole] * 6 + [anywhere] * 5,
        out_specs=(anywhere, whole, whole),
        scratch_shapes=[
            VMEM((ROWS, width), bf16),
            VMEM((SIDE,) + w_out.shape, bf16),
            VMEM((width, units), bf16),
            VMEM((units, width), bf16),
            VMEM((SIDE, SIDE, ROWS, heads * hd), bf16),
            VMEM((SIDE, SIDE, ROWS, width), bf16),
            VMEM((SIDE, SIDE, ROWS, width), bf16),
            VMEM((2, 2, ROWS, width), bf16),
            VMEM((2, SIDE, ROWS, width), bf16),
            VMEM((2, SIDE, ROWS, width), bf16),
            VMEM((2, 2, ROWS // 2, width), bf16),
            VMEM((2, 2, ROWS, width), bf16),
            VMEM((2, SIDE, decodes, width), bf16),
            VMEM((2, SIDE, decodes, width), bf16),
            pltpu.SemaphoreType.DMA((8,)),
            pltpu.SemaphoreType.DMA((n_copies,)),
            pltpu.SemaphoreType.DMA((n_copies,)),
        ],
        compiler_params=pltpu.CompilerParams(
            collective_id=1, has_side_effects=True, vmem_limit_bytes=60 << 20
        ),
        name="tail",
    )(
        dec_attn,
        x_dec,
        up_bias,
        biases,
        gains,
        shifts,
        attn,
        x_pre,
        w_row,
        w_up,
        w_down,
    )

    next_t, layer_out, dec_out, dec_next = pl.pallas_call(
        next_kernel,
        grid=(SIDE,),
        out_shape=(
            shape((columns, span), bf16),
            shape((ROWS, width), bf16),
            shape((decodes, width), bf16),
            shape((decodes, columns), bf16),
        ),
        in_specs=[
            pl.BlockSpec((SIDE, ROWS, width), lambda i: (i, 0, 0)),
            pl.BlockSpec((ROWS, width), lambda i: (0, 0)),
            pl.BlockSpec((decodes, width), lambda i: (0, 0)),
            pl.BlockSpec((columns, width), lambda i: (0, 0)),
        ],
        out_specs=(
            pl.BlockSpec((columns, SIDE * ROWS), lambda i: (0, i)),
            pl.BlockSpec((ROWS, width), lambda i: (0, 0)),
            pl.BlockSpec((decodes, width), lambda i: (0, 0)),
            pl.BlockSpec((decodes, columns), lambda i: (0, 0)),
        ),
        compiler_params=pltpu.CompilerParams(
            dimension_semantics=("arbitrary",), vmem_limit_bytes=48 << 20
        ),
        name="next",
    )(rows, own, dec_own, w_next.T)
    return layer_out, next_t.T, dec_out, dec_next


def solution(mesh):
    placed = (
        P(("rep", "tensor"), None),
        P(),
        P("rep", None, "tensor", None),
        P(None, "rep", "tensor", None),
        P(),
        P("rep"),
        P("rep", None),
        P(None, "tensor"),
        P("tensor", None),
        P(None, "tensor"),
        P("tensor"),
        P("tensor", None),
        P(),
        P(),
        P(),
        P(None, "tensor"),
    )
    return jax.shard_map(
        functools.partial(per_device, mesh.shape["rep"]),
        mesh=mesh,
        in_specs=placed,
        out_specs=(P(("rep", "tensor"), None), P("rep", "tensor"), P(), P(None, "tensor")),
        check_vma=False,
    )
```

```python
import functools

import jax
import jax.numpy as jnp
from jax import lax
from jax.experimental import pallas as pl
from jax.experimental.pallas import tpu as pltpu
from jax.sharding import PartitionSpec as P

MESH = pl.DeviceIdType.MESH
NEG = -1e30
LOG2E = 1.4426950408889634
SIDE = 4
ROWS = 64
VMEM = pltpu.VMEM
NT = (((1,), (1,)), ((), ()))


def place():
    t = lax.axis_index("tensor")
    core = lax.rem(lax.axis_index("rep"), 2)
    y, x = lax.div(t, SIDE), lax.rem(t, SIDE)
    major = y * (1 - core) + x * core
    minor = x * (1 - core) + y * core
    step_major, step_minor = SIDE - (SIDE - 1) * core, 1 + (SIDE - 1) * core

    def device(i, j):
        return lax.rem(i, SIDE) * step_major + lax.rem(j, SIDE) * step_minor

    return y, x, major, minor, device


class Copies:
    def __init__(self, send, recv):
        self.send, self.recv, self.used, self.all = send, recv, 0, []

    def start(self, src, dst, where):
        copy = pltpu.make_async_remote_copy(
            src_ref=src,
            dst_ref=dst,
            send_sem=self.send.at[self.used],
            recv_sem=self.recv.at[self.used],
            device_id=where,
            device_id_type=MESH,
        )
        copy.start()
        self.used += 1
        self.all.append(copy)
        return copy

    def drain(self):
        for copy in self.all:
            copy.wait_send()


def tensor(t):
    return {"tensor": t}


def greet(tensor_peers, rep_peers=()):
    barrier = pltpu.get_barrier_semaphore()
    for t in tensor_peers:
        pl.semaphore_signal(barrier, inc=1, device_id=tensor(t), device_id_type=MESH)
    for r in rep_peers:
        pl.semaphore_signal(barrier, inc=1, device_id={"rep": r}, device_id_type=MESH)
    pl.semaphore_wait(barrier, len(tensor_peers) + len(rep_peers))


class Gather:
    def __init__(self, copies, at, own=None):
        y, x, self.a, self.b, self.device = place()
        self.copies, self.at, self.own = copies, at, own

    def go(self, i, j, ti, tj):
        return self.copies.start(self.at(i, j), self.at(i, j), tensor(self.device(ti, tj)))

    def begin(self):
        a, b = self.a, self.b
        own = self.at(a, b) if self.own is None else self.own
        self.right, self.left, up, down = (
            self.copies.start(own, self.at(a, b), tensor(self.device(i, j)))
            for i, j in ((a, b + 1), (a, b + 3), (a + 1, b), (a + 3, b))
        )
        self.up, self.down = [up], [down]

    def spread(self, j):
        a, b = self.a, self.b
        self.up.append(self.go(a, j, a + 1, b))
        self.down.append(self.go(a, j, a + 3, b))

    def half(self, i, j, part):
        return self.at(i, j).at[pl.ds(part * (ROWS // 2), ROWS // 2)]

    def first(self):
        a, b = self.a, self.b
        self.right.wait_recv()
        one = self.half(a, b + 3, 0)
        far_one = self.copies.start(one, one, tensor(self.device(a, b + 1)))
        self.spread(b + 3)
        self.left.wait_recv()
        two = self.half(a, b + 1, 1)
        far_two = self.copies.start(two, two, tensor(self.device(a, b + 3)))
        self.spread(b + 1)
        far_one.wait_recv()
        far_two.wait_recv()
        self.spread(b + 2)

    def middle(self):
        a, b = self.a, self.b
        self.up[0].wait_recv()
        self.far = [self.go(a + 3, b, a + 1, b)]
        self.down[1].wait_recv()
        self.far.append(self.go(a + 1, b + 3, a + 3, b))
        self.down[2].wait_recv()
        self.far.append(self.go(a + 1, b + 1, a + 3, b))
        self.up[3].wait_recv()
        self.far.append(self.go(a + 3, b + 2, a + 1, b))
        self.up[1].wait_recv()
        self.up[2].wait_recv()
        self.down[0].wait_recv()
        self.down[3].wait_recv()

    def last(self):
        for copy in self.far:
            copy.wait_recv()


class RingSum:
    def __init__(self, copies, row, far, near, index, to):
        self.copies, self.slabs, self.far, self.near = copies, row, far, near
        self.c, self.next, self.prev = index, to(index + 1), to(index + 3)
        half = ROWS // 2
        self.top, self.low = pl.ds(0, half), pl.ds(half, half)

    def row(self, k):
        return self.slabs.at[lax.rem(self.c + k, SIDE)]

    def send_far(self):
        self.next_far = self.copies.start(self.row(2).at[self.top], self.far.at[0], self.next)
        self.prev_far = self.copies.start(self.row(2).at[self.low], self.far.at[1], self.prev)

    def send_next(self):
        self.next_near = self.copies.start(
            self.row(1).at[self.low], self.near.at[0, self.low], self.next
        )

    def send_prev(self):
        self.prev_near = self.copies.start(
            self.row(3).at[self.top], self.near.at[1, self.top], self.prev
        )

    def pass_on(self):
        self.next_far.wait_recv()
        add_into(self.row(1).at[self.top], self.far[0])
        self.next_sum = self.copies.start(
            self.row(1).at[self.top], self.near.at[0, self.top], self.next
        )
        self.prev_far.wait_recv()
        add_into(self.row(3).at[self.low], self.far[1])
        self.prev_sum = self.copies.start(
            self.row(3).at[self.low], self.near.at[1, self.low], self.prev
        )

    def finish(self, own):
        for copy in (self.next_near, self.prev_near, self.next_sum, self.prev_sum):
            copy.wait_recv()
        return own + self.near[0].astype(jnp.float32) + self.near[1].astype(jnp.float32)


def add_into(ref, value):
    ref[...] = (ref[...].astype(jnp.float32) + value.astype(jnp.float32)).astype(ref.dtype)


class Scatter:
    def __init__(self, copies, parts, far, near, row, row_far, row_near):
        y, x, a, b, self.device = place()
        self.a, self.b = a, b
        self.copies, self.parts, self.far, self.near = copies, parts, far, near
        self.ring = RingSum(
            copies, row, row_far, row_near, b, lambda j: tensor(self.device(a, j))
        )
        self.above, self.below = tensor(self.device(a + 1, b)), tensor(self.device(a + 3, b))
        self.ups, self.downs = (b + 2, b + 1), (b + 3, b)

    def part(self, i, j):
        return self.parts.at[lax.rem(i, SIDE), lax.rem(j, SIDE)]

    def landing(self, side, j):
        return self.near.at[side, lax.rem(j, SIDE)]

    def send_far(self):
        self.far_up, self.far_down = [], []
        for k in range(2):
            self.far_up.append(
                self.copies.start(self.part(self.a + 2, self.ups[k]), self.far.at[0, k], self.above)
            )
            self.far_down.append(
                self.copies.start(
                    self.part(self.a + 2, self.downs[k]), self.far.at[1, k], self.below
                )
            )

    def send_near(self):
        self.near_up, self.near_down = [], []
        for k in range(2):
            self.near_up.append(
                self.copies.start(
                    self.part(self.a + 1, self.downs[k]),
                    self.landing(0, self.downs[k]),
                    self.above,
                )
            )
            self.near_down.append(
                self.copies.start(
                    self.part(self.a + 3, self.ups[k]), self.landing(1, self.ups[k]), self.below
                )
            )

    def pass_on(self):
        self.sum_up, self.sum_down = [], []
        for k in range(2):
            self.far_up[k].wait_recv()
            add_into(self.part(self.a + 1, self.ups[k]), self.far[0, k])
            self.sum_up.append(
                self.copies.start(
                    self.part(self.a + 1, self.ups[k]), self.landing(0, self.ups[k]), self.above
                )
            )
            self.far_down[k].wait_recv()
            add_into(self.part(self.a + 3, self.downs[k]), self.far[1, k])
            self.sum_down.append(
                self.copies.start(
                    self.part(self.a + 3, self.downs[k]),
                    self.landing(1, self.downs[k]),
                    self.below,
                )
            )

    def total(self, j):
        at = lax.rem(j, SIDE)
        return (
            self.parts[self.a, at].astype(jnp.float32)
            + self.near[0, at].astype(jnp.float32)
            + self.near[1, at].astype(jnp.float32)
        )

    def finish(self):
        ring, b = self.ring, self.b
        self.sum_up[0].wait_recv()
        self.near_down[0].wait_recv()
        ring.row(2)[...] = self.total(b + 2).astype(jnp.bfloat16)
        ring.send_far()
        self.near_up[0].wait_recv()
        self.sum_down[0].wait_recv()
        ring.row(3)[...] = self.total(b + 3).astype(jnp.bfloat16)
        ring.send_prev()
        self.sum_up[1].wait_recv()
        self.near_down[1].wait_recv()
        ring.row(1)[...] = self.total(b + 1).astype(jnp.bfloat16)
        ring.send_next()
        ring.pass_on()
        self.near_up[1].wait_recv()
        self.sum_down[1].wait_recv()
        return ring.finish(self.total(b))


class SmallSum:
    def __init__(self, copies, over_x, over_y):
        t = lax.axis_index("tensor")
        self.y, self.x = lax.div(t, SIDE), lax.rem(t, SIDE)
        self.copies, self.over_x, self.over_y = copies, over_x, over_y

    def begin(self, value):
        self.over_x[self.x] = value.astype(jnp.bfloat16)
        mine = self.over_x.at[self.x]
        self.sent = [
            self.copies.start(
                mine, mine, tensor(SIDE * self.y + lax.rem(self.x + k, SIDE))
            )
            for k in (1, 2, 3)
        ]

    def middle(self):
        for copy in self.sent:
            copy.wait_recv()
        self.over_y[self.y] = sum(
            self.over_x[k].astype(jnp.float32) for k in range(SIDE)
        ).astype(jnp.bfloat16)
        mine = self.over_y.at[self.y]
        self.sent = [
            self.copies.start(
                mine, mine, tensor(SIDE * lax.rem(self.y + k, SIDE) + self.x)
            )
            for k in (1, 2, 3)
        ]

    def finish(self):
        for copy in self.sent:
            copy.wait_recv()
        return sum(self.over_y[k].astype(jnp.float32) for k in range(SIDE))


def layer_norm(values, gain_row, shift_row):
    average = jnp.mean(values, axis=-1, keepdims=True)
    centred = values - average
    spread = jnp.mean(centred * centred, axis=-1, keepdims=True)
    return centred * lax.rsqrt(spread + 1e-05) * gain_row + shift_row


def project_kernel(
    reps,
    scale,
    len_ref,
    dec_ref,
    x_hbm,
    w_hbm,
    cache_hbm,
    w_out_hbm,
    out_ref,
    attn_ref,
    w_row_hbm,
    rows,
    dec_rows,
    w_ref,
    cache_ref,
    states,
    local_sem,
    send_sem,
    recv_sem,
):
    y, x, a, b, device = place()
    load_x = pltpu.make_async_copy(x_hbm, rows.at[device(a, b)], local_sem.at[2])
    load_x.start()
    load_w = pltpu.make_async_copy(w_hbm, w_ref, local_sem.at[0])
    load_w.start()
    load_cache = pltpu.make_async_copy(cache_hbm, cache_ref, local_sem.at[1])
    load_cache.start()
    keep_w = pltpu.make_async_copy(w_out_hbm, w_row_hbm.at[b], local_sem.at[3])
    keep_w.start()
    rep = lax.axis_index("rep")
    copies = Copies(send_sem, recv_sem)
    greet(
        [device(a, b + k) for k in (1, 2, 3)] + [device(a + 1, b), device(a + 3, b)],
        [lax.rem(rep + k, reps) for k in range(1, reps)],
    )
    gather = Gather(copies, lambda i, j: rows.at[device(i, j)])
    planes = reps // 2
    quarter = w_out_hbm.shape[1] // planes
    mine = pl.ds(pl.multiple_of(lax.div(rep, 2) * quarter, 128), quarter)
    shards = [
        copies.start(
            w_out_hbm.at[:, mine], w_row_hbm.at[b, :, mine], tensor(device(a, b + k))
        )
        for k in (1, 3, 2)
    ]
    load_x.wait()
    gather.begin()
    dec_rows[...] = jnp.zeros_like(dec_rows)
    dec_rows[: dec_ref.shape[0]] = dec_ref[...]
    spread = []
    for k, shard in zip((1, 3, 2), shards):
        shard.wait_recv()
        piece = w_row_hbm.at[lax.rem(b - k + SIDE, SIDE), :, mine]
        spread += [
            copies.start(piece, piece, {"rep": lax.rem(rep + 2 * p, reps)})
            for p in range(1, planes)
        ]
    load_w.wait()
    dec = (
        lax.dot_general(w_ref[...], dec_rows[...], NT, preferred_element_type=jnp.float32)
        .astype(jnp.bfloat16)
        .astype(jnp.float32)
    )
    gather.first()
    load_cache.wait()
    hd = cache_ref.shape[2] // 2
    heads = cache_ref.shape[1]
    span = cache_ref.shape[3]
    lanes = dec.shape[1]
    lane = lax.broadcasted_iota(jnp.int32, (1, lanes), 1)
    position = rep * span + lax.broadcasted_iota(jnp.int32, (1, span), 1)

    def request(r, state):
        pick = lane == r
        column = jnp.sum(jnp.where(pick, dec, 0.0), axis=1, keepdims=True)
        valid = position < len_ref[r]
        out = []
        for h in range(heads):
            query = column[3 * hd * h : 3 * hd * h + hd]
            key = cache_ref[r, h, :hd].astype(jnp.float32)
            value = cache_ref[r, h, hd:].astype(jnp.float32)
            score = jnp.sum(key * query, axis=0, keepdims=True) * scale
            score = jnp.where(valid, score, NEG)
            high = jnp.max(score, axis=1, keepdims=True)
            weight = jnp.where(valid, jnp.exp(score - high), 0.0)
            total = jnp.sum(weight, axis=1, keepdims=True)
            mixed = jnp.sum(value * weight, axis=1, keepdims=True)
            highs, totals, mixes = state[h]
            out.append(
                (
                    jnp.where(pick, high, highs),
                    jnp.where(pick, total, totals),
                    jnp.where(pick, mixed, mixes),
                )
            )
        return tuple(out)

    empty = tuple(
        (
            jnp.full((1, lanes), NEG, jnp.float32),
            jnp.zeros((1, lanes), jnp.float32),
            jnp.zeros((hd, lanes), jnp.float32),
        )
        for _ in range(heads)
    )
    state = lax.fori_loop(0, cache_ref.shape[0], request, empty)
    for h in range(heads):
        states[rep, h, :hd] = state[h][2]
        states[rep, h, hd : hd + 8] = jnp.broadcast_to(state[h][0], (8, lanes))
        states[rep, h, hd + 8 : hd + 16] = jnp.broadcast_to(state[h][1], (8, lanes))
    sent = [
        copies.start(states.at[rep], states.at[rep], {"rep": lax.rem(rep + k, reps)})
        for k in range(1, reps)
    ]
    gather.middle()
    for copy in sent:
        copy.wait_recv()
    for h in range(heads):
        base = 3 * hd * h
        query, key, value = (dec[base + hd * k : base + hd * (k + 1)] for k in range(3))
        own = jnp.sum(query * key, axis=0, keepdims=True) * scale
        highest = own
        for k in range(reps):
            highest = jnp.maximum(highest, states[k, h, hd : hd + 1])
        own_weight = jnp.exp(own - highest)
        total, mixed = own_weight, own_weight * value
        for k in range(reps):
            factor = jnp.exp(states[k, h, hd : hd + 1] - highest)
            total = total + factor * states[k, h, hd + 8 : hd + 9]
            mixed = mixed + factor * states[k, h, :hd]
        attn_ref[:, hd * h : hd * (h + 1)] = (mixed / total).T[: attn_ref.shape[0]].astype(
            attn_ref.dtype
        )
    gather.last()

    @pl.loop(0, SIDE)
    def _(i):
        block = rows[pl.ds(SIDE * i, SIDE)].reshape(SIDE * ROWS, rows.shape[2])
        out_ref[:, pl.ds(pl.multiple_of(i * SIDE * ROWS, SIDE * ROWS), SIDE * ROWS)] = (
            lax.dot_general(w_ref[...], block, NT, preferred_element_type=jnp.float32).astype(
                out_ref.dtype
            )
        )

    for copy in spread:
        copy.wait_recv()
    keep_w.wait()
    copies.drain()


def attend_kernel(scale, offset_ref, seg_ref, qkv_ref, kv_ref, seg_row, out_ref, q_ref, *state):
    head = pl.program_id(0)
    hd = q_ref.shape[1]
    span = seg_row.shape[1]
    block, key_block = 256, 1024
    early = span // 2 // block
    factor = scale * LOG2E
    q_ref[...] = qkv_ref[0, 0].astype(jnp.float32).T.astype(jnp.bfloat16)
    offset = offset_ref[0]
    seg_keys = seg_row[...].astype(jnp.float32)
    seg_rows = jnp.broadcast_to(seg_keys, (8, span)).T[:, :1]
    states = [state[3 * i : 3 * i + 3] for i in range(early)]

    def rows(i):
        return slice(i * block, (i + 1) * block)

    def mix(weight, values):
        return lax.dot_general(
            weight.astype(jnp.bfloat16), values, NT, preferred_element_type=jnp.float32
        )

    def absorb(i, score, values):
        m_ref, l_ref, acc_ref = states[i]
        high = jnp.maximum(m_ref[...], jnp.max(score, axis=1, keepdims=True))
        decay = jnp.exp2((m_ref[...] - high) * factor)
        weight = jnp.exp2((score - high) * factor)
        m_ref[...] = high
        l_ref[...] = l_ref[...] * decay + jnp.sum(weight, axis=1, keepdims=True)
        acc_ref[...] = acc_ref[...] * decay + mix(weight, values)

    def prefix(count):
        def step(j, partial):
            at = pl.multiple_of(j * key_block, key_block)
            keys = kv_ref[0, :hd, pl.ds(at, key_block)]
            values = kv_ref[0, hd:, pl.ds(at, key_block)]
            where = at + lax.broadcasted_iota(jnp.int32, (1, key_block), 1)
            scores = [
                jnp.dot(q_ref[rows(i)], keys, preferred_element_type=jnp.float32)
                for i in range(count)
            ]
            for i, score in enumerate(scores):
                absorb(i, jnp.where(where < offset, score, NEG) if partial else score, values)

        full = lax.div(offset, key_block)
        pl.loop(0, full)(lambda j: step(j, False))
        pl.when(full * key_block < offset)(lambda: step(full, True))

    for m_ref, l_ref, acc_ref in states:
        m_ref[...] = jnp.full(m_ref.shape, NEG, jnp.float32)
        l_ref[...] = jnp.zeros(l_ref.shape, jnp.float32)
        acc_ref[...] = jnp.zeros(acc_ref.shape, jnp.float32)
    seen_to = sum(jnp.where(seg_ref[0, i * block] == 0, 1, 0) for i in range(early))
    for count in range(1, early + 1):
        pl.when((seen_to == count) & (offset > 0))(functools.partial(prefix, count))

    results = []
    for i in range(span // block):
        low = max(0, (i - early) * block)
        high = (i + 1) * block
        seg_q = seg_rows[rows(i)]
        score = jnp.dot(
            q_ref[rows(i)], qkv_ref[0, 1, :, low:high], preferred_element_type=jnp.float32
        )
        shape = (block, high - low)
        query_at = i * block + lax.broadcasted_iota(jnp.int32, shape, 0)
        key_at = low + lax.broadcasted_iota(jnp.int32, shape, 1)
        seen = (seg_keys[:, low:high] == seg_q) & (key_at <= query_at)
        score = jnp.where(seen, score, NEG)
        values = qkv_ref[0, 2, :, low:high]
        peak = jnp.max(score, axis=1, keepdims=True)
        if i < early:
            m_ref, l_ref, acc_ref = states[i]
            keep = seg_q == 0
            before = jnp.where(keep, m_ref[...], NEG)
            peak = jnp.maximum(peak, before)
            decay = jnp.where(keep, jnp.exp2((before - peak) * factor), 0.0)
        weight = jnp.exp2((score - peak) * factor)
        total = jnp.sum(weight, axis=1, keepdims=True)
        mixed = mix(weight, values)
        if i < early:
            total = total + l_ref[...] * decay
            mixed = mixed + acc_ref[...] * decay
        results.append((mixed / total).astype(out_ref.dtype))
    for h in range(out_ref.shape[1] // hd):

        @pl.when(head == h)
        def _():
            for i, result in enumerate(results):
                out_ref[rows(i), h * hd : (h + 1) * hd] = result


def tail_kernel(
    dec_attn_ref,
    x_dec_ref,
    up_bias_ref,
    biases_ref,
    gains_ref,
    shifts_ref,
    attn_hbm,
    x_hbm,
    w_row_hbm,
    w_up_hbm,
    w_down_hbm,
    rows,
    out_ref,
    dec_out_ref,
    x_ref,
    w_row_ref,
    w_up_ref,
    w_down_ref,
    heads_ref,
    slabs,
    parts,
    far,
    near,
    row,
    row_far,
    row_near,
    over_x,
    over_y,
    local_sem,
    send_sem,
    recv_sem,
):
    loads = []
    for k, (source, target) in enumerate(
        ((w_row_hbm, w_row_ref), (x_hbm, x_ref), (w_up_hbm, w_up_ref), (w_down_hbm, w_down_ref))
    ):
        loads.append(pltpu.make_async_copy(source, target, local_sem.at[k]))
        loads[-1].start()
    y, x, a, b, device = place()
    copies = Copies(send_sem, recv_sem)

    def tokens(i, j):
        at = pl.multiple_of(device(i, j) * ROWS, ROWS)
        return attn_hbm.at[pl.ds(at, ROWS)]

    for i in range(SIDE):
        loads.append(
            pltpu.make_async_copy(tokens(i, b), heads_ref.at[b, i], local_sem.at[4 + i])
        )
        loads[-1].start()
    greet(
        [SIDE * y + lax.rem(x + k, SIDE) for k in (1, 2, 3)]
        + [SIDE * lax.rem(y + k, SIDE) + x for k in (1, 2, 3)]
    )
    width = x_ref.shape[1]
    chunk = (SIDE, ROWS, width)

    swaps = [
        copies.start(tokens(i, b + k), heads_ref.at[b, i], tensor(device(a, b + k)))
        for k in (2, 1, 3)
        for i in range(SIDE)
    ]
    loads[0].wait()
    dec_sum = SmallSum(copies, over_x.at[0], over_y.at[0])
    dec_sum.begin(
        jnp.dot(dec_attn_ref[...], w_row_ref[b], preferred_element_type=jnp.float32)
    )
    for load in loads[4:]:
        load.wait()
    for swap in swaps:
        swap.wait_recv()
    ring = RingSum(
        copies, row.at[0], row_far.at[0], row_near.at[0], a, lambda i: tensor(device(i, b))
    )

    def out_share(k):
        left = heads_ref[:, lax.rem(a + k, SIDE)]
        total = sum(
            jnp.dot(left[j], w_row_ref[j], preferred_element_type=jnp.float32)
            for j in range(SIDE)
        )
        return total

    ring.row(2)[...] = out_share(2).astype(jnp.bfloat16)
    ring.send_far()
    ring.row(1)[...] = out_share(1).astype(jnp.bfloat16)
    ring.send_next()
    ring.row(3)[...] = out_share(3).astype(jnp.bfloat16)
    ring.send_prev()
    ring.pass_on()
    dec_sum.middle()
    own = out_share(0)
    dec_first = layer_norm(
        x_dec_ref[...].astype(jnp.float32) + dec_sum.finish() + biases_ref[0:1],
        gains_ref[0:1],
        shifts_ref[0:1],
    ).astype(jnp.bfloat16)
    loads[1].wait()
    attn_sum = ring.finish(own)
    first = layer_norm(
        x_ref[...].astype(jnp.float32) + attn_sum + biases_ref[0:1], gains_ref[0:1], shifts_ref[0:1]
    ).astype(jnp.bfloat16)

    def slab(i, j):
        return slabs.at[lax.rem(i, SIDE), lax.rem(j, SIDE)]

    slab(a, b)[...] = first
    gather = Gather(copies, slab)
    gather.begin()
    loads[2].wait()
    loads[3].wait()

    def mlp(value):
        inner = jnp.dot(value, w_up_ref[...], preferred_element_type=jnp.float32)
        inner = inner + up_bias_ref[...][None, :]
        hidden = (0.5 * inner * (1.0 + lax.erf(inner * 0.7071067811865476))).astype(jnp.bfloat16)
        return jnp.dot(hidden, w_down_ref[...], preferred_element_type=jnp.float32)

    dec_sum = SmallSum(copies, over_x.at[1], over_y.at[1])
    dec_sum.begin(mlp(dec_first))

    def mlp_share(i):
        at = lax.rem(i, SIDE)
        parts[at] = (
            mlp(slabs[at].reshape(SIDE * ROWS, width)).astype(jnp.bfloat16).reshape(chunk)
        )

    scatter = Scatter(copies, parts, far, near, row.at[1], row_far.at[1], row_near.at[1])
    gather.first()
    mlp_share(a)
    gather.middle()
    mlp_share(a + 1)
    mlp_share(a + 3)
    scatter.send_near()
    dec_sum.middle()
    gather.last()
    mlp_share(a + 2)
    scatter.send_far()
    dec_out = layer_norm(
        dec_first.astype(jnp.float32) + dec_sum.finish() + biases_ref[1:2],
        gains_ref[1:2],
        shifts_ref[1:2],
    ).astype(jnp.bfloat16)
    dec_out_ref[...] = dec_out
    scatter.pass_on()
    mlp_sum = scatter.finish()
    second = layer_norm(
        first.astype(jnp.float32) + mlp_sum + biases_ref[1:2], gains_ref[1:2], shifts_ref[1:2]
    ).astype(jnp.bfloat16)
    out_ref[...] = second
    keep = pltpu.make_async_copy(out_ref, rows.at[device(a, b)], local_sem.at[0])
    keep.start()
    gather = Gather(copies, lambda i, j: rows.at[device(i, j)], out_ref)
    gather.begin()
    gather.first()
    gather.middle()
    gather.last()
    keep.wait()
    copies.drain()


def next_kernel(rows_ref, own_ref, dec_ref, w_ref, next_ref, out_ref, dec_out_ref, dec_next_ref):
    block = rows_ref[...].reshape(SIDE * ROWS, rows_ref.shape[2])
    next_ref[...] = lax.dot_general(
        w_ref[...], block, NT, preferred_element_type=jnp.float32
    ).astype(next_ref.dtype)

    @pl.when(pl.program_id(0) == 0)
    def _():
        out_ref[...] = own_ref[...]
        dec_out_ref[...] = dec_ref[...]
        dec_next_ref[...] = lax.dot_general(
            dec_ref[...], w_ref[...], NT, preferred_element_type=jnp.float32
        ).astype(dec_next_ref.dtype)


def per_device(
    reps,
    x_pre,
    x_dec,
    prefix_kv,
    cache_kv,
    dec_len,
    offsets,
    segments,
    w_qkv,
    w_out,
    w_up,
    up_bias,
    w_down,
    biases,
    gains,
    shifts,
    w_next,
):
    heads = prefix_kv.shape[2]
    hd = prefix_kv.shape[3] // 2
    span = segments.shape[1]
    width = x_pre.shape[1]
    decodes = x_dec.shape[0]
    columns = w_qkv.shape[1]
    units = w_up.shape[1]
    scale = hd ** (-0.5)
    bf16, f32 = jnp.bfloat16, jnp.float32
    shape = jax.ShapeDtypeStruct
    whole = pl.BlockSpec(memory_space=VMEM)
    scalars = pl.BlockSpec(memory_space=pltpu.SMEM)
    anywhere = pl.BlockSpec(memory_space=pltpu.HBM)
    group = SIDE * SIDE

    cache_t = cache_kv.transpose(0, 2, 3, 1)
    planes = reps // 2
    n_copies = 16 + reps - 1 + (SIDE - 1) * planes
    qkv_t, dec_attn, w_row = pl.pallas_call(
        functools.partial(project_kernel, reps, scale),
        out_shape=(
            shape((columns, span), bf16),
            shape((decodes, heads * hd), bf16),
            shape((SIDE,) + w_out.shape, bf16),
        ),
        in_specs=[scalars, whole] + [anywhere] * 4,
        out_specs=(whole, whole, anywhere),
        scratch_shapes=[
            VMEM((group, ROWS, width), bf16),
            VMEM((128, width), bf16),
            VMEM((columns, width), bf16),
            VMEM(cache_t.shape, bf16),
            VMEM((reps, heads, hd + 16, 128), f32),
            pltpu.SemaphoreType.DMA((4,)),
            pltpu.SemaphoreType.DMA((n_copies,)),
            pltpu.SemaphoreType.DMA((n_copies,)),
        ],
        compiler_params=pltpu.CompilerParams(
            collective_id=0, has_side_effects=True, vmem_limit_bytes=62 << 20
        ),
        name="project",
    )(dec_len, x_dec, x_pre, w_qkv.T, cache_t, w_out)

    attn = pl.pallas_call(
        functools.partial(attend_kernel, scale),
        grid=(heads,),
        out_shape=shape((span, heads * hd), bf16),
        in_specs=[
            scalars,
            scalars,
            pl.BlockSpec((1, 3, hd, span), lambda h: (h, 0, 0, 0)),
            pl.BlockSpec((1, 2 * hd, prefix_kv.shape[1]), lambda h: (h, 0, 0)),
            pl.BlockSpec((1, span), lambda h: (0, 0)),
        ],
        out_specs=pl.BlockSpec((span, heads * hd), lambda h: (0, 0)),
        scratch_shapes=[
            VMEM((span, hd), bf16),
            *([VMEM((256, 1), f32), VMEM((256, 1), f32), VMEM((256, hd), f32)] * 2),
        ],
        compiler_params=pltpu.CompilerParams(
            dimension_semantics=("arbitrary",), vmem_limit_bytes=62 << 20
        ),
        name="attend",
    )(
        offsets,
        segments,
        qkv_t.reshape(heads, 3, hd, span),
        prefix_kv[0].transpose(1, 2, 0),
        segments,
    )

    n_copies = 2 * (16 + 6) + 12 + 12 + 6 + 6
    rows, own, dec_own = pl.pallas_call(
        tail_kernel,
        out_shape=(
            shape((group, ROWS, width), bf16),
            shape((ROWS, width), bf16),
            shape((decodes, width), bf16),
        ),
        in_specs=[whole] * 6 + [anywhere] * 5,
        out_specs=(anywhere, whole, whole),
        scratch_shapes=[
            VMEM((ROWS, width), bf16),
            VMEM((SIDE,) + w_out.shape, bf16),
            VMEM((width, units), bf16),
            VMEM((units, width), bf16),
            VMEM((SIDE, SIDE, ROWS, heads * hd), bf16),
            VMEM((SIDE, SIDE, ROWS, width), bf16),
            VMEM((SIDE, SIDE, ROWS, width), bf16),
            VMEM((2, 2, ROWS, width), bf16),
            VMEM((2, SIDE, ROWS, width), bf16),
            VMEM((2, SIDE, ROWS, width), bf16),
            VMEM((2, 2, ROWS // 2, width), bf16),
            VMEM((2, 2, ROWS, width), bf16),
            VMEM((2, SIDE, decodes, width), bf16),
            VMEM((2, SIDE, decodes, width), bf16),
            pltpu.SemaphoreType.DMA((8,)),
            pltpu.SemaphoreType.DMA((n_copies,)),
            pltpu.SemaphoreType.DMA((n_copies,)),
        ],
        compiler_params=pltpu.CompilerParams(
            collective_id=1, has_side_effects=True, vmem_limit_bytes=60 << 20
        ),
        name="tail",
    )(
        dec_attn,
        x_dec,
        up_bias,
        biases,
        gains,
        shifts,
        attn,
        x_pre,
        w_row,
        w_up,
        w_down,
    )

    next_t, layer_out, dec_out, dec_next = pl.pallas_call(
        next_kernel,
        grid=(SIDE,),
        out_shape=(
            shape((columns, span), bf16),
            shape((ROWS, width), bf16),
            shape((decodes, width), bf16),
            shape((decodes, columns), bf16),
        ),
        in_specs=[
            pl.BlockSpec((SIDE, ROWS, width), lambda i: (i, 0, 0)),
            pl.BlockSpec((ROWS, width), lambda i: (0, 0)),
            pl.BlockSpec((decodes, width), lambda i: (0, 0)),
            pl.BlockSpec((columns, width), lambda i: (0, 0)),
        ],
        out_specs=(
            pl.BlockSpec((columns, SIDE * ROWS), lambda i: (0, i)),
            pl.BlockSpec((ROWS, width), lambda i: (0, 0)),
            pl.BlockSpec((decodes, width), lambda i: (0, 0)),
            pl.BlockSpec((decodes, columns), lambda i: (0, 0)),
        ),
        compiler_params=pltpu.CompilerParams(
            dimension_semantics=("arbitrary",), vmem_limit_bytes=62 << 20
        ),
        name="next",
    )(rows, own, dec_own, w_next.T)
    return layer_out, next_t.T, dec_out, dec_next


def solution(mesh):
    placed = (
        P(("rep", "tensor"), None),
        P(),
        P("rep", None, "tensor", None),
        P(None, "rep", "tensor", None),
        P(),
        P("rep"),
        P("rep", None),
        P(None, "tensor"),
        P("tensor", None),
        P(None, "tensor"),
        P("tensor"),
        P("tensor", None),
        P(),
        P(),
        P(),
        P(None, "tensor"),
    )
    return jax.shard_map(
        functools.partial(per_device, mesh.shape["rep"]),
        mesh=mesh,
        in_specs=placed,
        out_specs=(P(("rep", "tensor"), None), P("rep", "tensor"), P(), P(None, "tensor")),
        check_vma=False,
    )
```

```python
import functools

import jax
import jax.numpy as jnp
from jax import lax
from jax.experimental import pallas as pl
from jax.experimental.pallas import tpu as pltpu
from jax.sharding import PartitionSpec as P

MESH = pl.DeviceIdType.MESH
NEG = -1e30
LOG2E = 1.4426950408889634
SIDE = 4
ROWS = 64
VMEM = pltpu.VMEM
NT = (((1,), (1,)), ((), ()))


def place():
    t = lax.axis_index("tensor")
    core = lax.rem(lax.axis_index("rep"), 2)
    y, x = lax.div(t, SIDE), lax.rem(t, SIDE)
    major = y * (1 - core) + x * core
    minor = x * (1 - core) + y * core
    step_major, step_minor = SIDE - (SIDE - 1) * core, 1 + (SIDE - 1) * core

    def device(i, j):
        return lax.rem(i, SIDE) * step_major + lax.rem(j, SIDE) * step_minor

    return y, x, major, minor, device


class Copies:
    def __init__(self, send, recv):
        self.send, self.recv, self.used, self.all = send, recv, 0, []

    def start(self, src, dst, where):
        copy = pltpu.make_async_remote_copy(
            src_ref=src,
            dst_ref=dst,
            send_sem=self.send.at[self.used],
            recv_sem=self.recv.at[self.used],
            device_id=where,
            device_id_type=MESH,
        )
        copy.start()
        self.used += 1
        self.all.append(copy)
        return copy

    def drain(self):
        for copy in self.all:
            copy.wait_send()


def tensor(t):
    return {"tensor": t}


def greet(tensor_peers, rep_peers=()):
    barrier = pltpu.get_barrier_semaphore()
    for t in tensor_peers:
        pl.semaphore_signal(barrier, inc=1, device_id=tensor(t), device_id_type=MESH)
    for r in rep_peers:
        pl.semaphore_signal(barrier, inc=1, device_id={"rep": r}, device_id_type=MESH)
    pl.semaphore_wait(barrier, len(tensor_peers) + len(rep_peers))


class Gather:
    def __init__(self, copies, at, own=None):
        y, x, self.a, self.b, self.device = place()
        self.copies, self.at, self.own = copies, at, own

    def go(self, i, j, ti, tj):
        return self.copies.start(self.at(i, j), self.at(i, j), tensor(self.device(ti, tj)))

    def begin(self):
        a, b = self.a, self.b
        own = self.at(a, b) if self.own is None else self.own
        self.right, self.left, up, down = (
            self.copies.start(own, self.at(a, b), tensor(self.device(i, j)))
            for i, j in ((a, b + 1), (a, b + 3), (a + 1, b), (a + 3, b))
        )
        self.up, self.down = [up], [down]

    def spread(self, j):
        a, b = self.a, self.b
        self.up.append(self.go(a, j, a + 1, b))
        self.down.append(self.go(a, j, a + 3, b))

    def half(self, i, j, part):
        return self.at(i, j).at[pl.ds(part * (ROWS // 2), ROWS // 2)]

    def first(self):
        a, b = self.a, self.b
        self.right.wait_recv()
        one = self.half(a, b + 3, 0)
        far_one = self.copies.start(one, one, tensor(self.device(a, b + 1)))
        self.spread(b + 3)
        self.left.wait_recv()
        two = self.half(a, b + 1, 1)
        far_two = self.copies.start(two, two, tensor(self.device(a, b + 3)))
        self.spread(b + 1)
        far_one.wait_recv()
        far_two.wait_recv()
        self.spread(b + 2)

    def middle(self):
        a, b = self.a, self.b
        self.up[0].wait_recv()
        self.far = [self.go(a + 3, b, a + 1, b)]
        self.down[1].wait_recv()
        self.far.append(self.go(a + 1, b + 3, a + 3, b))
        self.down[2].wait_recv()
        self.far.append(self.go(a + 1, b + 1, a + 3, b))
        self.up[3].wait_recv()
        self.far.append(self.go(a + 3, b + 2, a + 1, b))
        self.up[1].wait_recv()
        self.up[2].wait_recv()
        self.down[0].wait_recv()
        self.down[3].wait_recv()

    def last(self):
        for copy in self.far:
            copy.wait_recv()


class RingSum:
    def __init__(self, copies, row, far, near, index, to):
        self.copies, self.slabs, self.far, self.near = copies, row, far, near
        self.c, self.next, self.prev = index, to(index + 1), to(index + 3)
        half = ROWS // 2
        self.top, self.low = pl.ds(0, half), pl.ds(half, half)

    def row(self, k):
        return self.slabs.at[lax.rem(self.c + k, SIDE)]

    def send_far(self):
        self.next_far = self.copies.start(self.row(2).at[self.top], self.far.at[0], self.next)
        self.prev_far = self.copies.start(self.row(2).at[self.low], self.far.at[1], self.prev)

    def send_next(self):
        self.next_near = self.copies.start(
            self.row(1).at[self.low], self.near.at[0, self.low], self.next
        )

    def send_prev(self):
        self.prev_near = self.copies.start(
            self.row(3).at[self.top], self.near.at[1, self.top], self.prev
        )

    def pass_on(self):
        self.next_far.wait_recv()
        add_into(self.row(1).at[self.top], self.far[0])
        self.next_sum = self.copies.start(
            self.row(1).at[self.top], self.near.at[0, self.top], self.next
        )
        self.prev_far.wait_recv()
        add_into(self.row(3).at[self.low], self.far[1])
        self.prev_sum = self.copies.start(
            self.row(3).at[self.low], self.near.at[1, self.low], self.prev
        )

    def finish(self, own):
        for copy in (self.next_near, self.prev_near, self.next_sum, self.prev_sum):
            copy.wait_recv()
        return own + self.near[0].astype(jnp.float32) + self.near[1].astype(jnp.float32)


class RingGather:
    def __init__(self, copies, slabs, index, to):
        self.copies, self.slabs, self.c = copies, slabs, index
        self.next, self.prev = to(index + 1), to(index + 3)
        half = ROWS // 2
        self.top, self.low = pl.ds(0, half), pl.ds(half, half)

    def go(self, k, part, where):
        piece = self.slabs.at[lax.rem(self.c + k, SIDE)].at[part]
        return self.copies.start(piece, piece, where)

    def run(self):
        first = (self.go(0, self.top, self.next), self.go(0, self.low, self.prev))
        second = (self.go(0, self.low, self.next), self.go(0, self.top, self.prev))
        first[0].wait_recv()
        far = [self.go(3, self.top, self.next)]
        first[1].wait_recv()
        far.append(self.go(1, self.low, self.prev))
        for copy in (*second, *far):
            copy.wait_recv()


def add_into(ref, value):
    ref[...] = (ref[...].astype(jnp.float32) + value.astype(jnp.float32)).astype(ref.dtype)


class Scatter:
    def __init__(self, copies, parts, far, near, row, row_far, row_near):
        y, x, a, b, self.device = place()
        self.a, self.b = a, b
        self.copies, self.parts, self.far, self.near = copies, parts, far, near
        self.ring = RingSum(
            copies, row, row_far, row_near, b, lambda j: tensor(self.device(a, j))
        )
        self.above, self.below = tensor(self.device(a + 1, b)), tensor(self.device(a + 3, b))
        self.ups, self.downs = (b + 2, b + 1), (b + 3, b)

    def part(self, i, j):
        return self.parts.at[lax.rem(i, SIDE), lax.rem(j, SIDE)]

    def landing(self, side, j):
        return self.near.at[side, lax.rem(j, SIDE)]

    def send_far(self):
        self.far_up, self.far_down = [], []
        for k in range(2):
            self.far_up.append(
                self.copies.start(self.part(self.a + 2, self.ups[k]), self.far.at[0, k], self.above)
            )
            self.far_down.append(
                self.copies.start(
                    self.part(self.a + 2, self.downs[k]), self.far.at[1, k], self.below
                )
            )

    def send_near(self):
        self.near_up, self.near_down = [], []
        for k in range(2):
            self.near_up.append(
                self.copies.start(
                    self.part(self.a + 1, self.downs[k]),
                    self.landing(0, self.downs[k]),
                    self.above,
                )
            )
            self.near_down.append(
                self.copies.start(
                    self.part(self.a + 3, self.ups[k]), self.landing(1, self.ups[k]), self.below
                )
            )

    def pass_on(self):
        self.sum_up, self.sum_down = [], []
        for k in range(2):
            self.far_up[k].wait_recv()
            add_into(self.part(self.a + 1, self.ups[k]), self.far[0, k])
            self.sum_up.append(
                self.copies.start(
                    self.part(self.a + 1, self.ups[k]), self.landing(0, self.ups[k]), self.above
                )
            )
            self.far_down[k].wait_recv()
            add_into(self.part(self.a + 3, self.downs[k]), self.far[1, k])
            self.sum_down.append(
                self.copies.start(
                    self.part(self.a + 3, self.downs[k]),
                    self.landing(1, self.downs[k]),
                    self.below,
                )
            )

    def total(self, j):
        at = lax.rem(j, SIDE)
        return (
            self.parts[self.a, at].astype(jnp.float32)
            + self.near[0, at].astype(jnp.float32)
            + self.near[1, at].astype(jnp.float32)
        )

    def finish(self):
        ring, b = self.ring, self.b
        self.sum_up[0].wait_recv()
        self.near_down[0].wait_recv()
        ring.row(2)[...] = self.total(b + 2).astype(jnp.bfloat16)
        ring.send_far()
        self.near_up[0].wait_recv()
        self.sum_down[0].wait_recv()
        ring.row(3)[...] = self.total(b + 3).astype(jnp.bfloat16)
        ring.send_prev()
        self.sum_up[1].wait_recv()
        self.near_down[1].wait_recv()
        ring.row(1)[...] = self.total(b + 1).astype(jnp.bfloat16)
        ring.send_next()
        ring.pass_on()
        self.near_up[1].wait_recv()
        self.sum_down[1].wait_recv()
        return ring.finish(self.total(b))


class SmallSum:
    def __init__(self, copies, over_x, over_y):
        t = lax.axis_index("tensor")
        self.y, self.x = lax.div(t, SIDE), lax.rem(t, SIDE)
        self.copies, self.over_x, self.over_y = copies, over_x, over_y

    def begin(self, value):
        self.over_x[self.x] = value.astype(jnp.bfloat16)
        mine = self.over_x.at[self.x]
        self.sent = [
            self.copies.start(
                mine, mine, tensor(SIDE * self.y + lax.rem(self.x + k, SIDE))
            )
            for k in (1, 2, 3)
        ]

    def middle(self):
        for copy in self.sent:
            copy.wait_recv()
        self.over_y[self.y] = sum(
            self.over_x[k].astype(jnp.float32) for k in range(SIDE)
        ).astype(jnp.bfloat16)
        mine = self.over_y.at[self.y]
        self.sent = [
            self.copies.start(
                mine, mine, tensor(SIDE * lax.rem(self.y + k, SIDE) + self.x)
            )
            for k in (1, 2, 3)
        ]

    def finish(self):
        for copy in self.sent:
            copy.wait_recv()
        return sum(self.over_y[k].astype(jnp.float32) for k in range(SIDE))


def layer_norm(values, gain_row, shift_row):
    average = jnp.mean(values, axis=-1, keepdims=True)
    centred = values - average
    spread = jnp.mean(centred * centred, axis=-1, keepdims=True)
    return centred * lax.rsqrt(spread + 1e-05) * gain_row + shift_row


def project_kernel(
    reps,
    scale,
    len_ref,
    dec_ref,
    x_hbm,
    w_hbm,
    cache_hbm,
    w_out_hbm,
    out_ref,
    attn_ref,
    w_row_hbm,
    rows,
    dec_rows,
    w_ref,
    cache_ref,
    states,
    local_sem,
    send_sem,
    recv_sem,
):
    y, x, a, b, device = place()
    load_x = pltpu.make_async_copy(x_hbm, rows.at[device(a, b)], local_sem.at[2])
    load_x.start()
    load_w = pltpu.make_async_copy(w_hbm, w_ref, local_sem.at[0])
    load_w.start()
    load_cache = pltpu.make_async_copy(cache_hbm, cache_ref, local_sem.at[1])
    load_cache.start()
    keep_w = pltpu.make_async_copy(w_out_hbm, w_row_hbm.at[b], local_sem.at[3])
    keep_w.start()
    rep = lax.axis_index("rep")
    copies = Copies(send_sem, recv_sem)
    greet(
        [device(a, b + k) for k in (1, 2, 3)] + [device(a + 1, b), device(a + 3, b)],
        [lax.rem(rep + k, reps) for k in range(1, reps)],
    )
    gather = Gather(copies, lambda i, j: rows.at[device(i, j)])
    planes = reps // 2
    quarter = w_out_hbm.shape[1] // planes
    mine = pl.ds(pl.multiple_of(lax.div(rep, 2) * quarter, 128), quarter)
    shards = [
        copies.start(
            w_out_hbm.at[:, mine], w_row_hbm.at[b, :, mine], tensor(device(a, b + k))
        )
        for k in (1, 3, 2)
    ]
    dec_rows[...] = jnp.zeros_like(dec_rows)
    dec_rows[: dec_ref.shape[0]] = dec_ref[...]
    load_x.wait()
    spread = []
    for k, shard in zip((1, 3, 2), shards):
        shard.wait_recv()
        piece = w_row_hbm.at[lax.rem(b - k + SIDE, SIDE), :, mine]
        spread += [
            copies.start(piece, piece, {"rep": lax.rem(rep + 2 * p, reps)})
            for p in range(1, planes)
        ]
    gather.begin()
    load_w.wait()
    dec = (
        lax.dot_general(w_ref[...], dec_rows[...], NT, preferred_element_type=jnp.float32)
        .astype(jnp.bfloat16)
        .astype(jnp.float32)
    )
    gather.first()
    load_cache.wait()
    hd = cache_ref.shape[2] // 2
    heads = cache_ref.shape[1]
    span = cache_ref.shape[3]
    lanes = dec.shape[1]
    lane = lax.broadcasted_iota(jnp.int32, (1, lanes), 1)
    position = rep * span + lax.broadcasted_iota(jnp.int32, (1, span), 1)

    def request(r, state):
        pick = lane == r
        column = jnp.sum(jnp.where(pick, dec, 0.0), axis=1, keepdims=True)
        valid = position < len_ref[r]
        out = []
        for h in range(heads):
            query = column[3 * hd * h : 3 * hd * h + hd]
            key = cache_ref[r, h, :hd].astype(jnp.float32)
            value = cache_ref[r, h, hd:].astype(jnp.float32)
            score = jnp.sum(key * query, axis=0, keepdims=True) * scale
            score = jnp.where(valid, score, NEG)
            high = jnp.max(score, axis=1, keepdims=True)
            weight = jnp.where(valid, jnp.exp(score - high), 0.0)
            total = jnp.sum(weight, axis=1, keepdims=True)
            mixed = jnp.sum(value * weight, axis=1, keepdims=True)
            highs, totals, mixes = state[h]
            out.append(
                (
                    jnp.where(pick, high, highs),
                    jnp.where(pick, total, totals),
                    jnp.where(pick, mixed, mixes),
                )
            )
        return tuple(out)

    empty = tuple(
        (
            jnp.full((1, lanes), NEG, jnp.float32),
            jnp.zeros((1, lanes), jnp.float32),
            jnp.zeros((hd, lanes), jnp.float32),
        )
        for _ in range(heads)
    )
    state = lax.fori_loop(0, cache_ref.shape[0], request, empty)
    for h in range(heads):
        states[rep, h, :hd] = state[h][2]
        states[rep, h, hd : hd + 8] = jnp.broadcast_to(state[h][0], (8, lanes))
        states[rep, h, hd + 8 : hd + 16] = jnp.broadcast_to(state[h][1], (8, lanes))
    sent = [
        copies.start(states.at[rep], states.at[rep], {"rep": lax.rem(rep + k, reps)})
        for k in range(1, reps)
    ]
    gather.middle()
    for copy in sent:
        copy.wait_recv()
    for h in range(heads):
        base = 3 * hd * h
        query, key, value = (dec[base + hd * k : base + hd * (k + 1)] for k in range(3))
        own = jnp.sum(query * key, axis=0, keepdims=True) * scale
        highest = own
        for k in range(reps):
            highest = jnp.maximum(highest, states[k, h, hd : hd + 1])
        own_weight = jnp.exp(own - highest)
        total, mixed = own_weight, own_weight * value
        for k in range(reps):
            factor = jnp.exp(states[k, h, hd : hd + 1] - highest)
            total = total + factor * states[k, h, hd + 8 : hd + 9]
            mixed = mixed + factor * states[k, h, :hd]
        attn_ref[:, hd * h : hd * (h + 1)] = (mixed / total).T[: attn_ref.shape[0]].astype(
            attn_ref.dtype
        )
    gather.last()

    @pl.loop(0, SIDE)
    def _(i):
        block = rows[pl.ds(SIDE * i, SIDE)].reshape(SIDE * ROWS, rows.shape[2])
        out_ref[:, pl.ds(pl.multiple_of(i * SIDE * ROWS, SIDE * ROWS), SIDE * ROWS)] = (
            lax.dot_general(w_ref[...], block, NT, preferred_element_type=jnp.float32).astype(
                out_ref.dtype
            )
        )

    for copy in spread:
        copy.wait_recv()
    keep_w.wait()
    copies.drain()


def attend(head, scale, offset, qkv_ref, kv_ref, seg_row, out_ref, q_ref, state):
    hd = q_ref.shape[1]
    span = seg_row.shape[1]
    block, key_block = 256, 1024
    early = span // 2 // block
    factor = scale * LOG2E
    q_ref[...] = qkv_ref[head, 0].astype(jnp.float32).T.astype(jnp.bfloat16)
    seg_keys = seg_row[...].astype(jnp.float32)
    seg_rows = jnp.broadcast_to(seg_keys, (8, span)).T[:, :1]
    states = [state[3 * i : 3 * i + 3] for i in range(early)]

    def rows(i):
        return slice(i * block, (i + 1) * block)

    def mix(weight, values):
        return lax.dot_general(
            weight.astype(jnp.bfloat16), values, NT, preferred_element_type=jnp.float32
        )

    for m_ref, l_ref, acc_ref in states:
        m_ref[...] = jnp.full(m_ref.shape, NEG, jnp.float32)
        l_ref[...] = jnp.zeros(l_ref.shape, jnp.float32)
        acc_ref[...] = jnp.zeros(acc_ref.shape, jnp.float32)

    @pl.loop(0, kv_ref.shape[2] // key_block)
    def _(j):
        at = pl.multiple_of(j * key_block, key_block)
        keys = kv_ref[head, :hd, pl.ds(at, key_block)]
        values = kv_ref[head, hd:, pl.ds(at, key_block)]
        seen = at + lax.broadcasted_iota(jnp.int32, (1, key_block), 1) < offset
        scores = [
            jnp.dot(q_ref[rows(i)], keys, preferred_element_type=jnp.float32)
            for i in range(early)
        ]
        for score, (m_ref, l_ref, acc_ref) in zip(scores, states):
            score = jnp.where(seen, score, NEG)
            high = jnp.maximum(m_ref[...], jnp.max(score, axis=1, keepdims=True))
            decay = jnp.exp2((m_ref[...] - high) * factor)
            weight = jnp.exp2((score - high) * factor)
            m_ref[...] = high
            l_ref[...] = l_ref[...] * decay + jnp.sum(weight, axis=1, keepdims=True)
            acc_ref[...] = acc_ref[...] * decay + mix(weight, values)

    for i in range(span // block):
        low = max(0, (i - early) * block)
        high = (i + 1) * block
        seg_q = seg_rows[rows(i)]
        score = jnp.dot(
            q_ref[rows(i)], qkv_ref[head, 1, :, low:high], preferred_element_type=jnp.float32
        )
        shape = (block, high - low)
        query_at = i * block + lax.broadcasted_iota(jnp.int32, shape, 0)
        key_at = low + lax.broadcasted_iota(jnp.int32, shape, 1)
        seen = (seg_keys[:, low:high] == seg_q) & (key_at <= query_at)
        score = jnp.where(seen, score, NEG)
        values = qkv_ref[head, 2, :, low:high]
        peak = jnp.max(score, axis=1, keepdims=True)
        if i < early:
            m_ref, l_ref, acc_ref = states[i]
            keep = (seg_q == 0) & (offset > 0)
            before = jnp.where(keep, m_ref[...], NEG)
            peak = jnp.maximum(peak, before)
            decay = jnp.where(keep, jnp.exp2((before - peak) * factor), 0.0)
        weight = jnp.exp2((score - peak) * factor)
        total = jnp.sum(weight, axis=1, keepdims=True)
        mixed = mix(weight, values)
        if i < early:
            total = total + l_ref[...] * decay
            mixed = mixed + acc_ref[...] * decay
        out_ref[rows(i), head * hd : (head + 1) * hd] = (mixed / total).astype(out_ref.dtype)


def tail_kernel(
    scale,
    reps,
    offset_ref,
    seg_row,
    dec_attn_ref,
    x_dec_ref,
    up_bias_ref,
    biases_ref,
    gains_ref,
    shifts_ref,
    qkv_hbm,
    kv_hbm,
    x_hbm,
    w_row_hbm,
    w_up_hbm,
    w_down_hbm,
    w_next_hbm,
    result_hbm,
    out_ref,
    dec_out_ref,
    dec_next_ref,
    qkv_ref,
    kv_ref,
    x_ref,
    w_row_ref,
    w_up_ref,
    w_down_ref,
    w_next_ref,
    attn_ref,
    heads_ref,
    columns_ref,
    result_ref,
    slabs,
    parts,
    far,
    near,
    row,
    row_far,
    row_near,
    over_x,
    over_y,
    q_ref,
    m0_ref,
    l0_ref,
    acc0_ref,
    m1_ref,
    l1_ref,
    acc1_ref,
    local_sem,
    send_sem,
    recv_sem,
):
    y, x, a, b, device = place()
    loads = []
    for k, (source, target) in enumerate(
        (
            (qkv_hbm, qkv_ref),
            (kv_hbm, kv_ref),
            (w_row_hbm, w_row_ref),
            (x_hbm, x_ref),
            (w_next_hbm, w_next_ref.at[b]),
            (w_up_hbm, w_up_ref),
            (w_down_hbm, w_down_ref),
        )
    ):
        loads.append(pltpu.make_async_copy(source, target, local_sem.at[k]))
        loads[-1].start()
    load_qkv, load_kv, load_row, load_x, load_next, load_up, load_down = loads
    copies = Copies(send_sem, recv_sem)
    rep = lax.axis_index("rep")
    plane, planes = lax.div(rep, 2), reps // 2
    columns, width = w_next_hbm.shape

    def level(k):
        return {"rep": lax.rem(rep + 2 * k, reps)}

    def quarter(p):
        size = width // planes
        return pl.ds(pl.multiple_of(lax.rem(p, planes) * size, 128), size)

    greet(
        [SIDE * y + lax.rem(x + k, SIDE) for k in (1, 2, 3)]
        + [SIDE * lax.rem(y + k, SIDE) + x for k in (1, 2, 3)],
        [lax.rem(rep + 2 * k, reps) for k in (1, planes - 1)],
    )
    mine = quarter(plane)
    shards = [
        copies.start(
            w_next_hbm.at[:, mine], w_next_ref.at[b, :, mine], tensor(device(a, b + k))
        )
        for k in (3, 2, 1)
    ]
    attn_ref[...] = jnp.zeros_like(attn_ref)
    result_ref[...] = jnp.zeros_like(result_ref)
    chunk = (SIDE, ROWS, width)
    load_row.wait()
    dec_sum = SmallSum(copies, over_x.at[0], over_y.at[0])
    dec_sum.begin(
        jnp.dot(dec_attn_ref[...], w_row_ref[b], preferred_element_type=jnp.float32)
    )
    load_qkv.wait()
    load_kv.wait()
    state = (m0_ref, l0_ref, acc0_ref, m1_ref, l1_ref, acc1_ref)
    offset = offset_ref[0]
    heads = qkv_ref.shape[0]
    for head in range(heads):
        attend(head, scale, offset, qkv_ref, kv_ref, seg_row, attn_ref, q_ref, state)
        if head == 0:
            dec_sum.middle()

    def tokens(i, j):
        return attn_ref.at[pl.ds(pl.multiple_of(device(i, j) * ROWS, ROWS), ROWS)]

    swaps = [
        copies.start(tokens(i, b + k), heads_ref.at[b, i], tensor(device(a, b + k)))
        for k in (2, 1, 3)
        for i in range(SIDE)
    ]
    for i in range(SIDE):
        heads_ref[b, i] = tokens(i, b)[...]
    spread = []
    for k, shard in enumerate(shards):
        shard.wait_recv()
        piece = w_next_ref.at[lax.rem(b + 1 + k, SIDE), :, mine]
        spread += [copies.start(piece, piece, level(p)) for p in (1, planes - 1)]
    dec_first = layer_norm(
        x_dec_ref[...].astype(jnp.float32) + dec_sum.finish() + biases_ref[0:1],
        gains_ref[0:1],
        shifts_ref[0:1],
    ).astype(jnp.bfloat16)
    for swap in swaps:
        swap.wait_recv()
    ring = RingSum(
        copies, row.at[0], row_far.at[0], row_near.at[0], a, lambda i: tensor(device(i, b))
    )
    depth = w_row_ref.shape[1]
    step = width // 5
    for n in range(0, width, step):
        total = sum(
            jnp.dot(
                heads_ref[j].reshape(SIDE * ROWS, heads_ref.shape[3])[:, :depth],
                w_row_ref[j, :, n : n + step],
                preferred_element_type=jnp.float32,
            )
            for j in range(SIDE)
        )
        row[0, :, :, n : n + step] = total.astype(jnp.bfloat16).reshape(SIDE, ROWS, step)
    ring.send_far()
    ring.send_next()
    ring.send_prev()
    ring.pass_on()
    own = row[0, a].astype(jnp.float32)
    load_x.wait()
    attn_sum = ring.finish(own)
    first = layer_norm(
        x_ref[...].astype(jnp.float32) + attn_sum + biases_ref[0:1], gains_ref[0:1], shifts_ref[0:1]
    ).astype(jnp.bfloat16)

    def slab(i, j):
        return slabs.at[lax.rem(i, SIDE), lax.rem(j, SIDE)]

    slab(a, b)[...] = first
    gather = Gather(copies, slab)
    gather.begin()
    load_up.wait()
    load_down.wait()

    def mlp(value):
        inner = jnp.dot(value, w_up_ref[...], preferred_element_type=jnp.float32)
        inner = inner + up_bias_ref[...][None, :]
        hidden = (0.5 * inner * (1.0 + lax.erf(inner * 0.7071067811865476))).astype(jnp.bfloat16)
        return jnp.dot(hidden, w_down_ref[...], preferred_element_type=jnp.float32)

    dec_sum = SmallSum(copies, over_x.at[1], over_y.at[1])
    dec_sum.begin(mlp(dec_first))

    def mlp_share(i):
        at = lax.rem(i, SIDE)
        parts[at] = (
            mlp(slabs[at].reshape(SIDE * ROWS, width)).astype(jnp.bfloat16).reshape(chunk)
        )

    scatter = Scatter(copies, parts, far, near, row.at[1], row_far.at[1], row_near.at[1])
    gather.first()
    mlp_share(a)
    gather.middle()
    mlp_share(a + 1)
    mlp_share(a + 3)
    scatter.send_near()
    dec_sum.middle()
    gather.last()
    mlp_share(a + 2)
    scatter.send_far()
    passed = []
    for at, copy in enumerate(spread):
        copy.wait_recv()
        j = lax.rem(b + 1 + at // 2, SIDE)
        go_on, from_plane, part = ((1, planes - 1, 0), (planes - 1, 1, 1))[at % 2]
        piece = w_next_ref.at[
            j, pl.ds(part * (columns // 2), columns // 2), quarter(plane + from_plane)
        ]
        passed.append(copies.start(piece, piece, level(go_on)))
    dec_out = layer_norm(
        dec_first.astype(jnp.float32) + dec_sum.finish() + biases_ref[1:2],
        gains_ref[1:2],
        shifts_ref[1:2],
    ).astype(jnp.bfloat16)
    dec_out_ref[...] = dec_out
    load_next.wait()
    dec_next_ref[...] = lax.dot_general(
        dec_out, w_next_ref[b], NT, preferred_element_type=jnp.float32
    ).astype(jnp.bfloat16)
    scatter.pass_on()
    mlp_sum = scatter.finish()
    second = layer_norm(
        first.astype(jnp.float32) + mlp_sum + biases_ref[1:2], gains_ref[1:2], shifts_ref[1:2]
    ).astype(jnp.bfloat16)
    out_ref[...] = second
    columns_ref[a] = second
    RingGather(copies, columns_ref, a, lambda i: tensor(device(i, b))).run()
    for copy in passed:
        copy.wait_recv()
    keeps = []
    for k in (2, 1, 3, 0):
        j = lax.rem(b + k, SIDE)
        result_ref[j, :, :, :columns] = (
            lax.dot_general(
                columns_ref[...].reshape(SIDE * ROWS, width),
                w_next_ref[j],
                NT,
                preferred_element_type=jnp.float32,
            )
            .astype(jnp.bfloat16)
            .reshape(SIDE, ROWS, columns)
        )
        for i in range(SIDE):
            source, target = result_ref.at[j, i], result_hbm.at[device(i, b)]
            if k:
                keeps.append(copies.start(source, target, tensor(device(a, j))))
            else:
                local = pltpu.make_async_copy(source, target, local_sem.at[i])
                local.start()
                loads.append(local)
    for copy in keeps:
        copy.wait_recv()
    for local in loads[-SIDE:]:
        local.wait()
    copies.drain()


def layout_kernel(
    result_ref, own_ref, dec_ref, dec_result_ref, next_ref, out_ref, dec_out_ref, dec_next_ref
):
    columns, lanes = next_ref.shape[0], result_ref.shape[2]
    same = lax.broadcasted_iota(jnp.int32, (columns, lanes), 0) == lax.broadcasted_iota(
        jnp.int32, (columns, lanes), 1
    )
    next_ref[...] = lax.dot_general(
        same.astype(jnp.float32).astype(jnp.bfloat16),
        result_ref[...].reshape(SIDE * ROWS, lanes),
        NT,
        preferred_element_type=jnp.float32,
    ).astype(next_ref.dtype)

    @pl.when(pl.program_id(0) == 0)
    def _():
        out_ref[...] = own_ref[...]
        dec_out_ref[...] = dec_ref[...]
        dec_next_ref[...] = dec_result_ref[...]


def per_device(
    reps,
    x_pre,
    x_dec,
    prefix_kv,
    cache_kv,
    dec_len,
    offsets,
    segments,
    w_qkv,
    w_out,
    w_up,
    up_bias,
    w_down,
    biases,
    gains,
    shifts,
    w_next,
):
    heads = prefix_kv.shape[2]
    hd = prefix_kv.shape[3] // 2
    span = segments.shape[1]
    width = x_pre.shape[1]
    decodes = x_dec.shape[0]
    columns = w_qkv.shape[1]
    units = w_up.shape[1]
    scale = hd ** (-0.5)
    bf16, f32 = jnp.bfloat16, jnp.float32
    shape = jax.ShapeDtypeStruct
    whole = pl.BlockSpec(memory_space=VMEM)
    scalars = pl.BlockSpec(memory_space=pltpu.SMEM)
    anywhere = pl.BlockSpec(memory_space=pltpu.HBM)
    group = SIDE * SIDE

    cache_t = cache_kv.transpose(0, 2, 3, 1)
    planes = reps // 2
    n_copies = 16 + reps - 1 + (SIDE - 1) * planes
    qkv_t, dec_attn, w_row = pl.pallas_call(
        functools.partial(project_kernel, reps, scale),
        out_shape=(
            shape((columns, span), bf16),
            shape((decodes, heads * hd), bf16),
            shape((SIDE,) + w_out.shape, bf16),
        ),
        in_specs=[scalars, whole] + [anywhere] * 4,
        out_specs=(whole, whole, anywhere),
        scratch_shapes=[
            VMEM((group, ROWS, width), bf16),
            VMEM((128, width), bf16),
            VMEM((columns, width), bf16),
            VMEM(cache_t.shape, bf16),
            VMEM((reps, heads, hd + 16, 128), f32),
            pltpu.SemaphoreType.DMA((4,)),
            pltpu.SemaphoreType.DMA((n_copies,)),
            pltpu.SemaphoreType.DMA((n_copies,)),
        ],
        compiler_params=pltpu.CompilerParams(
            collective_id=0, has_side_effects=True, vmem_limit_bytes=62 << 20
        ),
        name="project",
    )(dec_len, x_dec, x_pre, w_qkv.T, cache_t, w_out)

    n_copies = 100
    lanes = 512
    result, own, dec_own, dec_result = pl.pallas_call(
        functools.partial(tail_kernel, scale, reps),
        out_shape=(
            shape((group, ROWS, lanes), bf16),
            shape((ROWS, width), bf16),
            shape((decodes, width), bf16),
            shape((decodes, columns), bf16),
        ),
        in_specs=[scalars] + [whole] * 7 + [anywhere] * 7,
        out_specs=(anywhere, whole, whole, whole),
        scratch_shapes=[
            VMEM((heads, 3, hd, span), bf16),
            VMEM((heads, 2 * hd, prefix_kv.shape[1]), bf16),
            VMEM((ROWS, width), bf16),
            VMEM((SIDE,) + w_out.shape, bf16),
            VMEM((width, units), bf16),
            VMEM((units, width), bf16),
            VMEM((SIDE, columns, width), bf16),
            VMEM((span, 256), bf16),
            VMEM((SIDE, SIDE, ROWS, 256), bf16),
            VMEM((SIDE, ROWS, width), bf16),
            VMEM((SIDE, SIDE, ROWS, lanes), bf16),
            VMEM((SIDE, SIDE, ROWS, width), bf16),
            VMEM((SIDE, SIDE, ROWS, width), bf16),
            VMEM((2, 2, ROWS, width), bf16),
            VMEM((2, SIDE, ROWS, width), bf16),
            VMEM((2, SIDE, ROWS, width), bf16),
            VMEM((2, 2, ROWS // 2, width), bf16),
            VMEM((2, 2, ROWS, width), bf16),
            VMEM((2, SIDE, decodes, width), bf16),
            VMEM((2, SIDE, decodes, width), bf16),
            VMEM((span, hd), bf16),
            *([VMEM((256, 1), f32), VMEM((256, 1), f32), VMEM((256, hd), f32)] * 2),
            pltpu.SemaphoreType.DMA((8,)),
            pltpu.SemaphoreType.DMA((n_copies,)),
            pltpu.SemaphoreType.DMA((n_copies,)),
        ],
        compiler_params=pltpu.CompilerParams(
            collective_id=1, has_side_effects=True, vmem_limit_bytes=62 << 20
        ),
        name="tail",
    )(
        offsets,
        segments,
        dec_attn,
        x_dec,
        up_bias,
        biases,
        gains,
        shifts,
        qkv_t.reshape(heads, 3, hd, span),
        prefix_kv[0].transpose(1, 2, 0),
        x_pre,
        w_row,
        w_up,
        w_down,
        w_next.T,
    )

    next_t, layer_out, dec_out, dec_next = pl.pallas_call(
        layout_kernel,
        grid=(SIDE,),
        out_shape=(
            shape((columns, span), bf16),
            shape((ROWS, width), bf16),
            shape((decodes, width), bf16),
            shape((decodes, columns), bf16),
        ),
        in_specs=[
            pl.BlockSpec((SIDE, ROWS, lanes), lambda i: (i, 0, 0)),
            pl.BlockSpec((ROWS, width), lambda i: (0, 0)),
            pl.BlockSpec((decodes, width), lambda i: (0, 0)),
            pl.BlockSpec((decodes, columns), lambda i: (0, 0)),
        ],
        out_specs=(
            pl.BlockSpec((columns, SIDE * ROWS), lambda i: (0, i)),
            pl.BlockSpec((ROWS, width), lambda i: (0, 0)),
            pl.BlockSpec((decodes, width), lambda i: (0, 0)),
            pl.BlockSpec((decodes, columns), lambda i: (0, 0)),
        ),
        compiler_params=pltpu.CompilerParams(
            dimension_semantics=("arbitrary",), vmem_limit_bytes=62 << 20
        ),
        name="layout",
    )(result, own, dec_own, dec_result)
    return layer_out, next_t.T, dec_out, dec_next


def solution(mesh):
    placed = (
        P(("rep", "tensor"), None),
        P(),
        P("rep", None, "tensor", None),
        P(None, "rep", "tensor", None),
        P(),
        P("rep"),
        P("rep", None),
        P(None, "tensor"),
        P("tensor", None),
        P(None, "tensor"),
        P("tensor"),
        P("tensor", None),
        P(),
        P(),
        P(),
        P(None, "tensor"),
    )
    return jax.shard_map(
        functools.partial(per_device, mesh.shape["rep"]),
        mesh=mesh,
        in_specs=placed,
        out_specs=(P(("rep", "tensor"), None), P("rep", "tensor"), P(), P(None, "tensor")),
        check_vma=False,
    )
```

```python
import functools

import jax
import jax.numpy as jnp
from jax import lax
from jax.experimental import pallas as pl
from jax.experimental.pallas import tpu as pltpu
from jax.sharding import PartitionSpec as P

MESH = pl.DeviceIdType.MESH
NEG = -1e30
LOG2E = 1.4426950408889634
SIDE = 4
ROWS = 64
VMEM = pltpu.VMEM
NT = (((1,), (1,)), ((), ()))


def place():
    t = lax.axis_index("tensor")
    core = lax.rem(lax.axis_index("rep"), 2)
    y, x = lax.div(t, SIDE), lax.rem(t, SIDE)
    major = y * (1 - core) + x * core
    minor = x * (1 - core) + y * core
    step_major, step_minor = SIDE - (SIDE - 1) * core, 1 + (SIDE - 1) * core

    def device(i, j):
        return lax.rem(i, SIDE) * step_major + lax.rem(j, SIDE) * step_minor

    return y, x, major, minor, device


class Copies:
    def __init__(self, send, recv):
        self.send, self.recv, self.used, self.all = send, recv, 0, []

    def start(self, src, dst, where):
        copy = pltpu.make_async_remote_copy(
            src_ref=src,
            dst_ref=dst,
            send_sem=self.send.at[self.used],
            recv_sem=self.recv.at[self.used],
            device_id=where,
            device_id_type=MESH,
        )
        copy.start()
        self.used += 1
        self.all.append(copy)
        return copy

    def drain(self):
        for copy in self.all:
            copy.wait_send()


def tensor(t):
    return {"tensor": t}


def greet(tensor_peers, rep_peers=()):
    barrier = pltpu.get_barrier_semaphore()
    for t in tensor_peers:
        pl.semaphore_signal(barrier, inc=1, device_id=tensor(t), device_id_type=MESH)
    for r in rep_peers:
        pl.semaphore_signal(barrier, inc=1, device_id={"rep": r}, device_id_type=MESH)
    pl.semaphore_wait(barrier, len(tensor_peers) + len(rep_peers))


class Gather:
    def __init__(self, copies, at, own=None):
        y, x, self.a, self.b, self.device = place()
        self.copies, self.at, self.own = copies, at, own

    def go(self, i, j, ti, tj):
        return self.copies.start(self.at(i, j), self.at(i, j), tensor(self.device(ti, tj)))

    def begin(self):
        a, b = self.a, self.b
        own = self.at(a, b) if self.own is None else self.own
        self.right, self.left, up, down = (
            self.copies.start(own, self.at(a, b), tensor(self.device(i, j)))
            for i, j in ((a, b + 1), (a, b + 3), (a + 1, b), (a + 3, b))
        )
        self.up, self.down = [up], [down]

    def spread(self, j):
        a, b = self.a, self.b
        self.up.append(self.go(a, j, a + 1, b))
        self.down.append(self.go(a, j, a + 3, b))

    def half(self, i, j, part):
        return self.at(i, j).at[pl.ds(part * (ROWS // 2), ROWS // 2)]

    def first(self):
        a, b = self.a, self.b
        self.right.wait_recv()
        one = self.half(a, b + 3, 0)
        far_one = self.copies.start(one, one, tensor(self.device(a, b + 1)))
        self.spread(b + 3)
        self.left.wait_recv()
        two = self.half(a, b + 1, 1)
        far_two = self.copies.start(two, two, tensor(self.device(a, b + 3)))
        self.spread(b + 1)
        far_one.wait_recv()
        far_two.wait_recv()
        self.spread(b + 2)

    def middle(self):
        a, b = self.a, self.b
        self.up[0].wait_recv()
        self.far = [self.go(a + 3, b, a + 1, b)]
        self.down[1].wait_recv()
        self.far.append(self.go(a + 1, b + 3, a + 3, b))
        self.down[2].wait_recv()
        self.far.append(self.go(a + 1, b + 1, a + 3, b))
        self.up[3].wait_recv()
        self.far.append(self.go(a + 3, b + 2, a + 1, b))
        self.up[1].wait_recv()
        self.up[2].wait_recv()
        self.down[0].wait_recv()
        self.down[3].wait_recv()

    def last(self):
        for copy in self.far:
            copy.wait_recv()


class RingSum:
    def __init__(self, copies, row, far, near, index, to):
        self.copies, self.slabs, self.far, self.near = copies, row, far, near
        self.c, self.next, self.prev = index, to(index + 1), to(index + 3)
        half = ROWS // 2
        self.top, self.low = pl.ds(0, half), pl.ds(half, half)

    def row(self, k):
        return self.slabs.at[lax.rem(self.c + k, SIDE)]

    def send_far(self):
        self.next_far = self.copies.start(self.row(2).at[self.top], self.far.at[0], self.next)
        self.prev_far = self.copies.start(self.row(2).at[self.low], self.far.at[1], self.prev)

    def send_next(self):
        self.next_near = self.copies.start(
            self.row(1).at[self.low], self.near.at[0, self.low], self.next
        )

    def send_prev(self):
        self.prev_near = self.copies.start(
            self.row(3).at[self.top], self.near.at[1, self.top], self.prev
        )

    def pass_on(self):
        self.next_far.wait_recv()
        add_into(self.row(1).at[self.top], self.far[0])
        self.next_sum = self.copies.start(
            self.row(1).at[self.top], self.near.at[0, self.top], self.next
        )
        self.prev_far.wait_recv()
        add_into(self.row(3).at[self.low], self.far[1])
        self.prev_sum = self.copies.start(
            self.row(3).at[self.low], self.near.at[1, self.low], self.prev
        )

    def finish(self, own):
        for copy in (self.next_near, self.prev_near, self.next_sum, self.prev_sum):
            copy.wait_recv()
        return own + self.near[0].astype(jnp.float32) + self.near[1].astype(jnp.float32)


class RingGather:
    def __init__(self, copies, slabs, index, to):
        self.copies, self.slabs, self.c = copies, slabs, index
        self.next, self.prev = to(index + 1), to(index + 3)
        half = ROWS // 2
        self.top, self.low = pl.ds(0, half), pl.ds(half, half)

    def go(self, k, part, where):
        piece = self.slabs.at[lax.rem(self.c + k, SIDE)].at[part]
        return self.copies.start(piece, piece, where)

    def run(self):
        first = (self.go(0, self.top, self.next), self.go(0, self.low, self.prev))
        second = (self.go(0, self.low, self.next), self.go(0, self.top, self.prev))
        first[0].wait_recv()
        far = [self.go(3, self.top, self.next)]
        first[1].wait_recv()
        far.append(self.go(1, self.low, self.prev))
        for copy in (*second, *far):
            copy.wait_recv()


def quarter(width, plane, planes):
    size = width // planes
    return pl.ds(pl.multiple_of(lax.rem(plane, planes) * size, 128), size)


class Levels:
    def __init__(self, copies, rep, reps):
        self.copies, self.plane, self.planes = copies, lax.div(rep, 2), reps // 2
        self.above, self.below = (
            {"rep": lax.rem(rep + 2 * k, reps)} for k in (1, self.planes - 1)
        )
        self.sent = []

    def share(self, array, k):
        return array.at[:, quarter(array.shape[1], self.plane + k, self.planes)]

    def spread(self, array):
        piece = self.share(array, 0)
        self.sent.append(
            (
                array,
                self.copies.start(piece, piece, self.above),
                self.copies.start(piece, piece, self.below),
            )
        )

    def pass_on(self):
        self.far = []
        for array, from_below, from_above in self.sent:
            half = array.shape[0] // 2
            from_below.wait_recv()
            piece = self.share(array, self.planes - 1).at[pl.ds(0, half)]
            self.far.append(self.copies.start(piece, piece, self.above))
            from_above.wait_recv()
            piece = self.share(array, 1).at[pl.ds(half, half)]
            self.far.append(self.copies.start(piece, piece, self.below))

    def finish(self):
        for copy in self.far:
            copy.wait_recv()


class RowRing:
    def __init__(self, copies, shards, own, columns, index, to):
        self.copies, self.shards, self.columns, self.c = copies, shards, columns, index
        self.next, self.prev = to(index + 1), to(index + 3)
        half = own.shape[0] // 2
        self.parts = pl.ds(0, half), pl.ds(half, half)
        top, low = (own.at[part, columns] for part in self.parts)
        self.first = (self.go(0, 0, self.next, top), self.go(0, 1, self.prev, low))
        self.second = (self.go(0, 1, self.next, low), self.go(0, 0, self.prev, top))

    def go(self, k, part, where, source=None):
        piece = self.shards.at[lax.rem(self.c + k, SIDE), self.parts[part], self.columns]
        return self.copies.start(piece if source is None else source, piece, where)

    def pass_on(self):
        self.first[0].wait_recv()
        self.far = [self.go(3, 0, self.next)]
        self.first[1].wait_recv()
        self.far.append(self.go(1, 1, self.prev))

    def finish(self):
        for copy in (*self.second, *self.far):
            copy.wait_recv()


def add_into(ref, value):
    ref[...] = (ref[...].astype(jnp.float32) + value.astype(jnp.float32)).astype(ref.dtype)


class Scatter:
    def __init__(self, copies, parts, far, near, row, row_far, row_near):
        y, x, a, b, self.device = place()
        self.a, self.b = a, b
        self.copies, self.parts, self.far, self.near = copies, parts, far, near
        self.ring = RingSum(
            copies, row, row_far, row_near, b, lambda j: tensor(self.device(a, j))
        )
        self.above, self.below = tensor(self.device(a + 1, b)), tensor(self.device(a + 3, b))
        self.ups, self.downs = (b + 2, b + 1), (b + 3, b)

    def part(self, i, j):
        return self.parts.at[lax.rem(i, SIDE), lax.rem(j, SIDE)]

    def landing(self, side, j):
        return self.near.at[side, lax.rem(j, SIDE)]

    def send_far(self):
        self.far_up, self.far_down = [], []
        for k in range(2):
            self.far_up.append(
                self.copies.start(self.part(self.a + 2, self.ups[k]), self.far.at[0, k], self.above)
            )
            self.far_down.append(
                self.copies.start(
                    self.part(self.a + 2, self.downs[k]), self.far.at[1, k], self.below
                )
            )

    def send_near(self):
        self.near_up, self.near_down = [], []
        for k in range(2):
            self.near_up.append(
                self.copies.start(
                    self.part(self.a + 1, self.downs[k]),
                    self.landing(0, self.downs[k]),
                    self.above,
                )
            )
            self.near_down.append(
                self.copies.start(
                    self.part(self.a + 3, self.ups[k]), self.landing(1, self.ups[k]), self.below
                )
            )

    def pass_on(self):
        self.sum_up, self.sum_down = [], []
        for k in range(2):
            self.far_up[k].wait_recv()
            add_into(self.part(self.a + 1, self.ups[k]), self.far[0, k])
            self.sum_up.append(
                self.copies.start(
                    self.part(self.a + 1, self.ups[k]), self.landing(0, self.ups[k]), self.above
                )
            )
            self.far_down[k].wait_recv()
            add_into(self.part(self.a + 3, self.downs[k]), self.far[1, k])
            self.sum_down.append(
                self.copies.start(
                    self.part(self.a + 3, self.downs[k]),
                    self.landing(1, self.downs[k]),
                    self.below,
                )
            )

    def total(self, j):
        at = lax.rem(j, SIDE)
        return (
            self.parts[self.a, at].astype(jnp.float32)
            + self.near[0, at].astype(jnp.float32)
            + self.near[1, at].astype(jnp.float32)
        )

    def finish(self):
        ring, b = self.ring, self.b
        self.sum_up[0].wait_recv()
        self.near_down[0].wait_recv()
        ring.row(2)[...] = self.total(b + 2).astype(jnp.bfloat16)
        ring.send_far()
        self.near_up[0].wait_recv()
        self.sum_down[0].wait_recv()
        ring.row(3)[...] = self.total(b + 3).astype(jnp.bfloat16)
        ring.send_prev()
        self.sum_up[1].wait_recv()
        self.near_down[1].wait_recv()
        ring.row(1)[...] = self.total(b + 1).astype(jnp.bfloat16)
        ring.send_next()
        ring.pass_on()
        self.near_up[1].wait_recv()
        self.sum_down[1].wait_recv()
        return ring.finish(self.total(b))


class SmallSum:
    def __init__(self, copies, over_x, over_y):
        t = lax.axis_index("tensor")
        self.y, self.x = lax.div(t, SIDE), lax.rem(t, SIDE)
        self.copies, self.over_x, self.over_y = copies, over_x, over_y

    def begin(self, value):
        self.over_x[self.x] = value.astype(jnp.bfloat16)
        mine = self.over_x.at[self.x]
        self.sent = [
            self.copies.start(
                mine, mine, tensor(SIDE * self.y + lax.rem(self.x + k, SIDE))
            )
            for k in (1, 2, 3)
        ]

    def middle(self):
        for copy in self.sent:
            copy.wait_recv()
        self.over_y[self.y] = sum(
            self.over_x[k].astype(jnp.float32) for k in range(SIDE)
        ).astype(jnp.bfloat16)
        mine = self.over_y.at[self.y]
        self.sent = [
            self.copies.start(
                mine, mine, tensor(SIDE * lax.rem(self.y + k, SIDE) + self.x)
            )
            for k in (1, 2, 3)
        ]

    def finish(self):
        for copy in self.sent:
            copy.wait_recv()
        return sum(self.over_y[k].astype(jnp.float32) for k in range(SIDE))


def layer_norm(values, gain_row, shift_row):
    average = jnp.mean(values, axis=-1, keepdims=True)
    centred = values - average
    spread = jnp.mean(centred * centred, axis=-1, keepdims=True)
    return centred * lax.rsqrt(spread + 1e-05) * gain_row + shift_row


def project_kernel(
    reps,
    scale,
    len_ref,
    dec_ref,
    x_hbm,
    w_hbm,
    cache_hbm,
    w_out_hbm,
    out_ref,
    attn_ref,
    w_row_hbm,
    rows,
    dec_rows,
    w_ref,
    cache_ref,
    states,
    local_sem,
    send_sem,
    recv_sem,
):
    y, x, a, b, device = place()
    load_x = pltpu.make_async_copy(x_hbm, rows.at[device(a, b)], local_sem.at[2])
    load_x.start()
    load_w = pltpu.make_async_copy(w_hbm, w_ref, local_sem.at[0])
    load_w.start()
    load_cache = pltpu.make_async_copy(cache_hbm, cache_ref, local_sem.at[1])
    load_cache.start()
    keep_w = pltpu.make_async_copy(w_out_hbm, w_row_hbm.at[b], local_sem.at[3])
    keep_w.start()
    rep = lax.axis_index("rep")
    copies = Copies(send_sem, recv_sem)
    greet(
        [device(a, b + k) for k in (1, 2, 3)] + [device(a + 1, b), device(a + 3, b)],
        [lax.rem(rep + k, reps) for k in range(1, reps)],
    )
    gather = Gather(copies, lambda i, j: rows.at[device(i, j)])
    mine = quarter(w_out_hbm.shape[1], lax.div(rep, 2), reps // 2)
    shards = [
        copies.start(
            w_out_hbm.at[:, mine], w_row_hbm.at[b, :, mine], tensor(device(a, b + k))
        )
        for k in (1, 3, 2)
    ]
    load_x.wait()
    gather.begin()
    dec_rows[...] = jnp.zeros_like(dec_rows)
    dec_rows[: dec_ref.shape[0]] = dec_ref[...]
    load_w.wait()
    dec = (
        lax.dot_general(w_ref[...], dec_rows[...], NT, preferred_element_type=jnp.float32)
        .astype(jnp.bfloat16)
        .astype(jnp.float32)
    )
    gather.first()
    levels = Levels(copies, rep, reps)
    for k, shard in zip((1, 3, 2), shards):
        shard.wait_recv()
        levels.spread(w_row_hbm.at[lax.rem(b - k + SIDE, SIDE)])
    load_cache.wait()
    hd = cache_ref.shape[2] // 2
    heads = cache_ref.shape[1]
    span = cache_ref.shape[3]
    lanes = dec.shape[1]
    lane = lax.broadcasted_iota(jnp.int32, (1, lanes), 1)
    position = rep * span + lax.broadcasted_iota(jnp.int32, (1, span), 1)

    def request(r, state):
        pick = lane == r
        column = jnp.sum(jnp.where(pick, dec, 0.0), axis=1, keepdims=True)
        valid = position < len_ref[r]
        out = []
        for h in range(heads):
            query = column[3 * hd * h : 3 * hd * h + hd]
            key = cache_ref[r, h, :hd].astype(jnp.float32)
            value = cache_ref[r, h, hd:].astype(jnp.float32)
            score = jnp.sum(key * query, axis=0, keepdims=True) * scale
            score = jnp.where(valid, score, NEG)
            high = jnp.max(score, axis=1, keepdims=True)
            weight = jnp.where(valid, jnp.exp(score - high), 0.0)
            total = jnp.sum(weight, axis=1, keepdims=True)
            mixed = jnp.sum(value * weight, axis=1, keepdims=True)
            highs, totals, mixes = state[h]
            out.append(
                (
                    jnp.where(pick, high, highs),
                    jnp.where(pick, total, totals),
                    jnp.where(pick, mixed, mixes),
                )
            )
        return tuple(out)

    empty = tuple(
        (
            jnp.full((1, lanes), NEG, jnp.float32),
            jnp.zeros((1, lanes), jnp.float32),
            jnp.zeros((hd, lanes), jnp.float32),
        )
        for _ in range(heads)
    )
    state = lax.fori_loop(0, cache_ref.shape[0], request, empty)
    for h in range(heads):
        states[rep, h, :hd] = state[h][2]
        states[rep, h, hd : hd + 8] = jnp.broadcast_to(state[h][0], (8, lanes))
        states[rep, h, hd + 8 : hd + 16] = jnp.broadcast_to(state[h][1], (8, lanes))
    sent = [
        copies.start(states.at[rep], states.at[rep], {"rep": lax.rem(rep + k, reps)})
        for k in range(1, reps)
    ]
    gather.middle()
    levels.pass_on()
    for copy in sent:
        copy.wait_recv()
    for h in range(heads):
        base = 3 * hd * h
        query, key, value = (dec[base + hd * k : base + hd * (k + 1)] for k in range(3))
        own = jnp.sum(query * key, axis=0, keepdims=True) * scale
        highest = own
        for k in range(reps):
            highest = jnp.maximum(highest, states[k, h, hd : hd + 1])
        own_weight = jnp.exp(own - highest)
        total, mixed = own_weight, own_weight * value
        for k in range(reps):
            factor = jnp.exp(states[k, h, hd : hd + 1] - highest)
            total = total + factor * states[k, h, hd + 8 : hd + 9]
            mixed = mixed + factor * states[k, h, :hd]
        attn_ref[:, hd * h : hd * (h + 1)] = (mixed / total).T[: attn_ref.shape[0]].astype(
            attn_ref.dtype
        )
    gather.last()

    @pl.loop(0, SIDE)
    def _(i):
        block = rows[pl.ds(SIDE * i, SIDE)].reshape(SIDE * ROWS, rows.shape[2])
        out_ref[:, pl.ds(pl.multiple_of(i * SIDE * ROWS, SIDE * ROWS), SIDE * ROWS)] = (
            lax.dot_general(w_ref[...], block, NT, preferred_element_type=jnp.float32).astype(
                out_ref.dtype
            )
        )

    levels.finish()
    keep_w.wait()
    copies.drain()


def attend(head, scale, offset, qkv_ref, kv_ref, seg_row, out_ref, q_ref, state):
    hd = q_ref.shape[1]
    span = seg_row.shape[1]
    block, key_block = 256, 1024
    early = span // 2 // block
    factor = scale * LOG2E
    q_ref[...] = qkv_ref[head, 0].astype(jnp.float32).T.astype(jnp.bfloat16)
    seg_keys = seg_row[...].astype(jnp.float32)
    seg_rows = jnp.broadcast_to(seg_keys, (8, span)).T[:, :1]
    states = [state[3 * i : 3 * i + 3] for i in range(early)]

    def rows(i):
        return slice(i * block, (i + 1) * block)

    def mix(weight, values):
        return lax.dot_general(
            weight.astype(jnp.bfloat16), values, NT, preferred_element_type=jnp.float32
        )

    for m_ref, l_ref, acc_ref in states:
        m_ref[...] = jnp.full(m_ref.shape, NEG, jnp.float32)
        l_ref[...] = jnp.zeros(l_ref.shape, jnp.float32)
        acc_ref[...] = jnp.zeros(acc_ref.shape, jnp.float32)

    @pl.loop(0, kv_ref.shape[2] // key_block)
    def _(j):
        at = pl.multiple_of(j * key_block, key_block)
        keys = kv_ref[head, :hd, pl.ds(at, key_block)]
        values = kv_ref[head, hd:, pl.ds(at, key_block)]
        seen = at + lax.broadcasted_iota(jnp.int32, (1, key_block), 1) < offset
        scores = [
            jnp.dot(q_ref[rows(i)], keys, preferred_element_type=jnp.float32)
            for i in range(early)
        ]
        for score, (m_ref, l_ref, acc_ref) in zip(scores, states):
            score = jnp.where(seen, score, NEG)
            high = jnp.maximum(m_ref[...], jnp.max(score, axis=1, keepdims=True))
            decay = jnp.exp2((m_ref[...] - high) * factor)
            weight = jnp.exp2((score - high) * factor)
            m_ref[...] = high
            l_ref[...] = l_ref[...] * decay + jnp.sum(weight, axis=1, keepdims=True)
            acc_ref[...] = acc_ref[...] * decay + mix(weight, values)

    for i in range(span // block):
        low = max(0, (i - early) * block)
        high = (i + 1) * block
        seg_q = seg_rows[rows(i)]
        score = jnp.dot(
            q_ref[rows(i)], qkv_ref[head, 1, :, low:high], preferred_element_type=jnp.float32
        )
        shape = (block, high - low)
        query_at = i * block + lax.broadcasted_iota(jnp.int32, shape, 0)
        key_at = low + lax.broadcasted_iota(jnp.int32, shape, 1)
        seen = (seg_keys[:, low:high] == seg_q) & (key_at <= query_at)
        score = jnp.where(seen, score, NEG)
        values = qkv_ref[head, 2, :, low:high]
        peak = jnp.max(score, axis=1, keepdims=True)
        if i < early:
            m_ref, l_ref, acc_ref = states[i]
            keep = (seg_q == 0) & (offset > 0)
            before = jnp.where(keep, m_ref[...], NEG)
            peak = jnp.maximum(peak, before)
            decay = jnp.where(keep, jnp.exp2((before - peak) * factor), 0.0)
        weight = jnp.exp2((score - peak) * factor)
        total = jnp.sum(weight, axis=1, keepdims=True)
        mixed = mix(weight, values)
        if i < early:
            total = total + l_ref[...] * decay
            mixed = mixed + acc_ref[...] * decay
        out_ref[rows(i), head * hd : (head + 1) * hd] = (mixed / total).astype(out_ref.dtype)


def tail_kernel(
    scale,
    reps,
    offset_ref,
    seg_row,
    dec_attn_ref,
    x_dec_ref,
    up_bias_ref,
    biases_ref,
    gains_ref,
    shifts_ref,
    qkv_hbm,
    kv_hbm,
    x_hbm,
    w_row_hbm,
    w_up_hbm,
    w_down_hbm,
    w_next_hbm,
    result_hbm,
    out_ref,
    dec_out_ref,
    dec_next_ref,
    qkv_ref,
    kv_ref,
    x_ref,
    w_row_ref,
    w_up_ref,
    w_down_ref,
    w_next_ref,
    attn_ref,
    heads_ref,
    columns_ref,
    result_ref,
    slabs,
    parts,
    far,
    near,
    row,
    row_far,
    row_near,
    over_x,
    over_y,
    q_ref,
    m0_ref,
    l0_ref,
    acc0_ref,
    m1_ref,
    l1_ref,
    acc1_ref,
    local_sem,
    send_sem,
    recv_sem,
):
    y, x, a, b, device = place()
    loads = []
    for k, (source, target) in enumerate(
        (
            (qkv_hbm, qkv_ref),
            (kv_hbm, kv_ref),
            (w_row_hbm, w_row_ref),
            (x_hbm, x_ref),
            (w_next_hbm, w_next_ref.at[b]),
            (w_up_hbm, w_up_ref),
            (w_down_hbm, w_down_ref),
        )
    ):
        loads.append(pltpu.make_async_copy(source, target, local_sem.at[k]))
        loads[-1].start()
    load_qkv, load_kv, load_row, load_x, load_next, load_up, load_down = loads
    copies = Copies(send_sem, recv_sem)
    rep = lax.axis_index("rep")
    plane, planes = lax.div(rep, 2), reps // 2
    columns, width = w_next_hbm.shape

    greet(
        [SIDE * y + lax.rem(x + k, SIDE) for k in (1, 2, 3)]
        + [SIDE * lax.rem(y + k, SIDE) + x for k in (1, 2, 3)],
        [lax.rem(rep + 2 * k, reps) for k in (1, planes - 1)],
    )
    chunk = (SIDE, ROWS, width)
    load_row.wait()
    dec_sum = SmallSum(copies, over_x.at[0], over_y.at[0])
    dec_sum.begin(
        jnp.dot(dec_attn_ref[...], w_row_ref[b], preferred_element_type=jnp.float32)
    )
    shards = RowRing(
        copies,
        w_next_ref,
        w_next_hbm,
        quarter(width, plane, planes),
        b,
        lambda j: tensor(device(a, j)),
    )
    attn_ref[...] = jnp.zeros_like(attn_ref)
    result_ref[...] = jnp.zeros_like(result_ref)
    load_qkv.wait()
    load_kv.wait()
    state = (m0_ref, l0_ref, acc0_ref, m1_ref, l1_ref, acc1_ref)
    offset = offset_ref[0]
    heads = qkv_ref.shape[0]
    for head in range(heads):
        attend(head, scale, offset, qkv_ref, kv_ref, seg_row, attn_ref, q_ref, state)
        if head == 0:
            dec_sum.middle()
            shards.pass_on()

    def tokens(i, j):
        return attn_ref.at[pl.ds(pl.multiple_of(device(i, j) * ROWS, ROWS), ROWS)]

    swaps = [
        copies.start(tokens(i, b + k), heads_ref.at[b, i], tensor(device(a, b + k)))
        for k in (2, 1, 3)
        for i in range(SIDE)
    ]
    for i in range(SIDE):
        heads_ref[b, i] = tokens(i, b)[...]
    for swap in swaps:
        swap.wait_recv()
    ring = RingSum(
        copies, row.at[0], row_far.at[0], row_near.at[0], a, lambda i: tensor(device(i, b))
    )
    depth = w_row_ref.shape[1]
    step = width // 5
    for n in range(0, width, step):
        total = sum(
            jnp.dot(
                heads_ref[j].reshape(SIDE * ROWS, heads_ref.shape[3])[:, :depth],
                w_row_ref[j, :, n : n + step],
                preferred_element_type=jnp.float32,
            )
            for j in range(SIDE)
        )
        row[0, :, :, n : n + step] = total.astype(jnp.bfloat16).reshape(SIDE, ROWS, step)
    ring.send_far()
    ring.send_next()
    ring.send_prev()
    ring.pass_on()
    shards.finish()
    levels = Levels(copies, rep, reps)
    for k in (1, 2, 3):
        levels.spread(w_next_ref.at[lax.rem(b + k, SIDE)])
    dec_first = layer_norm(
        x_dec_ref[...].astype(jnp.float32) + dec_sum.finish() + biases_ref[0:1],
        gains_ref[0:1],
        shifts_ref[0:1],
    ).astype(jnp.bfloat16)
    own = row[0, a].astype(jnp.float32)
    load_x.wait()
    attn_sum = ring.finish(own)
    first = layer_norm(
        x_ref[...].astype(jnp.float32) + attn_sum + biases_ref[0:1], gains_ref[0:1], shifts_ref[0:1]
    ).astype(jnp.bfloat16)

    def slab(i, j):
        return slabs.at[lax.rem(i, SIDE), lax.rem(j, SIDE)]

    slab(a, b)[...] = first
    gather = Gather(copies, slab)
    gather.begin()
    load_up.wait()
    load_down.wait()

    def mlp(value):
        inner = jnp.dot(value, w_up_ref[...], preferred_element_type=jnp.float32)
        inner = inner + up_bias_ref[...][None, :]
        hidden = (0.5 * inner * (1.0 + lax.erf(inner * 0.7071067811865476))).astype(jnp.bfloat16)
        return jnp.dot(hidden, w_down_ref[...], preferred_element_type=jnp.float32)

    dec_sum = SmallSum(copies, over_x.at[1], over_y.at[1])
    dec_sum.begin(mlp(dec_first))

    def mlp_share(i):
        at = lax.rem(i, SIDE)
        parts[at] = (
            mlp(slabs[at].reshape(SIDE * ROWS, width)).astype(jnp.bfloat16).reshape(chunk)
        )

    scatter = Scatter(copies, parts, far, near, row.at[1], row_far.at[1], row_near.at[1])
    gather.first()
    mlp_share(a)
    gather.middle()
    mlp_share(a + 1)
    mlp_share(a + 3)
    scatter.send_near()
    dec_sum.middle()
    gather.last()
    mlp_share(a + 2)
    scatter.send_far()
    scatter.pass_on()
    levels.pass_on()
    dec_out = layer_norm(
        dec_first.astype(jnp.float32) + dec_sum.finish() + biases_ref[1:2],
        gains_ref[1:2],
        shifts_ref[1:2],
    ).astype(jnp.bfloat16)
    dec_out_ref[...] = dec_out
    load_next.wait()
    dec_next_ref[...] = lax.dot_general(
        dec_out, w_next_ref[b], NT, preferred_element_type=jnp.float32
    ).astype(jnp.bfloat16)
    mlp_sum = scatter.finish()
    second = layer_norm(
        first.astype(jnp.float32) + mlp_sum + biases_ref[1:2], gains_ref[1:2], shifts_ref[1:2]
    ).astype(jnp.bfloat16)
    out_ref[...] = second
    columns_ref[a] = second
    RingGather(copies, columns_ref, a, lambda i: tensor(device(i, b))).run()
    levels.finish()
    keeps = []
    for k in (2, 1, 3, 0):
        j = lax.rem(b + k, SIDE)
        result_ref[j, :, :, :columns] = (
            lax.dot_general(
                columns_ref[...].reshape(SIDE * ROWS, width),
                w_next_ref[j],
                NT,
                preferred_element_type=jnp.float32,
            )
            .astype(jnp.bfloat16)
            .reshape(SIDE, ROWS, columns)
        )
        for i in range(SIDE):
            source, target = result_ref.at[j, i], result_hbm.at[device(i, b)]
            if k:
                keeps.append(copies.start(source, target, tensor(device(a, j))))
            else:
                local = pltpu.make_async_copy(source, target, local_sem.at[i])
                local.start()
                loads.append(local)
    for copy in keeps:
        copy.wait_recv()
    for local in loads[-SIDE:]:
        local.wait()
    copies.drain()


def layout_kernel(
    result_ref, own_ref, dec_ref, dec_result_ref, next_ref, out_ref, dec_out_ref, dec_next_ref
):
    columns, lanes = next_ref.shape[0], result_ref.shape[2]
    same = lax.broadcasted_iota(jnp.int32, (columns, lanes), 0) == lax.broadcasted_iota(
        jnp.int32, (columns, lanes), 1
    )
    next_ref[...] = lax.dot_general(
        same.astype(jnp.float32).astype(jnp.bfloat16),
        result_ref[...].reshape(SIDE * ROWS, lanes),
        NT,
        preferred_element_type=jnp.float32,
    ).astype(next_ref.dtype)

    @pl.when(pl.program_id(0) == 0)
    def _():
        out_ref[...] = own_ref[...]
        dec_out_ref[...] = dec_ref[...]
        dec_next_ref[...] = dec_result_ref[...]


def per_device(
    reps,
    x_pre,
    x_dec,
    prefix_kv,
    cache_kv,
    dec_len,
    offsets,
    segments,
    w_qkv,
    w_out,
    w_up,
    up_bias,
    w_down,
    biases,
    gains,
    shifts,
    w_next,
):
    heads = prefix_kv.shape[2]
    hd = prefix_kv.shape[3] // 2
    span = segments.shape[1]
    width = x_pre.shape[1]
    decodes = x_dec.shape[0]
    columns = w_qkv.shape[1]
    units = w_up.shape[1]
    scale = hd ** (-0.5)
    bf16, f32 = jnp.bfloat16, jnp.float32
    shape = jax.ShapeDtypeStruct
    whole = pl.BlockSpec(memory_space=VMEM)
    scalars = pl.BlockSpec(memory_space=pltpu.SMEM)
    anywhere = pl.BlockSpec(memory_space=pltpu.HBM)
    group = SIDE * SIDE

    cache_t = cache_kv.transpose(0, 2, 3, 1)
    n_copies = 16 + reps - 1 + (SIDE - 1) * 5
    qkv_t, dec_attn, w_row = pl.pallas_call(
        functools.partial(project_kernel, reps, scale),
        out_shape=(
            shape((columns, span), bf16),
            shape((decodes, heads * hd), bf16),
            shape((SIDE,) + w_out.shape, bf16),
        ),
        in_specs=[scalars, whole] + [anywhere] * 4,
        out_specs=(whole, whole, anywhere),
        scratch_shapes=[
            VMEM((group, ROWS, width), bf16),
            VMEM((128, width), bf16),
            VMEM((columns, width), bf16),
            VMEM(cache_t.shape, bf16),
            VMEM((reps, heads, hd + 16, 128), f32),
            pltpu.SemaphoreType.DMA((4,)),
            pltpu.SemaphoreType.DMA((n_copies,)),
            pltpu.SemaphoreType.DMA((n_copies,)),
        ],
        compiler_params=pltpu.CompilerParams(
            collective_id=0, has_side_effects=True, vmem_limit_bytes=62 << 20
        ),
        name="project",
    )(dec_len, x_dec, x_pre, w_qkv.T, cache_t, w_out)

    n_copies = 100
    lanes = 512
    result, own, dec_own, dec_result = pl.pallas_call(
        functools.partial(tail_kernel, scale, reps),
        out_shape=(
            shape((group, ROWS, lanes), bf16),
            shape((ROWS, width), bf16),
            shape((decodes, width), bf16),
            shape((decodes, columns), bf16),
        ),
        in_specs=[scalars] + [whole] * 7 + [anywhere] * 7,
        out_specs=(anywhere, whole, whole, whole),
        scratch_shapes=[
            VMEM((heads, 3, hd, span), bf16),
            VMEM((heads, 2 * hd, prefix_kv.shape[1]), bf16),
            VMEM((ROWS, width), bf16),
            VMEM((SIDE,) + w_out.shape, bf16),
            VMEM((width, units), bf16),
            VMEM((units, width), bf16),
            VMEM((SIDE, columns, width), bf16),
            VMEM((span, 256), bf16),
            VMEM((SIDE, SIDE, ROWS, 256), bf16),
            VMEM((SIDE, ROWS, width), bf16),
            VMEM((SIDE, SIDE, ROWS, lanes), bf16),
            VMEM((SIDE, SIDE, ROWS, width), bf16),
            VMEM((SIDE, SIDE, ROWS, width), bf16),
            VMEM((2, 2, ROWS, width), bf16),
            VMEM((2, SIDE, ROWS, width), bf16),
            VMEM((2, SIDE, ROWS, width), bf16),
            VMEM((2, 2, ROWS // 2, width), bf16),
            VMEM((2, 2, ROWS, width), bf16),
            VMEM((2, SIDE, decodes, width), bf16),
            VMEM((2, SIDE, decodes, width), bf16),
            VMEM((span, hd), bf16),
            *([VMEM((256, 1), f32), VMEM((256, 1), f32), VMEM((256, hd), f32)] * 2),
            pltpu.SemaphoreType.DMA((8,)),
            pltpu.SemaphoreType.DMA((n_copies,)),
            pltpu.SemaphoreType.DMA((n_copies,)),
        ],
        compiler_params=pltpu.CompilerParams(
            collective_id=1, has_side_effects=True, vmem_limit_bytes=62 << 20
        ),
        name="tail",
    )(
        offsets,
        segments,
        dec_attn,
        x_dec,
        up_bias,
        biases,
        gains,
        shifts,
        qkv_t.reshape(heads, 3, hd, span),
        prefix_kv[0].transpose(1, 2, 0),
        x_pre,
        w_row,
        w_up,
        w_down,
        w_next.T,
    )

    next_t, layer_out, dec_out, dec_next = pl.pallas_call(
        layout_kernel,
        grid=(SIDE,),
        out_shape=(
            shape((columns, span), bf16),
            shape((ROWS, width), bf16),
            shape((decodes, width), bf16),
            shape((decodes, columns), bf16),
        ),
        in_specs=[
            pl.BlockSpec((SIDE, ROWS, lanes), lambda i: (i, 0, 0)),
            pl.BlockSpec((ROWS, width), lambda i: (0, 0)),
            pl.BlockSpec((decodes, width), lambda i: (0, 0)),
            pl.BlockSpec((decodes, columns), lambda i: (0, 0)),
        ],
        out_specs=(
            pl.BlockSpec((columns, SIDE * ROWS), lambda i: (0, i)),
            pl.BlockSpec((ROWS, width), lambda i: (0, 0)),
            pl.BlockSpec((decodes, width), lambda i: (0, 0)),
            pl.BlockSpec((decodes, columns), lambda i: (0, 0)),
        ),
        compiler_params=pltpu.CompilerParams(
            dimension_semantics=("arbitrary",), vmem_limit_bytes=62 << 20
        ),
        name="layout",
    )(result, own, dec_own, dec_result)
    return layer_out, next_t.T, dec_out, dec_next


def solution(mesh):
    placed = (
        P(("rep", "tensor"), None),
        P(),
        P("rep", None, "tensor", None),
        P(None, "rep", "tensor", None),
        P(),
        P("rep"),
        P("rep", None),
        P(None, "tensor"),
        P("tensor", None),
        P(None, "tensor"),
        P("tensor"),
        P("tensor", None),
        P(),
        P(),
        P(),
        P(None, "tensor"),
    )
    return jax.shard_map(
        functools.partial(per_device, mesh.shape["rep"]),
        mesh=mesh,
        in_specs=placed,
        out_specs=(P(("rep", "tensor"), None), P("rep", "tensor"), P(), P(None, "tensor")),
        check_vma=False,
    )
```

```python
import functools

import jax
import jax.numpy as jnp
from jax import lax
from jax.experimental import pallas as pl
from jax.experimental.pallas import tpu as pltpu
from jax.sharding import PartitionSpec as P

MESH = pl.DeviceIdType.MESH
NEG = -1e30
LOG2E = 1.4426950408889634
SIDE = 4
ROWS = 64
VMEM = pltpu.VMEM
NT = (((1,), (1,)), ((), ()))


def place():
    t = lax.axis_index("tensor")
    core = lax.rem(lax.axis_index("rep"), 2)
    y, x = lax.div(t, SIDE), lax.rem(t, SIDE)
    major = y * (1 - core) + x * core
    minor = x * (1 - core) + y * core
    step_major, step_minor = SIDE - (SIDE - 1) * core, 1 + (SIDE - 1) * core

    def device(i, j):
        return lax.rem(i, SIDE) * step_major + lax.rem(j, SIDE) * step_minor

    return y, x, major, minor, device


class Copies:
    def __init__(self, send, recv):
        self.send, self.recv, self.used, self.all = send, recv, 0, []

    def start(self, src, dst, where):
        copy = pltpu.make_async_remote_copy(
            src_ref=src,
            dst_ref=dst,
            send_sem=self.send.at[self.used],
            recv_sem=self.recv.at[self.used],
            device_id=where,
            device_id_type=MESH,
        )
        copy.start()
        self.used += 1
        self.all.append(copy)
        return copy

    def drain(self):
        for copy in self.all:
            copy.wait_send()


def tensor(t):
    return {"tensor": t}


def greet(tensor_peers, rep_peers=()):
    barrier = pltpu.get_barrier_semaphore()
    for t in tensor_peers:
        pl.semaphore_signal(barrier, inc=1, device_id=tensor(t), device_id_type=MESH)
    for r in rep_peers:
        pl.semaphore_signal(barrier, inc=1, device_id={"rep": r}, device_id_type=MESH)
    pl.semaphore_wait(barrier, len(tensor_peers) + len(rep_peers))


class Gather:
    def __init__(self, copies, at, own=None):
        y, x, self.a, self.b, self.device = place()
        self.copies, self.at, self.own = copies, at, own

    def go(self, i, j, ti, tj):
        return self.copies.start(self.at(i, j), self.at(i, j), tensor(self.device(ti, tj)))

    def begin(self):
        a, b = self.a, self.b
        own = self.at(a, b) if self.own is None else self.own
        self.right, self.left, up, down = (
            self.copies.start(own, self.at(a, b), tensor(self.device(i, j)))
            for i, j in ((a, b + 1), (a, b + 3), (a + 1, b), (a + 3, b))
        )
        self.up, self.down = [up], [down]

    def spread(self, j):
        a, b = self.a, self.b
        self.up.append(self.go(a, j, a + 1, b))
        self.down.append(self.go(a, j, a + 3, b))

    def half(self, i, j, part):
        return self.at(i, j).at[pl.ds(part * (ROWS // 2), ROWS // 2)]

    def first(self):
        a, b = self.a, self.b
        self.right.wait_recv()
        one = self.half(a, b + 3, 0)
        far_one = self.copies.start(one, one, tensor(self.device(a, b + 1)))
        self.spread(b + 3)
        self.left.wait_recv()
        two = self.half(a, b + 1, 1)
        far_two = self.copies.start(two, two, tensor(self.device(a, b + 3)))
        self.spread(b + 1)
        far_one.wait_recv()
        far_two.wait_recv()
        self.spread(b + 2)

    def middle(self):
        a, b = self.a, self.b
        self.up[0].wait_recv()
        self.far = [self.go(a + 3, b, a + 1, b)]
        self.down[1].wait_recv()
        self.far.append(self.go(a + 1, b + 3, a + 3, b))
        self.down[2].wait_recv()
        self.far.append(self.go(a + 1, b + 1, a + 3, b))
        self.up[3].wait_recv()
        self.far.append(self.go(a + 3, b + 2, a + 1, b))
        self.up[1].wait_recv()
        self.up[2].wait_recv()
        self.down[0].wait_recv()
        self.down[3].wait_recv()

    def last(self):
        for copy in self.far:
            copy.wait_recv()


class RingSum:
    def __init__(self, copies, row, far, near, index, to):
        self.copies, self.slabs, self.far, self.near = copies, row, far, near
        self.c, self.next, self.prev = index, to(index + 1), to(index + 3)
        half = ROWS // 2
        self.top, self.low = pl.ds(0, half), pl.ds(half, half)

    def row(self, k):
        return self.slabs.at[lax.rem(self.c + k, SIDE)]

    def send_far(self):
        self.next_far = self.copies.start(self.row(2).at[self.top], self.far.at[0], self.next)
        self.prev_far = self.copies.start(self.row(2).at[self.low], self.far.at[1], self.prev)

    def send_next(self):
        self.next_near = self.copies.start(
            self.row(1).at[self.low], self.near.at[0, self.low], self.next
        )

    def send_prev(self):
        self.prev_near = self.copies.start(
            self.row(3).at[self.top], self.near.at[1, self.top], self.prev
        )

    def pass_on(self):
        self.next_far.wait_recv()
        add_into(self.row(1).at[self.top], self.far[0])
        self.next_sum = self.copies.start(
            self.row(1).at[self.top], self.near.at[0, self.top], self.next
        )
        self.prev_far.wait_recv()
        add_into(self.row(3).at[self.low], self.far[1])
        self.prev_sum = self.copies.start(
            self.row(3).at[self.low], self.near.at[1, self.low], self.prev
        )

    def finish(self, own):
        for copy in (self.next_near, self.prev_near, self.next_sum, self.prev_sum):
            copy.wait_recv()
        return own + self.near[0].astype(jnp.float32) + self.near[1].astype(jnp.float32)


class RingGather:
    def __init__(self, copies, slabs, index, to):
        self.copies, self.slabs, self.c = copies, slabs, index
        self.next, self.prev = to(index + 1), to(index + 3)
        half = ROWS // 2
        self.top, self.low = pl.ds(0, half), pl.ds(half, half)

    def go(self, k, part, where):
        piece = self.slabs.at[lax.rem(self.c + k, SIDE)].at[part]
        return self.copies.start(piece, piece, where)

    def run(self):
        first = (self.go(0, self.top, self.next), self.go(0, self.low, self.prev))
        second = (self.go(0, self.low, self.next), self.go(0, self.top, self.prev))
        first[0].wait_recv()
        far = [self.go(3, self.top, self.next)]
        first[1].wait_recv()
        far.append(self.go(1, self.low, self.prev))
        for copy in (*second, *far):
            copy.wait_recv()


def quarter(width, plane, planes):
    size = width // planes
    return pl.ds(pl.multiple_of(lax.rem(plane, planes) * size, 128), size)


class Levels:
    def __init__(self, copies, rep, reps):
        self.copies, self.plane, self.planes = copies, lax.div(rep, 2), reps // 2
        self.above, self.below = (
            {"rep": lax.rem(rep + 2 * k, reps)} for k in (1, self.planes - 1)
        )
        self.sent = []

    def share(self, array, k):
        return array.at[:, quarter(array.shape[1], self.plane + k, self.planes)]

    def spread(self, array):
        piece = self.share(array, 0)
        self.sent.append(
            (
                array,
                self.copies.start(piece, piece, self.above),
                self.copies.start(piece, piece, self.below),
            )
        )

    def pass_on(self):
        self.far = []
        for array, from_below, from_above in self.sent:
            half = array.shape[0] // 2
            from_below.wait_recv()
            piece = self.share(array, self.planes - 1).at[pl.ds(0, half)]
            self.far.append(self.copies.start(piece, piece, self.above))
            from_above.wait_recv()
            piece = self.share(array, 1).at[pl.ds(half, half)]
            self.far.append(self.copies.start(piece, piece, self.below))

    def finish(self):
        for copy in self.far:
            copy.wait_recv()


class RowRing:
    def __init__(self, copies, shards, own, columns, index, to):
        self.copies, self.shards, self.columns, self.c = copies, shards, columns, index
        self.next, self.prev = to(index + 1), to(index + 3)
        half = own.shape[0] // 2
        self.parts = pl.ds(0, half), pl.ds(half, half)
        top, low = (own.at[part, columns] for part in self.parts)
        self.first = (self.go(0, 0, self.next, top), self.go(0, 1, self.prev, low))
        self.second = (self.go(0, 1, self.next, low), self.go(0, 0, self.prev, top))

    def go(self, k, part, where, source=None):
        piece = self.shards.at[lax.rem(self.c + k, SIDE), self.parts[part], self.columns]
        return self.copies.start(piece if source is None else source, piece, where)

    def pass_on(self):
        self.first[0].wait_recv()
        self.far = [self.go(3, 0, self.next)]
        self.first[1].wait_recv()
        self.far.append(self.go(1, 1, self.prev))

    def finish(self):
        for copy in (*self.second, *self.far):
            copy.wait_recv()


def add_into(ref, value):
    ref[...] = (ref[...].astype(jnp.float32) + value.astype(jnp.float32)).astype(ref.dtype)


class Scatter:
    def __init__(self, copies, parts, far, near, row, row_far, row_near):
        y, x, a, b, self.device = place()
        self.a, self.b = a, b
        self.copies, self.parts, self.far, self.near = copies, parts, far, near
        self.ring = RingSum(
            copies, row, row_far, row_near, b, lambda j: tensor(self.device(a, j))
        )
        self.above, self.below = tensor(self.device(a + 1, b)), tensor(self.device(a + 3, b))
        self.ups, self.downs = (b + 2, b + 1), (b + 3, b)

    def part(self, i, j):
        return self.parts.at[lax.rem(i, SIDE), lax.rem(j, SIDE)]

    def landing(self, side, j):
        return self.near.at[side, lax.rem(j, SIDE)]

    def send_far(self):
        self.far_up, self.far_down = [], []
        for k in range(2):
            self.far_up.append(
                self.copies.start(self.part(self.a + 2, self.ups[k]), self.far.at[0, k], self.above)
            )
            self.far_down.append(
                self.copies.start(
                    self.part(self.a + 2, self.downs[k]), self.far.at[1, k], self.below
                )
            )

    def send_near(self):
        self.near_up, self.near_down = [], []
        for k in range(2):
            self.near_up.append(
                self.copies.start(
                    self.part(self.a + 1, self.downs[k]),
                    self.landing(0, self.downs[k]),
                    self.above,
                )
            )
            self.near_down.append(
                self.copies.start(
                    self.part(self.a + 3, self.ups[k]), self.landing(1, self.ups[k]), self.below
                )
            )

    def pass_on(self):
        self.sum_up, self.sum_down = [], []
        for k in range(2):
            self.far_up[k].wait_recv()
            add_into(self.part(self.a + 1, self.ups[k]), self.far[0, k])
            self.sum_up.append(
                self.copies.start(
                    self.part(self.a + 1, self.ups[k]), self.landing(0, self.ups[k]), self.above
                )
            )
            self.far_down[k].wait_recv()
            add_into(self.part(self.a + 3, self.downs[k]), self.far[1, k])
            self.sum_down.append(
                self.copies.start(
                    self.part(self.a + 3, self.downs[k]),
                    self.landing(1, self.downs[k]),
                    self.below,
                )
            )

    def total(self, j):
        at = lax.rem(j, SIDE)
        return (
            self.parts[self.a, at].astype(jnp.float32)
            + self.near[0, at].astype(jnp.float32)
            + self.near[1, at].astype(jnp.float32)
        )

    def finish(self):
        ring, b = self.ring, self.b
        self.sum_up[0].wait_recv()
        self.near_down[0].wait_recv()
        ring.row(2)[...] = self.total(b + 2).astype(jnp.bfloat16)
        ring.send_far()
        self.near_up[0].wait_recv()
        self.sum_down[0].wait_recv()
        ring.row(3)[...] = self.total(b + 3).astype(jnp.bfloat16)
        ring.send_prev()
        self.sum_up[1].wait_recv()
        self.near_down[1].wait_recv()
        ring.row(1)[...] = self.total(b + 1).astype(jnp.bfloat16)
        ring.send_next()
        ring.pass_on()
        self.near_up[1].wait_recv()
        self.sum_down[1].wait_recv()
        return ring.finish(self.total(b))


class SmallSum:
    def __init__(self, copies, over_x, over_y):
        t = lax.axis_index("tensor")
        self.y, self.x = lax.div(t, SIDE), lax.rem(t, SIDE)
        self.copies, self.over_x, self.over_y = copies, over_x, over_y

    def begin(self, value):
        self.over_x[self.x] = value.astype(jnp.bfloat16)
        mine = self.over_x.at[self.x]
        self.sent = [
            self.copies.start(
                mine, mine, tensor(SIDE * self.y + lax.rem(self.x + k, SIDE))
            )
            for k in (1, 2, 3)
        ]

    def middle(self):
        for copy in self.sent:
            copy.wait_recv()
        self.over_y[self.y] = sum(
            self.over_x[k].astype(jnp.float32) for k in range(SIDE)
        ).astype(jnp.bfloat16)
        mine = self.over_y.at[self.y]
        self.sent = [
            self.copies.start(
                mine, mine, tensor(SIDE * lax.rem(self.y + k, SIDE) + self.x)
            )
            for k in (1, 2, 3)
        ]

    def finish(self):
        for copy in self.sent:
            copy.wait_recv()
        return sum(self.over_y[k].astype(jnp.float32) for k in range(SIDE))


def layer_norm(values, gain_row, shift_row):
    average = jnp.mean(values, axis=-1, keepdims=True)
    centred = values - average
    spread = jnp.mean(centred * centred, axis=-1, keepdims=True)
    return centred * lax.rsqrt(spread + 1e-05) * gain_row + shift_row


def project_kernel(
    reps,
    scale,
    len_ref,
    dec_ref,
    x_hbm,
    w_hbm,
    cache_hbm,
    w_out_hbm,
    out_ref,
    attn_ref,
    w_row_hbm,
    rows,
    dec_rows,
    w_ref,
    cache_ref,
    states,
    local_sem,
    send_sem,
    recv_sem,
):
    y, x, a, b, device = place()
    load_x = pltpu.make_async_copy(x_hbm, rows.at[device(a, b)], local_sem.at[2])
    load_x.start()
    load_w = pltpu.make_async_copy(w_hbm, w_ref, local_sem.at[0])
    load_w.start()
    load_cache = pltpu.make_async_copy(cache_hbm, cache_ref, local_sem.at[1])
    load_cache.start()
    keep_w = pltpu.make_async_copy(w_out_hbm, w_row_hbm.at[b], local_sem.at[3])
    keep_w.start()
    rep = lax.axis_index("rep")
    copies = Copies(send_sem, recv_sem)
    greet(
        [device(a, b + k) for k in (1, 2, 3)] + [device(a + 1, b), device(a + 3, b)],
        [lax.rem(rep + k, reps) for k in range(1, reps)],
    )
    gather = Gather(copies, lambda i, j: rows.at[device(i, j)])
    mine = quarter(w_out_hbm.shape[1], lax.div(rep, 2), reps // 2)
    shards = [
        copies.start(
            w_out_hbm.at[:, mine], w_row_hbm.at[b, :, mine], tensor(device(a, b + k))
        )
        for k in (1, 3, 2)
    ]
    dec_rows[...] = jnp.zeros_like(dec_rows)
    dec_rows[: dec_ref.shape[0]] = dec_ref[...]
    load_x.wait()
    levels = Levels(copies, rep, reps)
    for k, shard in zip((1, 3, 2), shards):
        shard.wait_recv()
        levels.spread(w_row_hbm.at[lax.rem(b - k + SIDE, SIDE)])
    gather.begin()
    load_w.wait()
    dec = (
        lax.dot_general(w_ref[...], dec_rows[...], NT, preferred_element_type=jnp.float32)
        .astype(jnp.bfloat16)
        .astype(jnp.float32)
    )
    gather.first()
    load_cache.wait()
    hd = cache_ref.shape[2] // 2
    heads = cache_ref.shape[1]
    span = cache_ref.shape[3]
    lanes = dec.shape[1]
    lane = lax.broadcasted_iota(jnp.int32, (1, lanes), 1)
    position = rep * span + lax.broadcasted_iota(jnp.int32, (1, span), 1)

    def request(r, state):
        pick = lane == r
        column = jnp.sum(jnp.where(pick, dec, 0.0), axis=1, keepdims=True)
        valid = position < len_ref[r]
        out = []
        for h in range(heads):
            query = column[3 * hd * h : 3 * hd * h + hd]
            key = cache_ref[r, h, :hd].astype(jnp.float32)
            value = cache_ref[r, h, hd:].astype(jnp.float32)
            score = jnp.sum(key * query, axis=0, keepdims=True) * scale
            score = jnp.where(valid, score, NEG)
            high = jnp.max(score, axis=1, keepdims=True)
            weight = jnp.where(valid, jnp.exp(score - high), 0.0)
            total = jnp.sum(weight, axis=1, keepdims=True)
            mixed = jnp.sum(value * weight, axis=1, keepdims=True)
            highs, totals, mixes = state[h]
            out.append(
                (
                    jnp.where(pick, high, highs),
                    jnp.where(pick, total, totals),
                    jnp.where(pick, mixed, mixes),
                )
            )
        return tuple(out)

    empty = tuple(
        (
            jnp.full((1, lanes), NEG, jnp.float32),
            jnp.zeros((1, lanes), jnp.float32),
            jnp.zeros((hd, lanes), jnp.float32),
        )
        for _ in range(heads)
    )
    state = lax.fori_loop(0, cache_ref.shape[0], request, empty)
    for h in range(heads):
        states[rep, h, :hd] = state[h][2]
        states[rep, h, hd : hd + 8] = jnp.broadcast_to(state[h][0], (8, lanes))
        states[rep, h, hd + 8 : hd + 16] = jnp.broadcast_to(state[h][1], (8, lanes))
    sent = [
        copies.start(states.at[rep], states.at[rep], {"rep": lax.rem(rep + k, reps)})
        for k in range(1, reps)
    ]
    levels.pass_on()
    gather.middle()
    for copy in sent:
        copy.wait_recv()
    for h in range(heads):
        base = 3 * hd * h
        query, key, value = (dec[base + hd * k : base + hd * (k + 1)] for k in range(3))
        own = jnp.sum(query * key, axis=0, keepdims=True) * scale
        highest = own
        for k in range(reps):
            highest = jnp.maximum(highest, states[k, h, hd : hd + 1])
        own_weight = jnp.exp(own - highest)
        total, mixed = own_weight, own_weight * value
        for k in range(reps):
            factor = jnp.exp(states[k, h, hd : hd + 1] - highest)
            total = total + factor * states[k, h, hd + 8 : hd + 9]
            mixed = mixed + factor * states[k, h, :hd]
        attn_ref[:, hd * h : hd * (h + 1)] = (mixed / total).T[: attn_ref.shape[0]].astype(
            attn_ref.dtype
        )
    gather.last()

    @pl.loop(0, SIDE)
    def _(i):
        block = rows[pl.ds(SIDE * i, SIDE)].reshape(SIDE * ROWS, rows.shape[2])
        out_ref[:, pl.ds(pl.multiple_of(i * SIDE * ROWS, SIDE * ROWS), SIDE * ROWS)] = (
            lax.dot_general(w_ref[...], block, NT, preferred_element_type=jnp.float32).astype(
                out_ref.dtype
            )
        )

    levels.finish()
    keep_w.wait()
    copies.drain()


def attend(head, scale, offset, qkv_ref, kv_ref, seg_row, out_ref, q_ref, state):
    hd = q_ref.shape[1]
    span = seg_row.shape[1]
    block, key_block = 256, 1024
    early = span // 2 // block
    factor = scale * LOG2E
    q_ref[...] = qkv_ref[head, 0].astype(jnp.float32).T.astype(jnp.bfloat16)
    seg_keys = seg_row[...].astype(jnp.float32)
    seg_rows = jnp.broadcast_to(seg_keys, (8, span)).T[:, :1]
    states = [state[3 * i : 3 * i + 3] for i in range(early)]

    def rows(i):
        return slice(i * block, (i + 1) * block)

    def mix(weight, values):
        return lax.dot_general(
            weight.astype(jnp.bfloat16), values, NT, preferred_element_type=jnp.float32
        )

    for m_ref, l_ref, acc_ref in states:
        m_ref[...] = jnp.full(m_ref.shape, NEG, jnp.float32)
        l_ref[...] = jnp.zeros(l_ref.shape, jnp.float32)
        acc_ref[...] = jnp.zeros(acc_ref.shape, jnp.float32)

    @pl.loop(0, kv_ref.shape[2] // key_block)
    def _(j):
        at = pl.multiple_of(j * key_block, key_block)
        keys = kv_ref[head, :hd, pl.ds(at, key_block)]
        values = kv_ref[head, hd:, pl.ds(at, key_block)]
        seen = at + lax.broadcasted_iota(jnp.int32, (1, key_block), 1) < offset
        scores = [
            jnp.dot(q_ref[rows(i)], keys, preferred_element_type=jnp.float32)
            for i in range(early)
        ]
        for score, (m_ref, l_ref, acc_ref) in zip(scores, states):
            score = jnp.where(seen, score, NEG)
            high = jnp.maximum(m_ref[...], jnp.max(score, axis=1, keepdims=True))
            decay = jnp.exp2((m_ref[...] - high) * factor)
            weight = jnp.exp2((score - high) * factor)
            m_ref[...] = high
            l_ref[...] = l_ref[...] * decay + jnp.sum(weight, axis=1, keepdims=True)
            acc_ref[...] = acc_ref[...] * decay + mix(weight, values)

    for i in range(span // block):
        low = max(0, (i - early) * block)
        high = (i + 1) * block
        seg_q = seg_rows[rows(i)]
        score = jnp.dot(
            q_ref[rows(i)], qkv_ref[head, 1, :, low:high], preferred_element_type=jnp.float32
        )
        shape = (block, high - low)
        query_at = i * block + lax.broadcasted_iota(jnp.int32, shape, 0)
        key_at = low + lax.broadcasted_iota(jnp.int32, shape, 1)
        seen = (seg_keys[:, low:high] == seg_q) & (key_at <= query_at)
        score = jnp.where(seen, score, NEG)
        values = qkv_ref[head, 2, :, low:high]
        peak = jnp.max(score, axis=1, keepdims=True)
        if i < early:
            m_ref, l_ref, acc_ref = states[i]
            keep = (seg_q == 0) & (offset > 0)
            before = jnp.where(keep, m_ref[...], NEG)
            peak = jnp.maximum(peak, before)
            decay = jnp.where(keep, jnp.exp2((before - peak) * factor), 0.0)
        weight = jnp.exp2((score - peak) * factor)
        total = jnp.sum(weight, axis=1, keepdims=True)
        mixed = mix(weight, values)
        if i < early:
            total = total + l_ref[...] * decay
            mixed = mixed + acc_ref[...] * decay
        out_ref[rows(i), head * hd : (head + 1) * hd] = (mixed / total).astype(out_ref.dtype)


def tail_kernel(
    scale,
    reps,
    offset_ref,
    seg_row,
    dec_attn_ref,
    x_dec_ref,
    up_bias_ref,
    biases_ref,
    gains_ref,
    shifts_ref,
    qkv_hbm,
    kv_hbm,
    x_hbm,
    w_row_hbm,
    w_up_hbm,
    w_down_hbm,
    w_next_hbm,
    result_hbm,
    out_ref,
    dec_out_ref,
    dec_next_ref,
    qkv_ref,
    kv_ref,
    x_ref,
    w_row_ref,
    w_up_ref,
    w_down_ref,
    w_next_ref,
    attn_ref,
    heads_ref,
    columns_ref,
    result_ref,
    slabs,
    parts,
    far,
    near,
    row,
    row_far,
    row_near,
    over_x,
    over_y,
    q_ref,
    m0_ref,
    l0_ref,
    acc0_ref,
    m1_ref,
    l1_ref,
    acc1_ref,
    local_sem,
    send_sem,
    recv_sem,
):
    y, x, a, b, device = place()
    loads = []
    for k, (source, target) in enumerate(
        (
            (qkv_hbm, qkv_ref),
            (kv_hbm, kv_ref),
            (w_row_hbm, w_row_ref),
            (x_hbm, x_ref),
            (w_next_hbm, w_next_ref.at[b]),
            (w_up_hbm, w_up_ref),
            (w_down_hbm, w_down_ref),
        )
    ):
        loads.append(pltpu.make_async_copy(source, target, local_sem.at[k]))
        loads[-1].start()
    load_qkv, load_kv, load_row, load_x, load_next, load_up, load_down = loads
    copies = Copies(send_sem, recv_sem)
    rep = lax.axis_index("rep")
    plane, planes = lax.div(rep, 2), reps // 2
    columns, width = w_next_hbm.shape

    greet(
        [SIDE * y + lax.rem(x + k, SIDE) for k in (1, 2, 3)]
        + [SIDE * lax.rem(y + k, SIDE) + x for k in (1, 2, 3)],
        [lax.rem(rep + 2 * k, reps) for k in (1, planes - 1)],
    )
    chunk = (SIDE, ROWS, width)
    load_row.wait()
    dec_sum = SmallSum(copies, over_x.at[0], over_y.at[0])
    dec_sum.begin(
        jnp.dot(dec_attn_ref[...], w_row_ref[b], preferred_element_type=jnp.float32)
    )
    shards = RowRing(
        copies,
        w_next_ref,
        w_next_hbm,
        quarter(width, plane, planes),
        b,
        lambda j: tensor(device(a, j)),
    )
    attn_ref[...] = jnp.zeros_like(attn_ref)
    result_ref[...] = jnp.zeros_like(result_ref)
    load_qkv.wait()
    load_kv.wait()
    state = (m0_ref, l0_ref, acc0_ref, m1_ref, l1_ref, acc1_ref)
    offset = offset_ref[0]
    heads = qkv_ref.shape[0]
    for head in range(heads):
        attend(head, scale, offset, qkv_ref, kv_ref, seg_row, attn_ref, q_ref, state)
        if head == 0:
            dec_sum.middle()
            shards.pass_on()

    def tokens(i, j):
        return attn_ref.at[pl.ds(pl.multiple_of(device(i, j) * ROWS, ROWS), ROWS)]

    swaps = [
        copies.start(tokens(i, b + k), heads_ref.at[b, i], tensor(device(a, b + k)))
        for k in (2, 1, 3)
        for i in range(SIDE)
    ]
    for i in range(SIDE):
        heads_ref[b, i] = tokens(i, b)[...]
    for swap in swaps:
        swap.wait_recv()
    ring = RingSum(
        copies, row.at[0], row_far.at[0], row_near.at[0], a, lambda i: tensor(device(i, b))
    )
    depth = w_row_ref.shape[1]
    step = width // 5
    for n in range(0, width, step):
        total = sum(
            jnp.dot(
                heads_ref[j].reshape(SIDE * ROWS, heads_ref.shape[3])[:, :depth],
                w_row_ref[j, :, n : n + step],
                preferred_element_type=jnp.float32,
            )
            for j in range(SIDE)
        )
        row[0, :, :, n : n + step] = total.astype(jnp.bfloat16).reshape(SIDE, ROWS, step)
    ring.send_far()
    ring.send_next()
    ring.send_prev()
    ring.pass_on()
    shards.finish()
    levels = Levels(copies, rep, reps)
    for k in (1, 2, 3):
        levels.spread(w_next_ref.at[lax.rem(b + k, SIDE)])
    dec_first = layer_norm(
        x_dec_ref[...].astype(jnp.float32) + dec_sum.finish() + biases_ref[0:1],
        gains_ref[0:1],
        shifts_ref[0:1],
    ).astype(jnp.bfloat16)
    own = row[0, a].astype(jnp.float32)
    load_x.wait()
    attn_sum = ring.finish(own)
    first = layer_norm(
        x_ref[...].astype(jnp.float32) + attn_sum + biases_ref[0:1], gains_ref[0:1], shifts_ref[0:1]
    ).astype(jnp.bfloat16)

    def slab(i, j):
        return slabs.at[lax.rem(i, SIDE), lax.rem(j, SIDE)]

    slab(a, b)[...] = first
    gather = Gather(copies, slab)
    gather.begin()
    load_up.wait()
    load_down.wait()

    def mlp(value):
        inner = jnp.dot(value, w_up_ref[...], preferred_element_type=jnp.float32)
        inner = inner + up_bias_ref[...][None, :]
        hidden = (0.5 * inner * (1.0 + lax.erf(inner * 0.7071067811865476))).astype(jnp.bfloat16)
        return jnp.dot(hidden, w_down_ref[...], preferred_element_type=jnp.float32)

    dec_sum = SmallSum(copies, over_x.at[1], over_y.at[1])
    dec_sum.begin(mlp(dec_first))

    def mlp_share(i):
        at = lax.rem(i, SIDE)
        parts[at] = (
            mlp(slabs[at].reshape(SIDE * ROWS, width)).astype(jnp.bfloat16).reshape(chunk)
        )

    scatter = Scatter(copies, parts, far, near, row.at[1], row_far.at[1], row_near.at[1])
    gather.first()
    mlp_share(a)
    dec_sum.middle()
    gather.middle()
    mlp_share(a + 1)
    mlp_share(a + 3)
    scatter.send_near()
    gather.last()
    mlp_share(a + 2)
    scatter.send_far()
    scatter.pass_on()
    levels.pass_on()
    dec_out = layer_norm(
        dec_first.astype(jnp.float32) + dec_sum.finish() + biases_ref[1:2],
        gains_ref[1:2],
        shifts_ref[1:2],
    ).astype(jnp.bfloat16)
    dec_out_ref[...] = dec_out
    load_next.wait()
    dec_next_ref[...] = lax.dot_general(
        dec_out, w_next_ref[b], NT, preferred_element_type=jnp.float32
    ).astype(jnp.bfloat16)
    mlp_sum = scatter.finish()
    second = layer_norm(
        first.astype(jnp.float32) + mlp_sum + biases_ref[1:2], gains_ref[1:2], shifts_ref[1:2]
    ).astype(jnp.bfloat16)
    out_ref[...] = second
    columns_ref[a] = second
    RingGather(copies, columns_ref, a, lambda i: tensor(device(i, b))).run()
    levels.finish()
    keeps = []
    for k in (2, 1, 3, 0):
        j = lax.rem(b + k, SIDE)
        result_ref[j, :, :, :columns] = (
            lax.dot_general(
                columns_ref[...].reshape(SIDE * ROWS, width),
                w_next_ref[j],
                NT,
                preferred_element_type=jnp.float32,
            )
            .astype(jnp.bfloat16)
            .reshape(SIDE, ROWS, columns)
        )
        for i in range(SIDE):
            source, target = result_ref.at[j, i], result_hbm.at[device(i, b)]
            if k:
                keeps.append(copies.start(source, target, tensor(device(a, j))))
            else:
                local = pltpu.make_async_copy(source, target, local_sem.at[i])
                local.start()
                loads.append(local)
    for copy in keeps:
        copy.wait_recv()
    for local in loads[-SIDE:]:
        local.wait()
    copies.drain()


def layout_kernel(
    result_ref, own_ref, dec_ref, dec_result_ref, next_ref, out_ref, dec_out_ref, dec_next_ref
):
    columns, lanes = next_ref.shape[0], result_ref.shape[2]
    same = lax.broadcasted_iota(jnp.int32, (columns, lanes), 0) == lax.broadcasted_iota(
        jnp.int32, (columns, lanes), 1
    )
    next_ref[...] = lax.dot_general(
        same.astype(jnp.float32).astype(jnp.bfloat16),
        result_ref[...].reshape(SIDE * ROWS, lanes),
        NT,
        preferred_element_type=jnp.float32,
    ).astype(next_ref.dtype)

    @pl.when(pl.program_id(0) == 0)
    def _():
        out_ref[...] = own_ref[...]
        dec_out_ref[...] = dec_ref[...]
        dec_next_ref[...] = dec_result_ref[...]


def per_device(
    reps,
    x_pre,
    x_dec,
    prefix_kv,
    cache_kv,
    dec_len,
    offsets,
    segments,
    w_qkv,
    w_out,
    w_up,
    up_bias,
    w_down,
    biases,
    gains,
    shifts,
    w_next,
):
    heads = prefix_kv.shape[2]
    hd = prefix_kv.shape[3] // 2
    span = segments.shape[1]
    width = x_pre.shape[1]
    decodes = x_dec.shape[0]
    columns = w_qkv.shape[1]
    units = w_up.shape[1]
    scale = hd ** (-0.5)
    bf16, f32 = jnp.bfloat16, jnp.float32
    shape = jax.ShapeDtypeStruct
    whole = pl.BlockSpec(memory_space=VMEM)
    scalars = pl.BlockSpec(memory_space=pltpu.SMEM)
    anywhere = pl.BlockSpec(memory_space=pltpu.HBM)
    group = SIDE * SIDE

    cache_t = cache_kv.transpose(0, 2, 3, 1)
    n_copies = 16 + reps - 1 + (SIDE - 1) * 5
    qkv_t, dec_attn, w_row = pl.pallas_call(
        functools.partial(project_kernel, reps, scale),
        out_shape=(
            shape((columns, span), bf16),
            shape((decodes, heads * hd), bf16),
            shape((SIDE,) + w_out.shape, bf16),
        ),
        in_specs=[scalars, whole] + [anywhere] * 4,
        out_specs=(whole, whole, anywhere),
        scratch_shapes=[
            VMEM((group, ROWS, width), bf16),
            VMEM((128, width), bf16),
            VMEM((columns, width), bf16),
            VMEM(cache_t.shape, bf16),
            VMEM((reps, heads, hd + 16, 128), f32),
            pltpu.SemaphoreType.DMA((4,)),
            pltpu.SemaphoreType.DMA((n_copies,)),
            pltpu.SemaphoreType.DMA((n_copies,)),
        ],
        compiler_params=pltpu.CompilerParams(
            collective_id=0, has_side_effects=True, vmem_limit_bytes=62 << 20
        ),
        name="project",
    )(dec_len, x_dec, x_pre, w_qkv.T, cache_t, w_out)

    n_copies = 100
    lanes = 512
    result, own, dec_own, dec_result = pl.pallas_call(
        functools.partial(tail_kernel, scale, reps),
        out_shape=(
            shape((group, ROWS, lanes), bf16),
            shape((ROWS, width), bf16),
            shape((decodes, width), bf16),
            shape((decodes, columns), bf16),
        ),
        in_specs=[scalars] + [whole] * 7 + [anywhere] * 7,
        out_specs=(anywhere, whole, whole, whole),
        scratch_shapes=[
            VMEM((heads, 3, hd, span), bf16),
            VMEM((heads, 2 * hd, prefix_kv.shape[1]), bf16),
            VMEM((ROWS, width), bf16),
            VMEM((SIDE,) + w_out.shape, bf16),
            VMEM((width, units), bf16),
            VMEM((units, width), bf16),
            VMEM((SIDE, columns, width), bf16),
            VMEM((span, 256), bf16),
            VMEM((SIDE, SIDE, ROWS, 256), bf16),
            VMEM((SIDE, ROWS, width), bf16),
            VMEM((SIDE, SIDE, ROWS, lanes), bf16),
            VMEM((SIDE, SIDE, ROWS, width), bf16),
            VMEM((SIDE, SIDE, ROWS, width), bf16),
            VMEM((2, 2, ROWS, width), bf16),
            VMEM((2, SIDE, ROWS, width), bf16),
            VMEM((2, SIDE, ROWS, width), bf16),
            VMEM((2, 2, ROWS // 2, width), bf16),
            VMEM((2, 2, ROWS, width), bf16),
            VMEM((2, SIDE, decodes, width), bf16),
            VMEM((2, SIDE, decodes, width), bf16),
            VMEM((span, hd), bf16),
            *([VMEM((256, 1), f32), VMEM((256, 1), f32), VMEM((256, hd), f32)] * 2),
            pltpu.SemaphoreType.DMA((8,)),
            pltpu.SemaphoreType.DMA((n_copies,)),
            pltpu.SemaphoreType.DMA((n_copies,)),
        ],
        compiler_params=pltpu.CompilerParams(
            collective_id=1, has_side_effects=True, vmem_limit_bytes=62 << 20
        ),
        name="tail",
    )(
        offsets,
        segments,
        dec_attn,
        x_dec,
        up_bias,
        biases,
        gains,
        shifts,
        qkv_t.reshape(heads, 3, hd, span),
        prefix_kv[0].transpose(1, 2, 0),
        x_pre,
        w_row,
        w_up,
        w_down,
        w_next.T,
    )

    next_t, layer_out, dec_out, dec_next = pl.pallas_call(
        layout_kernel,
        grid=(SIDE,),
        out_shape=(
            shape((columns, span), bf16),
            shape((ROWS, width), bf16),
            shape((decodes, width), bf16),
            shape((decodes, columns), bf16),
        ),
        in_specs=[
            pl.BlockSpec((SIDE, ROWS, lanes), lambda i: (i, 0, 0)),
            pl.BlockSpec((ROWS, width), lambda i: (0, 0)),
            pl.BlockSpec((decodes, width), lambda i: (0, 0)),
            pl.BlockSpec((decodes, columns), lambda i: (0, 0)),
        ],
        out_specs=(
            pl.BlockSpec((columns, SIDE * ROWS), lambda i: (0, i)),
            pl.BlockSpec((ROWS, width), lambda i: (0, 0)),
            pl.BlockSpec((decodes, width), lambda i: (0, 0)),
            pl.BlockSpec((decodes, columns), lambda i: (0, 0)),
        ),
        compiler_params=pltpu.CompilerParams(
            dimension_semantics=("arbitrary",), vmem_limit_bytes=62 << 20
        ),
        name="layout",
    )(result, own, dec_own, dec_result)
    return layer_out, next_t.T, dec_out, dec_next


def solution(mesh):
    placed = (
        P(("rep", "tensor"), None),
        P(),
        P("rep", None, "tensor", None),
        P(None, "rep", "tensor", None),
        P(),
        P("rep"),
        P("rep", None),
        P(None, "tensor"),
        P("tensor", None),
        P(None, "tensor"),
        P("tensor"),
        P("tensor", None),
        P(),
        P(),
        P(),
        P(None, "tensor"),
    )
    return jax.shard_map(
        functools.partial(per_device, mesh.shape["rep"]),
        mesh=mesh,
        in_specs=placed,
        out_specs=(P(("rep", "tensor"), None), P("rep", "tensor"), P(), P(None, "tensor")),
        check_vma=False,
    )
```

```python
import functools

import jax
import jax.numpy as jnp
from jax import lax
from jax.experimental import pallas as pl
from jax.experimental.pallas import tpu as pltpu
from jax.sharding import PartitionSpec as P

MESH = pl.DeviceIdType.MESH
NEG = -1e30
LOG2E = 1.4426950408889634
SIDE = 4
ROWS = 64
VMEM = pltpu.VMEM
NT = (((1,), (1,)), ((), ()))


def place():
    t = lax.axis_index("tensor")
    core = lax.rem(lax.axis_index("rep"), 2)
    y, x = lax.div(t, SIDE), lax.rem(t, SIDE)
    major = y * (1 - core) + x * core
    minor = x * (1 - core) + y * core
    step_major, step_minor = SIDE - (SIDE - 1) * core, 1 + (SIDE - 1) * core

    def device(i, j):
        return lax.rem(i, SIDE) * step_major + lax.rem(j, SIDE) * step_minor

    return y, x, major, minor, device


class Copies:
    def __init__(self, send, recv):
        self.send, self.recv, self.used, self.all = send, recv, 0, []

    def start(self, src, dst, where):
        copy = pltpu.make_async_remote_copy(
            src_ref=src,
            dst_ref=dst,
            send_sem=self.send.at[self.used],
            recv_sem=self.recv.at[self.used],
            device_id=where,
            device_id_type=MESH,
        )
        copy.start()
        self.used += 1
        self.all.append(copy)
        return copy

    def drain(self):
        for copy in self.all:
            copy.wait_send()


def tensor(t):
    return {"tensor": t}


def greet(tensor_peers, rep_peers=()):
    barrier = pltpu.get_barrier_semaphore()
    for t in tensor_peers:
        pl.semaphore_signal(barrier, inc=1, device_id=tensor(t), device_id_type=MESH)
    for r in rep_peers:
        pl.semaphore_signal(barrier, inc=1, device_id={"rep": r}, device_id_type=MESH)
    pl.semaphore_wait(barrier, len(tensor_peers) + len(rep_peers))


class Gather:
    def __init__(self, copies, at, own=None):
        y, x, self.a, self.b, self.device = place()
        self.copies, self.at, self.own = copies, at, own

    def go(self, i, j, ti, tj):
        return self.copies.start(self.at(i, j), self.at(i, j), tensor(self.device(ti, tj)))

    def begin(self):
        a, b = self.a, self.b
        own = self.at(a, b) if self.own is None else self.own
        self.right, self.left, up, down = (
            self.copies.start(own, self.at(a, b), tensor(self.device(i, j)))
            for i, j in ((a, b + 1), (a, b + 3), (a + 1, b), (a + 3, b))
        )
        self.up, self.down = [up], [down]

    def spread(self, j):
        a, b = self.a, self.b
        self.up.append(self.go(a, j, a + 1, b))
        self.down.append(self.go(a, j, a + 3, b))

    def half(self, i, j, part):
        return self.at(i, j).at[pl.ds(part * (ROWS // 2), ROWS // 2)]

    def first(self):
        a, b = self.a, self.b
        self.right.wait_recv()
        one = self.half(a, b + 3, 0)
        far_one = self.copies.start(one, one, tensor(self.device(a, b + 1)))
        self.spread(b + 3)
        self.left.wait_recv()
        two = self.half(a, b + 1, 1)
        far_two = self.copies.start(two, two, tensor(self.device(a, b + 3)))
        self.spread(b + 1)
        far_one.wait_recv()
        far_two.wait_recv()
        self.spread(b + 2)

    def middle(self):
        a, b = self.a, self.b
        self.up[0].wait_recv()
        self.far = [self.go(a + 3, b, a + 1, b)]
        self.down[1].wait_recv()
        self.far.append(self.go(a + 1, b + 3, a + 3, b))
        self.down[2].wait_recv()
        self.far.append(self.go(a + 1, b + 1, a + 3, b))
        self.up[3].wait_recv()
        self.far.append(self.go(a + 3, b + 2, a + 1, b))
        self.up[1].wait_recv()
        self.up[2].wait_recv()
        self.down[0].wait_recv()
        self.down[3].wait_recv()

    def last(self):
        for copy in self.far:
            copy.wait_recv()


class RingSum:
    def __init__(self, copies, row, far, near, index, to):
        self.copies, self.slabs, self.far, self.near = copies, row, far, near
        self.c, self.next, self.prev = index, to(index + 1), to(index + 3)
        half = ROWS // 2
        self.top, self.low = pl.ds(0, half), pl.ds(half, half)

    def row(self, k):
        return self.slabs.at[lax.rem(self.c + k, SIDE)]

    def send_far(self):
        self.next_far = self.copies.start(self.row(2).at[self.top], self.far.at[0], self.next)
        self.prev_far = self.copies.start(self.row(2).at[self.low], self.far.at[1], self.prev)

    def send_next(self):
        self.next_near = self.copies.start(
            self.row(1).at[self.low], self.near.at[0, self.low], self.next
        )

    def send_prev(self):
        self.prev_near = self.copies.start(
            self.row(3).at[self.top], self.near.at[1, self.top], self.prev
        )

    def pass_on(self):
        self.next_far.wait_recv()
        add_into(self.row(1).at[self.top], self.far[0])
        self.next_sum = self.copies.start(
            self.row(1).at[self.top], self.near.at[0, self.top], self.next
        )
        self.prev_far.wait_recv()
        add_into(self.row(3).at[self.low], self.far[1])
        self.prev_sum = self.copies.start(
            self.row(3).at[self.low], self.near.at[1, self.low], self.prev
        )

    def finish(self, own):
        for copy in (self.next_near, self.prev_near, self.next_sum, self.prev_sum):
            copy.wait_recv()
        return own + self.near[0].astype(jnp.float32) + self.near[1].astype(jnp.float32)


class RingGather:
    def __init__(self, copies, slabs, index, to):
        self.copies, self.slabs, self.c = copies, slabs, index
        self.next, self.prev = to(index + 1), to(index + 3)
        half = ROWS // 2
        self.top, self.low = pl.ds(0, half), pl.ds(half, half)

    def go(self, k, part, where):
        piece = self.slabs.at[lax.rem(self.c + k, SIDE)].at[part]
        return self.copies.start(piece, piece, where)

    def run(self):
        first = (self.go(0, self.top, self.next), self.go(0, self.low, self.prev))
        second = (self.go(0, self.low, self.next), self.go(0, self.top, self.prev))
        first[0].wait_recv()
        far = [self.go(3, self.top, self.next)]
        first[1].wait_recv()
        far.append(self.go(1, self.low, self.prev))
        for copy in (*second, *far):
            copy.wait_recv()


def quarter(width, plane, planes):
    size = width // planes
    return pl.ds(pl.multiple_of(lax.rem(plane, planes) * size, 128), size)


class Levels:
    def __init__(self, copies, rep, reps):
        self.copies, self.plane, self.planes = copies, lax.div(rep, 2), reps // 2
        self.above, self.below = (
            {"rep": lax.rem(rep + 2 * k, reps)} for k in (1, self.planes - 1)
        )
        self.sent = []

    def share(self, array, k):
        return array.at[:, quarter(array.shape[1], self.plane + k, self.planes)]

    def spread(self, array):
        piece = self.share(array, 0)
        self.sent.append(
            (
                array,
                self.copies.start(piece, piece, self.above),
                self.copies.start(piece, piece, self.below),
            )
        )

    def pass_on(self):
        self.far = []
        for array, from_below, from_above in self.sent:
            half = array.shape[0] // 2
            from_below.wait_recv()
            piece = self.share(array, self.planes - 1).at[pl.ds(0, half)]
            self.far.append(self.copies.start(piece, piece, self.above))
            from_above.wait_recv()
            piece = self.share(array, 1).at[pl.ds(half, half)]
            self.far.append(self.copies.start(piece, piece, self.below))

    def finish(self):
        for copy in self.far:
            copy.wait_recv()


class RowRing:
    def __init__(self, copies, shards, own, columns, index, to):
        self.copies, self.shards, self.columns, self.c = copies, shards, columns, index
        self.next, self.prev = to(index + 1), to(index + 3)
        half = own.shape[0] // 2
        self.parts = pl.ds(0, half), pl.ds(half, half)
        top, low = (own.at[part, columns] for part in self.parts)
        self.first = (self.go(0, 0, self.next, top), self.go(0, 1, self.prev, low))
        self.second = (self.go(0, 1, self.next, low), self.go(0, 0, self.prev, top))

    def go(self, k, part, where, source=None):
        piece = self.shards.at[lax.rem(self.c + k, SIDE), self.parts[part], self.columns]
        return self.copies.start(piece if source is None else source, piece, where)

    def pass_on(self):
        self.first[0].wait_recv()
        self.far = [self.go(3, 0, self.next)]
        self.first[1].wait_recv()
        self.far.append(self.go(1, 1, self.prev))

    def finish(self):
        for copy in (*self.second, *self.far):
            copy.wait_recv()


def add_into(ref, value):
    ref[...] = (ref[...].astype(jnp.float32) + value.astype(jnp.float32)).astype(ref.dtype)


class Scatter:
    def __init__(self, copies, parts, far, near, row, row_far, row_near):
        y, x, a, b, self.device = place()
        self.a, self.b = a, b
        self.copies, self.parts, self.far, self.near = copies, parts, far, near
        self.ring = RingSum(
            copies, row, row_far, row_near, b, lambda j: tensor(self.device(a, j))
        )
        self.above, self.below = tensor(self.device(a + 1, b)), tensor(self.device(a + 3, b))
        self.ups, self.downs = (b + 2, b + 1), (b + 3, b)

    def part(self, i, j):
        return self.parts.at[lax.rem(i, SIDE), lax.rem(j, SIDE)]

    def landing(self, side, j):
        return self.near.at[side, lax.rem(j, SIDE)]

    def send_far(self):
        self.far_up, self.far_down = [], []
        for k in range(2):
            self.far_up.append(
                self.copies.start(self.part(self.a + 2, self.ups[k]), self.far.at[0, k], self.above)
            )
            self.far_down.append(
                self.copies.start(
                    self.part(self.a + 2, self.downs[k]), self.far.at[1, k], self.below
                )
            )

    def send_near(self):
        self.near_up, self.near_down = [], []
        for k in range(2):
            self.near_up.append(
                self.copies.start(
                    self.part(self.a + 1, self.downs[k]),
                    self.landing(0, self.downs[k]),
                    self.above,
                )
            )
            self.near_down.append(
                self.copies.start(
                    self.part(self.a + 3, self.ups[k]), self.landing(1, self.ups[k]), self.below
                )
            )

    def pass_on(self):
        self.sum_up, self.sum_down = [], []
        for k in range(2):
            self.far_up[k].wait_recv()
            add_into(self.part(self.a + 1, self.ups[k]), self.far[0, k])
            self.sum_up.append(
                self.copies.start(
                    self.part(self.a + 1, self.ups[k]), self.landing(0, self.ups[k]), self.above
                )
            )
            self.far_down[k].wait_recv()
            add_into(self.part(self.a + 3, self.downs[k]), self.far[1, k])
            self.sum_down.append(
                self.copies.start(
                    self.part(self.a + 3, self.downs[k]),
                    self.landing(1, self.downs[k]),
                    self.below,
                )
            )

    def total(self, j):
        at = lax.rem(j, SIDE)
        return (
            self.parts[self.a, at].astype(jnp.float32)
            + self.near[0, at].astype(jnp.float32)
            + self.near[1, at].astype(jnp.float32)
        )

    def finish(self):
        ring, b = self.ring, self.b
        self.sum_up[0].wait_recv()
        self.near_down[0].wait_recv()
        ring.row(2)[...] = self.total(b + 2).astype(jnp.bfloat16)
        ring.send_far()
        self.near_up[0].wait_recv()
        self.sum_down[0].wait_recv()
        ring.row(3)[...] = self.total(b + 3).astype(jnp.bfloat16)
        ring.send_prev()
        self.sum_up[1].wait_recv()
        self.near_down[1].wait_recv()
        ring.row(1)[...] = self.total(b + 1).astype(jnp.bfloat16)
        ring.send_next()
        ring.pass_on()
        self.near_up[1].wait_recv()
        self.sum_down[1].wait_recv()
        return ring.finish(self.total(b))


class SmallSum:
    def __init__(self, copies, over_x, over_y):
        t = lax.axis_index("tensor")
        self.y, self.x = lax.div(t, SIDE), lax.rem(t, SIDE)
        self.copies, self.over_x, self.over_y = copies, over_x, over_y

    def begin(self, value):
        self.over_x[self.x] = value.astype(jnp.bfloat16)
        mine = self.over_x.at[self.x]
        self.sent = [
            self.copies.start(
                mine, mine, tensor(SIDE * self.y + lax.rem(self.x + k, SIDE))
            )
            for k in (1, 2, 3)
        ]

    def middle(self):
        for copy in self.sent:
            copy.wait_recv()
        self.over_y[self.y] = sum(
            self.over_x[k].astype(jnp.float32) for k in range(SIDE)
        ).astype(jnp.bfloat16)
        mine = self.over_y.at[self.y]
        self.sent = [
            self.copies.start(
                mine, mine, tensor(SIDE * lax.rem(self.y + k, SIDE) + self.x)
            )
            for k in (1, 2, 3)
        ]

    def finish(self):
        for copy in self.sent:
            copy.wait_recv()
        return sum(self.over_y[k].astype(jnp.float32) for k in range(SIDE))


def layer_norm(values, gain_row, shift_row):
    average = jnp.mean(values, axis=-1, keepdims=True)
    centred = values - average
    spread = jnp.mean(centred * centred, axis=-1, keepdims=True)
    return centred * lax.rsqrt(spread + 1e-05) * gain_row + shift_row


def project_kernel(
    reps,
    scale,
    len_ref,
    dec_ref,
    x_hbm,
    w_hbm,
    cache_hbm,
    w_out_hbm,
    out_ref,
    attn_ref,
    w_row_hbm,
    rows,
    dec_rows,
    w_ref,
    cache_ref,
    states,
    local_sem,
    send_sem,
    recv_sem,
):
    y, x, a, b, device = place()
    load_x = pltpu.make_async_copy(x_hbm, rows.at[device(a, b)], local_sem.at[2])
    load_x.start()
    load_w = pltpu.make_async_copy(w_hbm, w_ref, local_sem.at[0])
    load_w.start()
    load_cache = pltpu.make_async_copy(cache_hbm, cache_ref, local_sem.at[1])
    load_cache.start()
    keep_w = pltpu.make_async_copy(w_out_hbm, w_row_hbm.at[b], local_sem.at[3])
    keep_w.start()
    rep = lax.axis_index("rep")
    copies = Copies(send_sem, recv_sem)
    greet(
        [device(a, b + k) for k in (1, 2, 3)] + [device(a + 1, b), device(a + 3, b)],
        [lax.rem(rep + k, reps) for k in range(1, reps)],
    )
    gather = Gather(copies, lambda i, j: rows.at[device(i, j)])
    mine = quarter(w_out_hbm.shape[1], lax.div(rep, 2), reps // 2)
    shards = [
        copies.start(
            w_out_hbm.at[:, mine], w_row_hbm.at[b, :, mine], tensor(device(a, b + k))
        )
        for k in (1, 3, 2)
    ]
    dec_rows[...] = jnp.zeros_like(dec_rows)
    dec_rows[: dec_ref.shape[0]] = dec_ref[...]
    load_x.wait()
    levels = Levels(copies, rep, reps)
    for k, shard in zip((1, 3, 2), shards):
        shard.wait_recv()
        levels.spread(w_row_hbm.at[lax.rem(b - k + SIDE, SIDE)])
    gather.begin()
    load_w.wait()
    dec = (
        lax.dot_general(w_ref[...], dec_rows[...], NT, preferred_element_type=jnp.float32)
        .astype(jnp.bfloat16)
        .astype(jnp.float32)
    )
    gather.first()
    load_cache.wait()
    hd = cache_ref.shape[2] // 2
    heads = cache_ref.shape[1]
    span = cache_ref.shape[3]
    lanes = dec.shape[1]
    lane = lax.broadcasted_iota(jnp.int32, (1, lanes), 1)
    position = rep * span + lax.broadcasted_iota(jnp.int32, (1, span), 1)

    def request(r, state):
        pick = lane == r
        column = jnp.sum(jnp.where(pick, dec, 0.0), axis=1, keepdims=True)
        valid = position < len_ref[r]
        out = []
        for h in range(heads):
            query = column[3 * hd * h : 3 * hd * h + hd]
            key = cache_ref[r, h, :hd].astype(jnp.float32)
            value = cache_ref[r, h, hd:].astype(jnp.float32)
            score = jnp.sum(key * query, axis=0, keepdims=True) * scale
            score = jnp.where(valid, score, NEG)
            high = jnp.max(score, axis=1, keepdims=True)
            weight = jnp.where(valid, jnp.exp(score - high), 0.0)
            total = jnp.sum(weight, axis=1, keepdims=True)
            mixed = jnp.sum(value * weight, axis=1, keepdims=True)
            highs, totals, mixes = state[h]
            out.append(
                (
                    jnp.where(pick, high, highs),
                    jnp.where(pick, total, totals),
                    jnp.where(pick, mixed, mixes),
                )
            )
        return tuple(out)

    empty = tuple(
        (
            jnp.full((1, lanes), NEG, jnp.float32),
            jnp.zeros((1, lanes), jnp.float32),
            jnp.zeros((hd, lanes), jnp.float32),
        )
        for _ in range(heads)
    )
    state = lax.fori_loop(0, cache_ref.shape[0], request, empty)
    for h in range(heads):
        states[rep, h, :hd] = state[h][2]
        states[rep, h, hd : hd + 8] = jnp.broadcast_to(state[h][0], (8, lanes))
        states[rep, h, hd + 8 : hd + 16] = jnp.broadcast_to(state[h][1], (8, lanes))
    sent = [
        copies.start(states.at[rep], states.at[rep], {"rep": lax.rem(rep + k, reps)})
        for k in range(1, reps)
    ]
    levels.pass_on()
    gather.middle()

    def tiles(start):
        core = lax.rem(rep, 2)
        for k in (0, 2):
            at = []
            for n in (k, k + 1):
                row_at = (1 - core) * lax.rem(a + start + n // 2, SIDE) + core * n
                side = (1 - core) * (n % 2) + core * lax.rem(lax.div(a, 2) + start // 2, 2)
                at.append(2 * row_at + side)
            block = jnp.concatenate(
                [rows[pl.ds(2 * t, 2)].reshape(2 * ROWS, rows.shape[2]) for t in at], axis=0
            )
            result = lax.dot_general(
                w_ref[...], block, NT, preferred_element_type=jnp.float32
            ).astype(out_ref.dtype)
            for n, t in enumerate(at):
                out_ref[:, pl.ds(pl.multiple_of(t * 2 * ROWS, 2 * ROWS), 2 * ROWS)] = result[
                    :, n * 2 * ROWS : (n + 1) * 2 * ROWS
                ]

    tiles(0)
    for copy in sent:
        copy.wait_recv()
    for h in range(heads):
        base = 3 * hd * h
        query, key, value = (dec[base + hd * k : base + hd * (k + 1)] for k in range(3))
        own = jnp.sum(query * key, axis=0, keepdims=True) * scale
        highest = own
        for k in range(reps):
            highest = jnp.maximum(highest, states[k, h, hd : hd + 1])
        own_weight = jnp.exp(own - highest)
        total, mixed = own_weight, own_weight * value
        for k in range(reps):
            factor = jnp.exp(states[k, h, hd : hd + 1] - highest)
            total = total + factor * states[k, h, hd + 8 : hd + 9]
            mixed = mixed + factor * states[k, h, :hd]
        attn_ref[:, hd * h : hd * (h + 1)] = (mixed / total).T[: attn_ref.shape[0]].astype(
            attn_ref.dtype
        )
    gather.last()
    tiles(2)
    levels.finish()
    keep_w.wait()
    copies.drain()


def attend(head, scale, offset, qkv_ref, kv_ref, seg_row, out_ref, q_ref, state):
    hd = q_ref.shape[1]
    span = seg_row.shape[1]
    block, key_block = 256, 1024
    early = span // 2 // block
    factor = scale * LOG2E
    q_ref[...] = qkv_ref[head, 0].astype(jnp.float32).T.astype(jnp.bfloat16)
    seg_keys = seg_row[...].astype(jnp.float32)
    seg_rows = jnp.broadcast_to(seg_keys, (8, span)).T[:, :1]
    states = [state[2 * i : 2 * i + 2] for i in range(early)]

    def rows(i):
        return slice(i * block, (i + 1) * block)

    def mix(weight, values):
        ones = jnp.ones((16, values.shape[1]), jnp.bfloat16)
        return lax.dot_general(
            weight.astype(jnp.bfloat16),
            jnp.concatenate([values, ones], axis=0),
            NT,
            preferred_element_type=jnp.float32,
        )

    for m_ref, acc_ref in states:
        m_ref[...] = jnp.full(m_ref.shape, NEG, jnp.float32)
        acc_ref[...] = jnp.zeros(acc_ref.shape, jnp.float32)

    @pl.loop(0, kv_ref.shape[2] // key_block)
    def _(j):
        at = pl.multiple_of(j * key_block, key_block)
        keys = kv_ref[head, :hd, pl.ds(at, key_block)]
        values = kv_ref[head, hd:, pl.ds(at, key_block)]
        seen = at + lax.broadcasted_iota(jnp.int32, (1, key_block), 1) < offset
        scores = [
            jnp.dot(q_ref[rows(i)], keys, preferred_element_type=jnp.float32)
            for i in range(early)
        ]
        for score, (m_ref, acc_ref) in zip(scores, states):
            score = jnp.where(seen, score, NEG)
            high = jnp.maximum(m_ref[...], jnp.max(score, axis=1, keepdims=True))
            decay = jnp.exp2((m_ref[...] - high) * factor)
            weight = jnp.exp2((score - high) * factor)
            m_ref[...] = high
            acc_ref[...] = acc_ref[...] * decay + mix(weight, values)

    for i in range(span // block):
        low = max(0, (i - early) * block)
        high = (i + 1) * block
        seg_q = seg_rows[rows(i)]
        score = jnp.dot(
            q_ref[rows(i)], qkv_ref[head, 1, :, low:high], preferred_element_type=jnp.float32
        )
        shape = (block, high - low)
        query_at = i * block + lax.broadcasted_iota(jnp.int32, shape, 0)
        key_at = low + lax.broadcasted_iota(jnp.int32, shape, 1)
        seen = (seg_keys[:, low:high] == seg_q) & (key_at <= query_at)
        score = jnp.where(seen, score, NEG)
        values = qkv_ref[head, 2, :, low:high]
        peak = jnp.max(score, axis=1, keepdims=True)
        if i < early:
            m_ref, acc_ref = states[i]
            keep = (seg_q == 0) & (offset > 0)
            before = jnp.where(keep, m_ref[...], NEG)
            peak = jnp.maximum(peak, before)
            decay = jnp.where(keep, jnp.exp2((before - peak) * factor), 0.0)
        weight = jnp.exp2((score - peak) * factor)
        mixed = mix(weight, values)
        if i < early:
            mixed = mixed + acc_ref[...] * decay
        out_ref[rows(i), head * hd : (head + 1) * hd] = (
            mixed[:, :hd] / mixed[:, hd : hd + 1]
        ).astype(out_ref.dtype)


def tail_kernel(
    scale,
    reps,
    offset_ref,
    seg_row,
    dec_attn_ref,
    x_dec_ref,
    up_bias_ref,
    biases_ref,
    gains_ref,
    shifts_ref,
    qkv_hbm,
    kv_hbm,
    x_hbm,
    w_row_hbm,
    w_up_hbm,
    w_down_hbm,
    w_next_hbm,
    result_hbm,
    out_ref,
    dec_out_ref,
    dec_next_ref,
    qkv_ref,
    kv_ref,
    x_ref,
    w_row_ref,
    w_up_ref,
    w_down_ref,
    w_next_ref,
    attn_ref,
    heads_ref,
    columns_ref,
    result_ref,
    slabs,
    parts,
    far,
    near,
    row,
    row_far,
    row_near,
    over_x,
    over_y,
    q_ref,
    m0_ref,
    acc0_ref,
    m1_ref,
    acc1_ref,
    local_sem,
    send_sem,
    recv_sem,
):
    y, x, a, b, device = place()
    loads = []
    for k, (source, target) in enumerate(
        (
            (qkv_hbm, qkv_ref),
            (kv_hbm, kv_ref),
            (w_row_hbm, w_row_ref),
            (x_hbm, x_ref),
            (w_next_hbm, w_next_ref.at[b]),
            (w_up_hbm, w_up_ref),
            (w_down_hbm, w_down_ref),
        )
    ):
        loads.append(pltpu.make_async_copy(source, target, local_sem.at[k]))
        loads[-1].start()
    load_qkv, load_kv, load_row, load_x, load_next, load_up, load_down = loads
    copies = Copies(send_sem, recv_sem)
    rep = lax.axis_index("rep")
    plane, planes = lax.div(rep, 2), reps // 2
    columns, width = w_next_hbm.shape

    greet(
        [SIDE * y + lax.rem(x + k, SIDE) for k in (1, 2, 3)]
        + [SIDE * lax.rem(y + k, SIDE) + x for k in (1, 2, 3)],
        [lax.rem(rep + 2 * k, reps) for k in (1, planes - 1)],
    )
    chunk = (SIDE, ROWS, width)
    load_row.wait()
    dec_sum = SmallSum(copies, over_x.at[0], over_y.at[0])
    dec_sum.begin(
        jnp.dot(dec_attn_ref[...], w_row_ref[b], preferred_element_type=jnp.float32)
    )
    shards = RowRing(
        copies,
        w_next_ref,
        w_next_hbm,
        quarter(width, plane, planes),
        b,
        lambda j: tensor(device(a, j)),
    )
    attn_ref[...] = jnp.zeros_like(attn_ref)
    result_ref[...] = jnp.zeros_like(result_ref)
    load_qkv.wait()
    load_kv.wait()
    state = (m0_ref, acc0_ref, m1_ref, acc1_ref)
    offset = offset_ref[0]
    heads = qkv_ref.shape[0]
    for head in range(heads):
        attend(head, scale, offset, qkv_ref, kv_ref, seg_row, attn_ref, q_ref, state)
        if head == 0:
            dec_sum.middle()
            shards.pass_on()

    def tokens(i, j):
        return attn_ref.at[pl.ds(pl.multiple_of(device(i, j) * ROWS, ROWS), ROWS)]

    swaps = [
        copies.start(tokens(i, b + k), heads_ref.at[b, i], tensor(device(a, b + k)))
        for k in (2, 1, 3)
        for i in range(SIDE)
    ]
    for i in range(SIDE):
        heads_ref[b, i] = tokens(i, b)[...]
    for swap in swaps:
        swap.wait_recv()
    ring = RingSum(
        copies, row.at[0], row_far.at[0], row_near.at[0], a, lambda i: tensor(device(i, b))
    )
    depth = w_row_ref.shape[1]
    step = width // 5
    for n in range(0, width, step):
        total = sum(
            jnp.dot(
                heads_ref[j].reshape(SIDE * ROWS, heads_ref.shape[3])[:, :depth],
                w_row_ref[j, :, n : n + step],
                preferred_element_type=jnp.float32,
            )
            for j in range(SIDE)
        )
        row[0, :, :, n : n + step] = total.astype(jnp.bfloat16).reshape(SIDE, ROWS, step)
    ring.send_far()
    ring.send_next()
    ring.send_prev()
    ring.pass_on()
    shards.finish()
    levels = Levels(copies, rep, reps)
    for k in (1, 2, 3):
        levels.spread(w_next_ref.at[lax.rem(b + k, SIDE)])
    dec_first = layer_norm(
        x_dec_ref[...].astype(jnp.float32) + dec_sum.finish() + biases_ref[0:1],
        gains_ref[0:1],
        shifts_ref[0:1],
    ).astype(jnp.bfloat16)
    own = row[0, a].astype(jnp.float32)
    load_x.wait()
    attn_sum = ring.finish(own)
    first = layer_norm(
        x_ref[...].astype(jnp.float32) + attn_sum + biases_ref[0:1], gains_ref[0:1], shifts_ref[0:1]
    ).astype(jnp.bfloat16)

    def slab(i, j):
        return slabs.at[lax.rem(i, SIDE), lax.rem(j, SIDE)]

    slab(a, b)[...] = first
    gather = Gather(copies, slab)
    gather.begin()
    load_up.wait()
    load_down.wait()

    def mlp(value):
        inner = jnp.dot(value, w_up_ref[...], preferred_element_type=jnp.float32)
        inner = inner + up_bias_ref[...][None, :]
        hidden = (0.5 * inner * (1.0 + lax.erf(inner * 0.7071067811865476))).astype(jnp.bfloat16)
        return jnp.dot(hidden, w_down_ref[...], preferred_element_type=jnp.float32)

    def mlp_share(i):
        at = lax.rem(i, SIDE)
        parts[at] = (
            mlp(slabs[at].reshape(SIDE * ROWS, width)).astype(jnp.bfloat16).reshape(chunk)
        )

    scatter = Scatter(copies, parts, far, near, row.at[1], row_far.at[1], row_near.at[1])
    gather.first()
    mlp_share(a)
    dec_sum = SmallSum(copies, over_x.at[1], over_y.at[1])
    dec_sum.begin(mlp(dec_first))
    gather.middle()
    mlp_share(a + 1)
    mlp_share(a + 3)
    scatter.send_near()
    gather.last()
    mlp_share(a + 2)
    scatter.send_far()
    scatter.pass_on()
    levels.pass_on()
    dec_sum.middle()
    mlp_sum = scatter.finish()
    second = layer_norm(
        first.astype(jnp.float32) + mlp_sum + biases_ref[1:2], gains_ref[1:2], shifts_ref[1:2]
    ).astype(jnp.bfloat16)
    out_ref[...] = second
    columns_ref[a] = second
    RingGather(copies, columns_ref, a, lambda i: tensor(device(i, b))).run()
    levels.finish()
    load_next.wait()
    keeps = []
    for k in (2, 1, 3, 0):
        j = lax.rem(b + k, SIDE)
        result_ref[j, :, :, :columns] = (
            lax.dot_general(
                columns_ref[...].reshape(SIDE * ROWS, width),
                w_next_ref[j],
                NT,
                preferred_element_type=jnp.float32,
            )
            .astype(jnp.bfloat16)
            .reshape(SIDE, ROWS, columns)
        )
        for i in range(SIDE):
            source, target = result_ref.at[j, i], result_hbm.at[device(i, b)]
            if k:
                keeps.append(copies.start(source, target, tensor(device(a, j))))
            else:
                local = pltpu.make_async_copy(source, target, local_sem.at[i])
                local.start()
                loads.append(local)
    dec_out = layer_norm(
        dec_first.astype(jnp.float32) + dec_sum.finish() + biases_ref[1:2],
        gains_ref[1:2],
        shifts_ref[1:2],
    ).astype(jnp.bfloat16)
    dec_out_ref[...] = dec_out
    dec_next_ref[...] = lax.dot_general(
        dec_out, w_next_ref[b], NT, preferred_element_type=jnp.float32
    ).astype(jnp.bfloat16)
    for copy in keeps:
        copy.wait_recv()
    for local in loads[-SIDE:]:
        local.wait()
    copies.drain()


def layout_kernel(
    result_ref, own_ref, dec_ref, dec_result_ref, next_ref, out_ref, dec_out_ref, dec_next_ref
):
    columns, lanes = next_ref.shape[0], result_ref.shape[2]
    same = lax.broadcasted_iota(jnp.int32, (columns, lanes), 0) == lax.broadcasted_iota(
        jnp.int32, (columns, lanes), 1
    )
    next_ref[...] = lax.dot_general(
        same.astype(jnp.float32).astype(jnp.bfloat16),
        result_ref[...].reshape(SIDE * ROWS, lanes),
        NT,
        preferred_element_type=jnp.float32,
    ).astype(next_ref.dtype)

    @pl.when(pl.program_id(0) == 0)
    def _():
        out_ref[...] = own_ref[...]
        dec_out_ref[...] = dec_ref[...]
        dec_next_ref[...] = dec_result_ref[...]


def per_device(
    reps,
    x_pre,
    x_dec,
    prefix_kv,
    cache_kv,
    dec_len,
    offsets,
    segments,
    w_qkv,
    w_out,
    w_up,
    up_bias,
    w_down,
    biases,
    gains,
    shifts,
    w_next,
):
    heads = prefix_kv.shape[2]
    hd = prefix_kv.shape[3] // 2
    span = segments.shape[1]
    width = x_pre.shape[1]
    decodes = x_dec.shape[0]
    columns = w_qkv.shape[1]
    units = w_up.shape[1]
    scale = hd ** (-0.5)
    bf16, f32 = jnp.bfloat16, jnp.float32
    shape = jax.ShapeDtypeStruct
    whole = pl.BlockSpec(memory_space=VMEM)
    scalars = pl.BlockSpec(memory_space=pltpu.SMEM)
    anywhere = pl.BlockSpec(memory_space=pltpu.HBM)
    group = SIDE * SIDE

    cache_t = cache_kv.transpose(0, 2, 3, 1)
    n_copies = 16 + reps - 1 + (SIDE - 1) * 5
    qkv_t, dec_attn, w_row = pl.pallas_call(
        functools.partial(project_kernel, reps, scale),
        out_shape=(
            shape((columns, span), bf16),
            shape((decodes, heads * hd), bf16),
            shape((SIDE,) + w_out.shape, bf16),
        ),
        in_specs=[scalars, whole] + [anywhere] * 4,
        out_specs=(whole, whole, anywhere),
        scratch_shapes=[
            VMEM((group, ROWS, width), bf16),
            VMEM((128, width), bf16),
            VMEM((columns, width), bf16),
            VMEM(cache_t.shape, bf16),
            VMEM((reps, heads, hd + 16, 128), f32),
            pltpu.SemaphoreType.DMA((4,)),
            pltpu.SemaphoreType.DMA((n_copies,)),
            pltpu.SemaphoreType.DMA((n_copies,)),
        ],
        compiler_params=pltpu.CompilerParams(
            collective_id=0, has_side_effects=True, vmem_limit_bytes=62 << 20
        ),
        name="project",
    )(dec_len, x_dec, x_pre, w_qkv.T, cache_t, w_out)

    n_copies = 100
    lanes = 512
    result, own, dec_own, dec_result = pl.pallas_call(
        functools.partial(tail_kernel, scale, reps),
        out_shape=(
            shape((group, ROWS, lanes), bf16),
            shape((ROWS, width), bf16),
            shape((decodes, width), bf16),
            shape((decodes, columns), bf16),
        ),
        in_specs=[scalars] + [whole] * 7 + [anywhere] * 7,
        out_specs=(anywhere, whole, whole, whole),
        scratch_shapes=[
            VMEM((heads, 3, hd, span), bf16),
            VMEM((heads, 2 * hd, prefix_kv.shape[1]), bf16),
            VMEM((ROWS, width), bf16),
            VMEM((SIDE,) + w_out.shape, bf16),
            VMEM((width, units), bf16),
            VMEM((units, width), bf16),
            VMEM((SIDE, columns, width), bf16),
            VMEM((span, 256), bf16),
            VMEM((SIDE, SIDE, ROWS, 256), bf16),
            VMEM((SIDE, ROWS, width), bf16),
            VMEM((SIDE, SIDE, ROWS, lanes), bf16),
            VMEM((SIDE, SIDE, ROWS, width), bf16),
            VMEM((SIDE, SIDE, ROWS, width), bf16),
            VMEM((2, 2, ROWS, width), bf16),
            VMEM((2, SIDE, ROWS, width), bf16),
            VMEM((2, SIDE, ROWS, width), bf16),
            VMEM((2, 2, ROWS // 2, width), bf16),
            VMEM((2, 2, ROWS, width), bf16),
            VMEM((2, SIDE, decodes, width), bf16),
            VMEM((2, SIDE, decodes, width), bf16),
            VMEM((span, hd), bf16),
            *([VMEM((256, 1), f32), VMEM((256, hd + 16), f32)] * 2),
            pltpu.SemaphoreType.DMA((8,)),
            pltpu.SemaphoreType.DMA((n_copies,)),
            pltpu.SemaphoreType.DMA((n_copies,)),
        ],
        compiler_params=pltpu.CompilerParams(
            collective_id=1, has_side_effects=True, vmem_limit_bytes=62 << 20
        ),
        name="tail",
    )(
        offsets,
        segments,
        dec_attn,
        x_dec,
        up_bias,
        biases,
        gains,
        shifts,
        qkv_t.reshape(heads, 3, hd, span),
        prefix_kv[0].transpose(1, 2, 0),
        x_pre,
        w_row,
        w_up,
        w_down,
        w_next.T,
    )

    next_t, layer_out, dec_out, dec_next = pl.pallas_call(
        layout_kernel,
        grid=(SIDE,),
        out_shape=(
            shape((columns, span), bf16),
            shape((ROWS, width), bf16),
            shape((decodes, width), bf16),
            shape((decodes, columns), bf16),
        ),
        in_specs=[
            pl.BlockSpec((SIDE, ROWS, lanes), lambda i: (i, 0, 0)),
            pl.BlockSpec((ROWS, width), lambda i: (0, 0)),
            pl.BlockSpec((decodes, width), lambda i: (0, 0)),
            pl.BlockSpec((decodes, columns), lambda i: (0, 0)),
        ],
        out_specs=(
            pl.BlockSpec((columns, SIDE * ROWS), lambda i: (0, i)),
            pl.BlockSpec((ROWS, width), lambda i: (0, 0)),
            pl.BlockSpec((decodes, width), lambda i: (0, 0)),
            pl.BlockSpec((decodes, columns), lambda i: (0, 0)),
        ),
        compiler_params=pltpu.CompilerParams(
            dimension_semantics=("arbitrary",), vmem_limit_bytes=62 << 20
        ),
        name="layout",
    )(result, own, dec_own, dec_result)
    return layer_out, next_t.T, dec_out, dec_next


def solution(mesh):
    placed = (
        P(("rep", "tensor"), None),
        P(),
        P("rep", None, "tensor", None),
        P(None, "rep", "tensor", None),
        P(),
        P("rep"),
        P("rep", None),
        P(None, "tensor"),
        P("tensor", None),
        P(None, "tensor"),
        P("tensor"),
        P("tensor", None),
        P(),
        P(),
        P(),
        P(None, "tensor"),
    )
    return jax.shard_map(
        functools.partial(per_device, mesh.shape["rep"]),
        mesh=mesh,
        in_specs=placed,
        out_specs=(P(("rep", "tensor"), None), P("rep", "tensor"), P(), P(None, "tensor")),
        check_vma=False,
    )
```

```python
import functools

import jax
import jax.numpy as jnp
from jax import lax
from jax.experimental import pallas as pl
from jax.experimental.pallas import tpu as pltpu
from jax.sharding import PartitionSpec as P

MESH = pl.DeviceIdType.MESH
NEG = -1e30
LOG2E = 1.4426950408889634
SIDE = 4
ROWS = 64
VMEM = pltpu.VMEM
NT = (((1,), (1,)), ((), ()))


def place():
    t = lax.axis_index("tensor")
    core = lax.rem(lax.axis_index("rep"), 2)
    y, x = lax.div(t, SIDE), lax.rem(t, SIDE)
    major = y * (1 - core) + x * core
    minor = x * (1 - core) + y * core
    step_major, step_minor = SIDE - (SIDE - 1) * core, 1 + (SIDE - 1) * core

    def device(i, j):
        return lax.rem(i, SIDE) * step_major + lax.rem(j, SIDE) * step_minor

    return y, x, major, minor, device


class Copies:
    def __init__(self, send, recv):
        self.send, self.recv, self.used, self.all = send, recv, 0, []

    def start(self, src, dst, where):
        copy = pltpu.make_async_remote_copy(
            src_ref=src,
            dst_ref=dst,
            send_sem=self.send.at[self.used],
            recv_sem=self.recv.at[self.used],
            device_id=where,
            device_id_type=MESH,
        )
        copy.start()
        self.used += 1
        self.all.append(copy)
        return copy

    def drain(self):
        for copy in self.all:
            copy.wait_send()


def tensor(t):
    return {"tensor": t}


def greet(tensor_peers, rep_peers=()):
    barrier = pltpu.get_barrier_semaphore()
    for t in tensor_peers:
        pl.semaphore_signal(barrier, inc=1, device_id=tensor(t), device_id_type=MESH)
    for r in rep_peers:
        pl.semaphore_signal(barrier, inc=1, device_id={"rep": r}, device_id_type=MESH)
    pl.semaphore_wait(barrier, len(tensor_peers) + len(rep_peers))


class Gather:
    def __init__(self, copies, at, own=None):
        y, x, self.a, self.b, self.device = place()
        self.copies, self.at, self.own = copies, at, own

    def go(self, i, j, ti, tj):
        return self.copies.start(self.at(i, j), self.at(i, j), tensor(self.device(ti, tj)))

    def begin(self):
        a, b = self.a, self.b
        own = self.at(a, b) if self.own is None else self.own
        self.right, self.left, up, down = (
            self.copies.start(own, self.at(a, b), tensor(self.device(i, j)))
            for i, j in ((a, b + 1), (a, b + 3), (a + 1, b), (a + 3, b))
        )
        self.up, self.down = [up], [down]

    def spread(self, j):
        a, b = self.a, self.b
        self.up.append(self.go(a, j, a + 1, b))
        self.down.append(self.go(a, j, a + 3, b))

    def half(self, i, j, part):
        return self.at(i, j).at[pl.ds(part * (ROWS // 2), ROWS // 2)]

    def first(self):
        a, b = self.a, self.b
        self.right.wait_recv()
        one = self.half(a, b + 3, 0)
        far_one = self.copies.start(one, one, tensor(self.device(a, b + 1)))
        self.spread(b + 3)
        self.left.wait_recv()
        two = self.half(a, b + 1, 1)
        far_two = self.copies.start(two, two, tensor(self.device(a, b + 3)))
        self.spread(b + 1)
        far_one.wait_recv()
        far_two.wait_recv()
        self.spread(b + 2)

    def middle(self):
        a, b = self.a, self.b
        self.up[0].wait_recv()
        self.far = [self.go(a + 3, b, a + 1, b)]
        self.down[1].wait_recv()
        self.far.append(self.go(a + 1, b + 3, a + 3, b))
        self.down[2].wait_recv()
        self.far.append(self.go(a + 1, b + 1, a + 3, b))
        self.up[3].wait_recv()
        self.far.append(self.go(a + 3, b + 2, a + 1, b))
        self.up[1].wait_recv()
        self.up[2].wait_recv()
        self.down[0].wait_recv()
        self.down[3].wait_recv()

    def last(self):
        for copy in self.far:
            copy.wait_recv()


class RingSum:
    def __init__(self, copies, row, far, near, index, to):
        self.copies, self.slabs, self.far, self.near = copies, row, far, near
        self.c, self.next, self.prev = index, to(index + 1), to(index + 3)
        half = ROWS // 2
        self.top, self.low = pl.ds(0, half), pl.ds(half, half)

    def row(self, k):
        return self.slabs.at[lax.rem(self.c + k, SIDE)]

    def send_far(self):
        self.next_far = self.copies.start(self.row(2).at[self.top], self.far.at[0], self.next)
        self.prev_far = self.copies.start(self.row(2).at[self.low], self.far.at[1], self.prev)

    def send_next(self):
        self.next_near = self.copies.start(
            self.row(1).at[self.low], self.near.at[0, self.low], self.next
        )

    def send_prev(self):
        self.prev_near = self.copies.start(
            self.row(3).at[self.top], self.near.at[1, self.top], self.prev
        )

    def pass_on(self):
        self.next_far.wait_recv()
        add_into(self.row(1).at[self.top], self.far[0])
        self.next_sum = self.copies.start(
            self.row(1).at[self.top], self.near.at[0, self.top], self.next
        )
        self.prev_far.wait_recv()
        add_into(self.row(3).at[self.low], self.far[1])
        self.prev_sum = self.copies.start(
            self.row(3).at[self.low], self.near.at[1, self.low], self.prev
        )

    def finish(self, own):
        for copy in (self.next_near, self.prev_near, self.next_sum, self.prev_sum):
            copy.wait_recv()
        return own + self.near[0].astype(jnp.float32) + self.near[1].astype(jnp.float32)


class RingGather:
    def __init__(self, copies, slabs, index, to):
        self.copies, self.slabs, self.c = copies, slabs, index
        self.next, self.prev = to(index + 1), to(index + 3)
        half = ROWS // 2
        self.top, self.low = pl.ds(0, half), pl.ds(half, half)

    def go(self, k, part, where):
        piece = self.slabs.at[lax.rem(self.c + k, SIDE)].at[part]
        return self.copies.start(piece, piece, where)

    def run(self):
        first = (self.go(0, self.top, self.next), self.go(0, self.low, self.prev))
        second = (self.go(0, self.low, self.next), self.go(0, self.top, self.prev))
        first[0].wait_recv()
        far = [self.go(3, self.top, self.next)]
        first[1].wait_recv()
        far.append(self.go(1, self.low, self.prev))
        for copy in (*second, *far):
            copy.wait_recv()


def quarter(width, plane, planes):
    size = width // planes
    return pl.ds(pl.multiple_of(lax.rem(plane, planes) * size, 128), size)


class Levels:
    def __init__(self, copies, rep, reps):
        self.copies, self.plane, self.planes = copies, lax.div(rep, 2), reps // 2
        self.above, self.below = (
            {"rep": lax.rem(rep + 2 * k, reps)} for k in (1, self.planes - 1)
        )
        self.sent = []

    def share(self, array, k):
        return array.at[:, quarter(array.shape[1], self.plane + k, self.planes)]

    def spread(self, array):
        piece = self.share(array, 0)
        self.sent.append(
            (
                array,
                self.copies.start(piece, piece, self.above),
                self.copies.start(piece, piece, self.below),
            )
        )

    def pass_on(self):
        self.far = []
        for array, from_below, from_above in self.sent:
            half = array.shape[0] // 2
            from_below.wait_recv()
            piece = self.share(array, self.planes - 1).at[pl.ds(0, half)]
            self.far.append(self.copies.start(piece, piece, self.above))
            from_above.wait_recv()
            piece = self.share(array, 1).at[pl.ds(half, half)]
            self.far.append(self.copies.start(piece, piece, self.below))

    def finish(self):
        for copy in self.far:
            copy.wait_recv()


class RowRing:
    def __init__(self, copies, shards, own, columns, index, to):
        self.copies, self.shards, self.columns, self.c = copies, shards, columns, index
        self.next, self.prev = to(index + 1), to(index + 3)
        half = own.shape[0] // 2
        self.parts = pl.ds(0, half), pl.ds(half, half)
        top, low = (own.at[part, columns] for part in self.parts)
        self.first = (self.go(0, 0, self.next, top), self.go(0, 1, self.prev, low))
        self.second = (self.go(0, 1, self.next, low), self.go(0, 0, self.prev, top))

    def go(self, k, part, where, source=None):
        piece = self.shards.at[lax.rem(self.c + k, SIDE), self.parts[part], self.columns]
        return self.copies.start(piece if source is None else source, piece, where)

    def pass_on(self):
        self.first[0].wait_recv()
        self.far = [self.go(3, 0, self.next)]
        self.first[1].wait_recv()
        self.far.append(self.go(1, 1, self.prev))

    def finish(self):
        for copy in (*self.second, *self.far):
            copy.wait_recv()


def add_into(ref, value):
    ref[...] = (ref[...].astype(jnp.float32) + value.astype(jnp.float32)).astype(ref.dtype)


class Scatter:
    def __init__(self, copies, parts, far, near, row, row_far, row_near):
        y, x, a, b, self.device = place()
        self.a, self.b = a, b
        self.copies, self.parts, self.far, self.near = copies, parts, far, near
        self.ring = RingSum(
            copies, row, row_far, row_near, b, lambda j: tensor(self.device(a, j))
        )
        self.above, self.below = tensor(self.device(a + 1, b)), tensor(self.device(a + 3, b))
        self.ups, self.downs = (b + 2, b + 1), (b + 3, b)

    def part(self, i, j):
        return self.parts.at[lax.rem(i, SIDE), lax.rem(j, SIDE)]

    def landing(self, side, j):
        return self.near.at[side, lax.rem(j, SIDE)]

    def send_far(self):
        self.far_up, self.far_down = [], []
        for k in range(2):
            self.far_up.append(
                self.copies.start(self.part(self.a + 2, self.ups[k]), self.far.at[0, k], self.above)
            )
            self.far_down.append(
                self.copies.start(
                    self.part(self.a + 2, self.downs[k]), self.far.at[1, k], self.below
                )
            )

    def send_near(self):
        self.near_up, self.near_down = [], []
        for k in range(2):
            self.near_up.append(
                self.copies.start(
                    self.part(self.a + 1, self.downs[k]),
                    self.landing(0, self.downs[k]),
                    self.above,
                )
            )
            self.near_down.append(
                self.copies.start(
                    self.part(self.a + 3, self.ups[k]), self.landing(1, self.ups[k]), self.below
                )
            )

    def pass_on(self):
        self.sum_up, self.sum_down = [], []
        for k in range(2):
            self.far_up[k].wait_recv()
            add_into(self.part(self.a + 1, self.ups[k]), self.far[0, k])
            self.sum_up.append(
                self.copies.start(
                    self.part(self.a + 1, self.ups[k]), self.landing(0, self.ups[k]), self.above
                )
            )
            self.far_down[k].wait_recv()
            add_into(self.part(self.a + 3, self.downs[k]), self.far[1, k])
            self.sum_down.append(
                self.copies.start(
                    self.part(self.a + 3, self.downs[k]),
                    self.landing(1, self.downs[k]),
                    self.below,
                )
            )

    def total(self, j):
        at = lax.rem(j, SIDE)
        return (
            self.parts[self.a, at].astype(jnp.float32)
            + self.near[0, at].astype(jnp.float32)
            + self.near[1, at].astype(jnp.float32)
        )

    def finish(self):
        ring, b = self.ring, self.b
        self.sum_up[0].wait_recv()
        self.near_down[0].wait_recv()
        ring.row(2)[...] = self.total(b + 2).astype(jnp.bfloat16)
        ring.send_far()
        self.near_up[0].wait_recv()
        self.sum_down[0].wait_recv()
        ring.row(3)[...] = self.total(b + 3).astype(jnp.bfloat16)
        ring.send_prev()
        self.sum_up[1].wait_recv()
        self.near_down[1].wait_recv()
        ring.row(1)[...] = self.total(b + 1).astype(jnp.bfloat16)
        ring.send_next()
        ring.pass_on()
        self.near_up[1].wait_recv()
        self.sum_down[1].wait_recv()
        return ring.finish(self.total(b))


class SmallSum:
    def __init__(self, copies, over_x, over_y):
        t = lax.axis_index("tensor")
        self.y, self.x = lax.div(t, SIDE), lax.rem(t, SIDE)
        self.copies, self.over_x, self.over_y = copies, over_x, over_y

    def begin(self, value):
        self.over_x[self.x] = value.astype(jnp.bfloat16)
        mine = self.over_x.at[self.x]
        self.sent = [
            self.copies.start(
                mine, mine, tensor(SIDE * self.y + lax.rem(self.x + k, SIDE))
            )
            for k in (1, 2, 3)
        ]

    def middle(self):
        for copy in self.sent:
            copy.wait_recv()
        self.over_y[self.y] = sum(
            self.over_x[k].astype(jnp.float32) for k in range(SIDE)
        ).astype(jnp.bfloat16)
        mine = self.over_y.at[self.y]
        self.sent = [
            self.copies.start(
                mine, mine, tensor(SIDE * lax.rem(self.y + k, SIDE) + self.x)
            )
            for k in (1, 2, 3)
        ]

    def finish(self):
        for copy in self.sent:
            copy.wait_recv()
        return sum(self.over_y[k].astype(jnp.float32) for k in range(SIDE))


def layer_norm(values, gain_row, shift_row):
    average = jnp.mean(values, axis=-1, keepdims=True)
    centred = values - average
    spread = jnp.mean(centred * centred, axis=-1, keepdims=True)
    return centred * lax.rsqrt(spread + 1e-05) * gain_row + shift_row


def project_kernel(
    reps,
    scale,
    len_ref,
    dec_ref,
    x_hbm,
    w_hbm,
    cache_hbm,
    w_out_hbm,
    out_ref,
    attn_ref,
    w_row_hbm,
    rows,
    dec_rows,
    w_ref,
    cache_ref,
    states,
    local_sem,
    send_sem,
    recv_sem,
):
    y, x, a, b, device = place()
    load_x = pltpu.make_async_copy(x_hbm, rows.at[device(a, b)], local_sem.at[2])
    load_x.start()
    load_w = pltpu.make_async_copy(w_hbm, w_ref, local_sem.at[0])
    load_w.start()
    load_cache = pltpu.make_async_copy(cache_hbm, cache_ref, local_sem.at[1])
    load_cache.start()
    keep_w = pltpu.make_async_copy(w_out_hbm, w_row_hbm.at[b], local_sem.at[3])
    keep_w.start()
    rep = lax.axis_index("rep")
    copies = Copies(send_sem, recv_sem)
    greet(
        [device(a, b + k) for k in (1, 2, 3)] + [device(a + 1, b), device(a + 3, b)],
        [lax.rem(rep + k, reps) for k in range(1, reps)],
    )
    gather = Gather(copies, lambda i, j: rows.at[device(i, j)])
    mine = quarter(w_out_hbm.shape[1], lax.div(rep, 2), reps // 2)
    shards = RowRing(
        copies, w_row_hbm, w_out_hbm, mine, b, lambda j: tensor(device(a, j))
    )
    dec_rows[...] = jnp.zeros_like(dec_rows)
    dec_rows[: dec_ref.shape[0]] = dec_ref[...]
    load_x.wait()
    levels = Levels(copies, rep, reps)
    shards.pass_on()
    shards.finish()
    for k in (1, 2, 3):
        levels.spread(w_row_hbm.at[lax.rem(b + k, SIDE)])
    gather.begin()
    load_w.wait()
    dec = (
        lax.dot_general(w_ref[...], dec_rows[...], NT, preferred_element_type=jnp.float32)
        .astype(jnp.bfloat16)
        .astype(jnp.float32)
    )
    gather.first()
    load_cache.wait()
    hd = cache_ref.shape[2] // 2
    heads = cache_ref.shape[1]
    span = cache_ref.shape[3]
    lanes = dec.shape[1]
    lane = lax.broadcasted_iota(jnp.int32, (1, lanes), 1)
    position = rep * span + lax.broadcasted_iota(jnp.int32, (1, span), 1)

    def request(r, state):
        pick = lane == r
        column = jnp.sum(jnp.where(pick, dec, 0.0), axis=1, keepdims=True)
        valid = position < len_ref[r]
        out = []
        for h in range(heads):
            query = column[3 * hd * h : 3 * hd * h + hd]
            key = cache_ref[r, h, :hd].astype(jnp.float32)
            value = cache_ref[r, h, hd:].astype(jnp.float32)
            score = jnp.sum(key * query, axis=0, keepdims=True) * scale
            score = jnp.where(valid, score, NEG)
            high = jnp.max(score, axis=1, keepdims=True)
            weight = jnp.where(valid, jnp.exp(score - high), 0.0)
            total = jnp.sum(weight, axis=1, keepdims=True)
            mixed = jnp.sum(value * weight, axis=1, keepdims=True)
            highs, totals, mixes = state[h]
            out.append(
                (
                    jnp.where(pick, high, highs),
                    jnp.where(pick, total, totals),
                    jnp.where(pick, mixed, mixes),
                )
            )
        return tuple(out)

    empty = tuple(
        (
            jnp.full((1, lanes), NEG, jnp.float32),
            jnp.zeros((1, lanes), jnp.float32),
            jnp.zeros((hd, lanes), jnp.float32),
        )
        for _ in range(heads)
    )
    state = lax.fori_loop(0, cache_ref.shape[0], request, empty)
    for h in range(heads):
        states[rep, h, :hd] = state[h][2]
        states[rep, h, hd : hd + 8] = jnp.broadcast_to(state[h][0], (8, lanes))
        states[rep, h, hd + 8 : hd + 16] = jnp.broadcast_to(state[h][1], (8, lanes))
    sent = [
        copies.start(states.at[rep], states.at[rep], {"rep": lax.rem(rep + k, reps)})
        for k in range(1, reps)
    ]
    levels.pass_on()
    gather.middle()

    def tiles(start):
        core = lax.rem(rep, 2)
        for k in (0, 2):
            at = []
            for n in (k, k + 1):
                row_at = (1 - core) * lax.rem(a + start + n // 2, SIDE) + core * n
                side = (1 - core) * (n % 2) + core * lax.rem(lax.div(a, 2) + start // 2, 2)
                at.append(2 * row_at + side)
            block = jnp.concatenate(
                [rows[pl.ds(2 * t, 2)].reshape(2 * ROWS, rows.shape[2]) for t in at], axis=0
            )
            result = lax.dot_general(
                w_ref[...], block, NT, preferred_element_type=jnp.float32
            ).astype(out_ref.dtype)
            for n, t in enumerate(at):
                out_ref[:, pl.ds(pl.multiple_of(t * 2 * ROWS, 2 * ROWS), 2 * ROWS)] = result[
                    :, n * 2 * ROWS : (n + 1) * 2 * ROWS
                ]

    tiles(0)
    for copy in sent:
        copy.wait_recv()
    for h in range(heads):
        base = 3 * hd * h
        query, key, value = (dec[base + hd * k : base + hd * (k + 1)] for k in range(3))
        own = jnp.sum(query * key, axis=0, keepdims=True) * scale
        highest = own
        for k in range(reps):
            highest = jnp.maximum(highest, states[k, h, hd : hd + 1])
        own_weight = jnp.exp(own - highest)
        total, mixed = own_weight, own_weight * value
        for k in range(reps):
            factor = jnp.exp(states[k, h, hd : hd + 1] - highest)
            total = total + factor * states[k, h, hd + 8 : hd + 9]
            mixed = mixed + factor * states[k, h, :hd]
        attn_ref[:, hd * h : hd * (h + 1)] = (mixed / total).T[: attn_ref.shape[0]].astype(
            attn_ref.dtype
        )
    gather.last()
    tiles(2)
    levels.finish()
    keep_w.wait()
    copies.drain()


def attend(head, scale, offset, qkv_ref, kv_ref, seg_row, out_ref, q_ref, state):
    hd = q_ref.shape[1]
    span = seg_row.shape[1]
    block, key_block = 256, 1024
    early = span // 2 // block
    factor = scale * LOG2E
    q_ref[...] = qkv_ref[head, 0].astype(jnp.float32).T.astype(jnp.bfloat16)
    seg_keys = seg_row[...].astype(jnp.float32)
    seg_rows = jnp.broadcast_to(seg_keys, (8, span)).T[:, :1]
    states = [state[2 * i : 2 * i + 2] for i in range(early)]

    def rows(i):
        return slice(i * block, (i + 1) * block)

    def mix(weight, values):
        ones = jnp.ones((16, values.shape[1]), jnp.bfloat16)
        return lax.dot_general(
            weight.astype(jnp.bfloat16),
            jnp.concatenate([values, ones], axis=0),
            NT,
            preferred_element_type=jnp.float32,
        )

    for m_ref, acc_ref in states:
        m_ref[...] = jnp.full(m_ref.shape, NEG, jnp.float32)
        acc_ref[...] = jnp.zeros(acc_ref.shape, jnp.float32)

    @pl.loop(0, kv_ref.shape[2] // key_block)
    def _(j):
        at = pl.multiple_of(j * key_block, key_block)
        keys = kv_ref[head, :hd, pl.ds(at, key_block)]
        values = kv_ref[head, hd:, pl.ds(at, key_block)]
        seen = at + lax.broadcasted_iota(jnp.int32, (1, key_block), 1) < offset
        scores = [
            jnp.dot(q_ref[rows(i)], keys, preferred_element_type=jnp.float32)
            for i in range(early)
        ]
        for score, (m_ref, acc_ref) in zip(scores, states):
            score = jnp.where(seen, score, NEG)
            high = jnp.maximum(m_ref[...], jnp.max(score, axis=1, keepdims=True))
            decay = jnp.exp2((m_ref[...] - high) * factor)
            weight = jnp.exp2((score - high) * factor)
            m_ref[...] = high
            acc_ref[...] = acc_ref[...] * decay + mix(weight, values)

    for i in range(span // block):
        low = max(0, (i - early) * block)
        high = (i + 1) * block
        seg_q = seg_rows[rows(i)]
        score = jnp.dot(
            q_ref[rows(i)], qkv_ref[head, 1, :, low:high], preferred_element_type=jnp.float32
        )
        shape = (block, high - low)
        query_at = i * block + lax.broadcasted_iota(jnp.int32, shape, 0)
        key_at = low + lax.broadcasted_iota(jnp.int32, shape, 1)
        seen = (seg_keys[:, low:high] == seg_q) & (key_at <= query_at)
        score = jnp.where(seen, score, NEG)
        values = qkv_ref[head, 2, :, low:high]
        peak = jnp.max(score, axis=1, keepdims=True)
        if i < early:
            m_ref, acc_ref = states[i]
            keep = (seg_q == 0) & (offset > 0)
            before = jnp.where(keep, m_ref[...], NEG)
            peak = jnp.maximum(peak, before)
            decay = jnp.where(keep, jnp.exp2((before - peak) * factor), 0.0)
        weight = jnp.exp2((score - peak) * factor)
        mixed = mix(weight, values)
        if i < early:
            mixed = mixed + acc_ref[...] * decay
        out_ref[rows(i), head * hd : (head + 1) * hd] = (
            mixed[:, :hd] / mixed[:, hd : hd + 1]
        ).astype(out_ref.dtype)


def tail_kernel(
    scale,
    reps,
    offset_ref,
    seg_row,
    dec_attn_ref,
    x_dec_ref,
    up_bias_ref,
    biases_ref,
    gains_ref,
    shifts_ref,
    qkv_hbm,
    kv_hbm,
    x_hbm,
    w_row_hbm,
    w_up_hbm,
    w_down_hbm,
    w_next_hbm,
    result_hbm,
    out_ref,
    dec_out_ref,
    dec_next_ref,
    qkv_ref,
    kv_ref,
    x_ref,
    w_row_ref,
    w_up_ref,
    w_down_ref,
    w_next_ref,
    attn_ref,
    heads_ref,
    columns_ref,
    result_ref,
    slabs,
    parts,
    far,
    near,
    row,
    row_far,
    row_near,
    over_x,
    over_y,
    q_ref,
    m0_ref,
    acc0_ref,
    m1_ref,
    acc1_ref,
    local_sem,
    send_sem,
    recv_sem,
):
    y, x, a, b, device = place()
    loads = []
    for k, (source, target) in enumerate(
        (
            (qkv_hbm, qkv_ref),
            (kv_hbm, kv_ref),
            (w_row_hbm, w_row_ref),
            (x_hbm, x_ref),
            (w_next_hbm, w_next_ref.at[b]),
            (w_up_hbm, w_up_ref),
            (w_down_hbm, w_down_ref),
        )
    ):
        loads.append(pltpu.make_async_copy(source, target, local_sem.at[k]))
        loads[-1].start()
    load_qkv, load_kv, load_row, load_x, load_next, load_up, load_down = loads
    copies = Copies(send_sem, recv_sem)
    rep = lax.axis_index("rep")
    plane, planes = lax.div(rep, 2), reps // 2
    columns, width = w_next_hbm.shape

    greet(
        [SIDE * y + lax.rem(x + k, SIDE) for k in (1, 2, 3)]
        + [SIDE * lax.rem(y + k, SIDE) + x for k in (1, 2, 3)],
        [lax.rem(rep + 2 * k, reps) for k in (1, planes - 1)],
    )
    chunk = (SIDE, ROWS, width)
    load_row.wait()
    dec_sum = SmallSum(copies, over_x.at[0], over_y.at[0])
    dec_sum.begin(
        jnp.dot(dec_attn_ref[...], w_row_ref[b], preferred_element_type=jnp.float32)
    )
    shards = RowRing(
        copies,
        w_next_ref,
        w_next_hbm,
        quarter(width, plane, planes),
        b,
        lambda j: tensor(device(a, j)),
    )
    attn_ref[...] = jnp.zeros_like(attn_ref)
    result_ref[...] = jnp.zeros_like(result_ref)
    load_qkv.wait()
    load_kv.wait()
    state = (m0_ref, acc0_ref, m1_ref, acc1_ref)
    offset = offset_ref[0]
    heads = qkv_ref.shape[0]
    for head in range(heads):
        attend(head, scale, offset, qkv_ref, kv_ref, seg_row, attn_ref, q_ref, state)
        if head == 0:
            dec_sum.middle()
            shards.pass_on()

    def tokens(i, j):
        return attn_ref.at[pl.ds(pl.multiple_of(device(i, j) * ROWS, ROWS), ROWS)]

    swaps = [
        copies.start(tokens(i, b + k), heads_ref.at[b, i], tensor(device(a, b + k)))
        for k in (2, 1, 3)
        for i in range(SIDE)
    ]
    for i in range(SIDE):
        heads_ref[b, i] = tokens(i, b)[...]
    for swap in swaps:
        swap.wait_recv()
    ring = RingSum(
        copies, row.at[0], row_far.at[0], row_near.at[0], a, lambda i: tensor(device(i, b))
    )
    depth = w_row_ref.shape[1]
    step = width // 5
    for n in range(0, width, step):
        total = sum(
            jnp.dot(
                heads_ref[j].reshape(SIDE * ROWS, heads_ref.shape[3])[:, :depth],
                w_row_ref[j, :, n : n + step],
                preferred_element_type=jnp.float32,
            )
            for j in range(SIDE)
        )
        row[0, :, :, n : n + step] = total.astype(jnp.bfloat16).reshape(SIDE, ROWS, step)
    ring.send_far()
    ring.send_next()
    ring.send_prev()
    ring.pass_on()
    shards.finish()
    levels = Levels(copies, rep, reps)
    for k in (1, 2, 3):
        levels.spread(w_next_ref.at[lax.rem(b + k, SIDE)])
    dec_first = layer_norm(
        x_dec_ref[...].astype(jnp.float32) + dec_sum.finish() + biases_ref[0:1],
        gains_ref[0:1],
        shifts_ref[0:1],
    ).astype(jnp.bfloat16)
    own = row[0, a].astype(jnp.float32)
    load_x.wait()
    attn_sum = ring.finish(own)
    first = layer_norm(
        x_ref[...].astype(jnp.float32) + attn_sum + biases_ref[0:1], gains_ref[0:1], shifts_ref[0:1]
    ).astype(jnp.bfloat16)

    def slab(i, j):
        return slabs.at[lax.rem(i, SIDE), lax.rem(j, SIDE)]

    slab(a, b)[...] = first
    gather = Gather(copies, slab)
    gather.begin()
    load_up.wait()
    load_down.wait()

    def mlp(value):
        inner = jnp.dot(value, w_up_ref[...], preferred_element_type=jnp.float32)
        inner = inner + up_bias_ref[...][None, :]
        hidden = (0.5 * inner * (1.0 + lax.erf(inner * 0.7071067811865476))).astype(jnp.bfloat16)
        return jnp.dot(hidden, w_down_ref[...], preferred_element_type=jnp.float32)

    def mlp_share(i):
        at = lax.rem(i, SIDE)
        parts[at] = (
            mlp(slabs[at].reshape(SIDE * ROWS, width)).astype(jnp.bfloat16).reshape(chunk)
        )

    scatter = Scatter(copies, parts, far, near, row.at[1], row_far.at[1], row_near.at[1])
    gather.first()
    mlp_share(a)
    dec_sum = SmallSum(copies, over_x.at[1], over_y.at[1])
    dec_sum.begin(mlp(dec_first))
    gather.middle()
    mlp_share(a + 1)
    mlp_share(a + 3)
    scatter.send_near()
    gather.last()
    mlp_share(a + 2)
    scatter.send_far()
    levels.pass_on()
    scatter.pass_on()
    dec_sum.middle()
    mlp_sum = scatter.finish()
    second = layer_norm(
        first.astype(jnp.float32) + mlp_sum + biases_ref[1:2], gains_ref[1:2], shifts_ref[1:2]
    ).astype(jnp.bfloat16)
    out_ref[...] = second
    columns_ref[a] = second
    RingGather(copies, columns_ref, a, lambda i: tensor(device(i, b))).run()
    levels.finish()
    load_next.wait()
    keeps = []
    for k in (2, 1, 3, 0):
        j = lax.rem(b + k, SIDE)
        result_ref[j, :, :, :columns] = (
            lax.dot_general(
                columns_ref[...].reshape(SIDE * ROWS, width),
                w_next_ref[j],
                NT,
                preferred_element_type=jnp.float32,
            )
            .astype(jnp.bfloat16)
            .reshape(SIDE, ROWS, columns)
        )
        for i in range(SIDE):
            source, target = result_ref.at[j, i], result_hbm.at[device(i, b)]
            if k:
                keeps.append(copies.start(source, target, tensor(device(a, j))))
            else:
                local = pltpu.make_async_copy(source, target, local_sem.at[i])
                local.start()
                loads.append(local)
    dec_out = layer_norm(
        dec_first.astype(jnp.float32) + dec_sum.finish() + biases_ref[1:2],
        gains_ref[1:2],
        shifts_ref[1:2],
    ).astype(jnp.bfloat16)
    dec_out_ref[...] = dec_out
    dec_next_ref[...] = lax.dot_general(
        dec_out, w_next_ref[b], NT, preferred_element_type=jnp.float32
    ).astype(jnp.bfloat16)
    for copy in keeps:
        copy.wait_recv()
    for local in loads[-SIDE:]:
        local.wait()
    copies.drain()


def layout_kernel(
    result_ref, own_ref, dec_ref, dec_result_ref, next_ref, out_ref, dec_out_ref, dec_next_ref
):
    columns, lanes = next_ref.shape[0], result_ref.shape[2]
    same = lax.broadcasted_iota(jnp.int32, (columns, lanes), 0) == lax.broadcasted_iota(
        jnp.int32, (columns, lanes), 1
    )
    next_ref[...] = lax.dot_general(
        same.astype(jnp.float32).astype(jnp.bfloat16),
        result_ref[...].reshape(SIDE * ROWS, lanes),
        NT,
        preferred_element_type=jnp.float32,
    ).astype(next_ref.dtype)

    @pl.when(pl.program_id(0) == 0)
    def _():
        out_ref[...] = own_ref[...]
        dec_out_ref[...] = dec_ref[...]
        dec_next_ref[...] = dec_result_ref[...]


def per_device(
    reps,
    x_pre,
    x_dec,
    prefix_kv,
    cache_kv,
    dec_len,
    offsets,
    segments,
    w_qkv,
    w_out,
    w_up,
    up_bias,
    w_down,
    biases,
    gains,
    shifts,
    w_next,
):
    heads = prefix_kv.shape[2]
    hd = prefix_kv.shape[3] // 2
    span = segments.shape[1]
    width = x_pre.shape[1]
    decodes = x_dec.shape[0]
    columns = w_qkv.shape[1]
    units = w_up.shape[1]
    scale = hd ** (-0.5)
    bf16, f32 = jnp.bfloat16, jnp.float32
    shape = jax.ShapeDtypeStruct
    whole = pl.BlockSpec(memory_space=VMEM)
    scalars = pl.BlockSpec(memory_space=pltpu.SMEM)
    anywhere = pl.BlockSpec(memory_space=pltpu.HBM)
    group = SIDE * SIDE

    cache_t = cache_kv.transpose(0, 2, 3, 1)
    n_copies = 16 + reps - 1 + 6 + (SIDE - 1) * 4
    qkv_t, dec_attn, w_row = pl.pallas_call(
        functools.partial(project_kernel, reps, scale),
        out_shape=(
            shape((columns, span), bf16),
            shape((decodes, heads * hd), bf16),
            shape((SIDE,) + w_out.shape, bf16),
        ),
        in_specs=[scalars, whole] + [anywhere] * 4,
        out_specs=(whole, whole, anywhere),
        scratch_shapes=[
            VMEM((group, ROWS, width), bf16),
            VMEM((128, width), bf16),
            VMEM((columns, width), bf16),
            VMEM(cache_t.shape, bf16),
            VMEM((reps, heads, hd + 16, 128), f32),
            pltpu.SemaphoreType.DMA((4,)),
            pltpu.SemaphoreType.DMA((n_copies,)),
            pltpu.SemaphoreType.DMA((n_copies,)),
        ],
        compiler_params=pltpu.CompilerParams(
            collective_id=0, has_side_effects=True, vmem_limit_bytes=62 << 20
        ),
        name="project",
    )(dec_len, x_dec, x_pre, w_qkv.T, cache_t, w_out)

    n_copies = 100
    lanes = 512
    result, own, dec_own, dec_result = pl.pallas_call(
        functools.partial(tail_kernel, scale, reps),
        out_shape=(
            shape((group, ROWS, lanes), bf16),
            shape((ROWS, width), bf16),
            shape((decodes, width), bf16),
            shape((decodes, columns), bf16),
        ),
        in_specs=[scalars] + [whole] * 7 + [anywhere] * 7,
        out_specs=(anywhere, whole, whole, whole),
        scratch_shapes=[
            VMEM((heads, 3, hd, span), bf16),
            VMEM((heads, 2 * hd, prefix_kv.shape[1]), bf16),
            VMEM((ROWS, width), bf16),
            VMEM((SIDE,) + w_out.shape, bf16),
            VMEM((width, units), bf16),
            VMEM((units, width), bf16),
            VMEM((SIDE, columns, width), bf16),
            VMEM((span, 256), bf16),
            VMEM((SIDE, SIDE, ROWS, 256), bf16),
            VMEM((SIDE, ROWS, width), bf16),
            VMEM((SIDE, SIDE, ROWS, lanes), bf16),
            VMEM((SIDE, SIDE, ROWS, width), bf16),
            VMEM((SIDE, SIDE, ROWS, width), bf16),
            VMEM((2, 2, ROWS, width), bf16),
            VMEM((2, SIDE, ROWS, width), bf16),
            VMEM((2, SIDE, ROWS, width), bf16),
            VMEM((2, 2, ROWS // 2, width), bf16),
            VMEM((2, 2, ROWS, width), bf16),
            VMEM((2, SIDE, decodes, width), bf16),
            VMEM((2, SIDE, decodes, width), bf16),
            VMEM((span, hd), bf16),
            *([VMEM((256, 1), f32), VMEM((256, hd + 16), f32)] * 2),
            pltpu.SemaphoreType.DMA((8,)),
            pltpu.SemaphoreType.DMA((n_copies,)),
            pltpu.SemaphoreType.DMA((n_copies,)),
        ],
        compiler_params=pltpu.CompilerParams(
            collective_id=1, has_side_effects=True, vmem_limit_bytes=62 << 20
        ),
        name="tail",
    )(
        offsets,
        segments,
        dec_attn,
        x_dec,
        up_bias,
        biases,
        gains,
        shifts,
        qkv_t.reshape(heads, 3, hd, span),
        prefix_kv[0].transpose(1, 2, 0),
        x_pre,
        w_row,
        w_up,
        w_down,
        w_next.T,
    )

    next_t, layer_out, dec_out, dec_next = pl.pallas_call(
        layout_kernel,
        grid=(SIDE,),
        out_shape=(
            shape((columns, span), bf16),
            shape((ROWS, width), bf16),
            shape((decodes, width), bf16),
            shape((decodes, columns), bf16),
        ),
        in_specs=[
            pl.BlockSpec((SIDE, ROWS, lanes), lambda i: (i, 0, 0)),
            pl.BlockSpec((ROWS, width), lambda i: (0, 0)),
            pl.BlockSpec((decodes, width), lambda i: (0, 0)),
            pl.BlockSpec((decodes, columns), lambda i: (0, 0)),
        ],
        out_specs=(
            pl.BlockSpec((columns, SIDE * ROWS), lambda i: (0, i)),
            pl.BlockSpec((ROWS, width), lambda i: (0, 0)),
            pl.BlockSpec((decodes, width), lambda i: (0, 0)),
            pl.BlockSpec((decodes, columns), lambda i: (0, 0)),
        ),
        compiler_params=pltpu.CompilerParams(
            dimension_semantics=("arbitrary",), vmem_limit_bytes=62 << 20
        ),
        name="layout",
    )(result, own, dec_own, dec_result)
    return layer_out, next_t.T, dec_out, dec_next


def solution(mesh):
    placed = (
        P(("rep", "tensor"), None),
        P(),
        P("rep", None, "tensor", None),
        P(None, "rep", "tensor", None),
        P(),
        P("rep"),
        P("rep", None),
        P(None, "tensor"),
        P("tensor", None),
        P(None, "tensor"),
        P("tensor"),
        P("tensor", None),
        P(),
        P(),
        P(),
        P(None, "tensor"),
    )
    return jax.shard_map(
        functools.partial(per_device, mesh.shape["rep"]),
        mesh=mesh,
        in_specs=placed,
        out_specs=(P(("rep", "tensor"), None), P("rep", "tensor"), P(), P(None, "tensor")),
        check_vma=False,
    )
```

```python
import functools

import jax
import jax.numpy as jnp
from jax import lax
from jax.experimental import pallas as pl
from jax.experimental.pallas import tpu as pltpu
from jax.sharding import PartitionSpec as P

MESH = pl.DeviceIdType.MESH
NEG = -1e30
LOG2E = 1.4426950408889634
SIDE = 4
ROWS = 64
VMEM = pltpu.VMEM
NT = (((1,), (1,)), ((), ()))


def place():
    t = lax.axis_index("tensor")
    core = lax.rem(lax.axis_index("rep"), 2)
    y, x = lax.div(t, SIDE), lax.rem(t, SIDE)
    major = y * (1 - core) + x * core
    minor = x * (1 - core) + y * core
    step_major, step_minor = SIDE - (SIDE - 1) * core, 1 + (SIDE - 1) * core

    def device(i, j):
        return lax.rem(i, SIDE) * step_major + lax.rem(j, SIDE) * step_minor

    return y, x, major, minor, device


class Copies:
    def __init__(self, send, recv):
        self.send, self.recv, self.used, self.all = send, recv, 0, []

    def start(self, src, dst, where):
        copy = pltpu.make_async_remote_copy(
            src_ref=src,
            dst_ref=dst,
            send_sem=self.send.at[self.used],
            recv_sem=self.recv.at[self.used],
            device_id=where,
            device_id_type=MESH,
        )
        copy.start()
        self.used += 1
        self.all.append(copy)
        return copy

    def drain(self):
        for copy in self.all:
            copy.wait_send()


def tensor(t):
    return {"tensor": t}


def greet(tensor_peers, rep_peers=()):
    barrier = pltpu.get_barrier_semaphore()
    for t in tensor_peers:
        pl.semaphore_signal(barrier, inc=1, device_id=tensor(t), device_id_type=MESH)
    for r in rep_peers:
        pl.semaphore_signal(barrier, inc=1, device_id={"rep": r}, device_id_type=MESH)
    pl.semaphore_wait(barrier, len(tensor_peers) + len(rep_peers))


class Gather:
    def __init__(self, copies, at, own=None):
        y, x, self.a, self.b, self.device = place()
        self.copies, self.at, self.own = copies, at, own

    def go(self, i, j, ti, tj):
        return self.copies.start(self.at(i, j), self.at(i, j), tensor(self.device(ti, tj)))

    def begin(self):
        a, b = self.a, self.b
        own = self.at(a, b) if self.own is None else self.own
        self.right, self.left, up, down = (
            self.copies.start(own, self.at(a, b), tensor(self.device(i, j)))
            for i, j in ((a, b + 1), (a, b + 3), (a + 1, b), (a + 3, b))
        )
        self.up, self.down = [up], [down]

    def spread(self, j):
        a, b = self.a, self.b
        self.up.append(self.go(a, j, a + 1, b))
        self.down.append(self.go(a, j, a + 3, b))

    def half(self, i, j, part):
        return self.at(i, j).at[pl.ds(part * (ROWS // 2), ROWS // 2)]

    def first(self):
        a, b = self.a, self.b
        self.right.wait_recv()
        one = self.half(a, b + 3, 0)
        far_one = self.copies.start(one, one, tensor(self.device(a, b + 1)))
        self.spread(b + 3)
        self.left.wait_recv()
        two = self.half(a, b + 1, 1)
        far_two = self.copies.start(two, two, tensor(self.device(a, b + 3)))
        self.spread(b + 1)
        far_one.wait_recv()
        far_two.wait_recv()
        self.spread(b + 2)

    def middle(self):
        a, b = self.a, self.b
        self.up[0].wait_recv()
        self.far = [self.go(a + 3, b, a + 1, b)]
        self.down[1].wait_recv()
        self.far.append(self.go(a + 1, b + 3, a + 3, b))
        self.down[2].wait_recv()
        self.far.append(self.go(a + 1, b + 1, a + 3, b))
        self.up[3].wait_recv()
        self.far.append(self.go(a + 3, b + 2, a + 1, b))
        self.up[1].wait_recv()
        self.up[2].wait_recv()
        self.down[0].wait_recv()
        self.down[3].wait_recv()

    def last(self):
        for copy in self.far:
            copy.wait_recv()


class RingSum:
    def __init__(self, copies, row, far, near, index, to):
        self.copies, self.slabs, self.far, self.near = copies, row, far, near
        self.c, self.next, self.prev = index, to(index + 1), to(index + 3)
        half = ROWS // 2
        self.top, self.low = pl.ds(0, half), pl.ds(half, half)

    def row(self, k):
        return self.slabs.at[lax.rem(self.c + k, SIDE)]

    def send_far(self):
        self.next_far = self.copies.start(self.row(2).at[self.top], self.far.at[0], self.next)
        self.prev_far = self.copies.start(self.row(2).at[self.low], self.far.at[1], self.prev)

    def send_next(self):
        self.next_near = self.copies.start(
            self.row(1).at[self.low], self.near.at[0, self.low], self.next
        )

    def send_prev(self):
        self.prev_near = self.copies.start(
            self.row(3).at[self.top], self.near.at[1, self.top], self.prev
        )

    def pass_on(self):
        self.next_far.wait_recv()
        add_into(self.row(1).at[self.top], self.far[0])
        self.next_sum = self.copies.start(
            self.row(1).at[self.top], self.near.at[0, self.top], self.next
        )
        self.prev_far.wait_recv()
        add_into(self.row(3).at[self.low], self.far[1])
        self.prev_sum = self.copies.start(
            self.row(3).at[self.low], self.near.at[1, self.low], self.prev
        )

    def finish(self, own):
        for copy in (self.next_near, self.prev_near, self.next_sum, self.prev_sum):
            copy.wait_recv()
        return own + self.near[0].astype(jnp.float32) + self.near[1].astype(jnp.float32)


class RingGather:
    def __init__(self, copies, slabs, index, to):
        self.copies, self.slabs, self.c = copies, slabs, index
        self.next, self.prev = to(index + 1), to(index + 3)
        half = ROWS // 2
        self.top, self.low = pl.ds(0, half), pl.ds(half, half)

    def go(self, k, part, where):
        piece = self.slabs.at[lax.rem(self.c + k, SIDE)].at[part]
        return self.copies.start(piece, piece, where)

    def run(self):
        first = (self.go(0, self.top, self.next), self.go(0, self.low, self.prev))
        second = (self.go(0, self.low, self.next), self.go(0, self.top, self.prev))
        first[0].wait_recv()
        far = [self.go(3, self.top, self.next)]
        first[1].wait_recv()
        far.append(self.go(1, self.low, self.prev))
        for copy in (*second, *far):
            copy.wait_recv()


def quarter(width, plane, planes):
    size = width // planes
    return pl.ds(pl.multiple_of(lax.rem(plane, planes) * size, 128), size)


class Levels:
    def __init__(self, copies, rep, reps):
        self.copies, self.plane, self.planes = copies, lax.div(rep, 2), reps // 2
        self.above, self.below = (
            {"rep": lax.rem(rep + 2 * k, reps)} for k in (1, self.planes - 1)
        )
        self.sent = []

    def share(self, array, k):
        return array.at[:, quarter(array.shape[1], self.plane + k, self.planes)]

    def spread(self, array):
        piece = self.share(array, 0)
        self.sent.append(
            (
                array,
                self.copies.start(piece, piece, self.above),
                self.copies.start(piece, piece, self.below),
            )
        )

    def pass_on(self):
        self.far = []
        for array, from_below, from_above in self.sent:
            half = array.shape[0] // 2
            from_below.wait_recv()
            piece = self.share(array, self.planes - 1).at[pl.ds(0, half)]
            self.far.append(self.copies.start(piece, piece, self.above))
            from_above.wait_recv()
            piece = self.share(array, 1).at[pl.ds(half, half)]
            self.far.append(self.copies.start(piece, piece, self.below))

    def finish(self):
        for copy in self.far:
            copy.wait_recv()


class RowRing:
    def __init__(self, copies, shards, own, columns, index, to):
        self.copies, self.shards, self.columns, self.c = copies, shards, columns, index
        self.next, self.prev = to(index + 1), to(index + 3)
        half = own.shape[0] // 2
        self.parts = pl.ds(0, half), pl.ds(half, half)
        top, low = (own.at[part, columns] for part in self.parts)
        self.first = (self.go(0, 0, self.next, top), self.go(0, 1, self.prev, low))
        self.second = (self.go(0, 1, self.next, low), self.go(0, 0, self.prev, top))

    def go(self, k, part, where, source=None):
        piece = self.shards.at[lax.rem(self.c + k, SIDE), self.parts[part], self.columns]
        return self.copies.start(piece if source is None else source, piece, where)

    def pass_on(self):
        self.first[0].wait_recv()
        self.far = [self.go(3, 0, self.next)]
        self.first[1].wait_recv()
        self.far.append(self.go(1, 1, self.prev))

    def finish(self):
        for copy in (*self.second, *self.far):
            copy.wait_recv()


def add_into(ref, value):
    ref[...] = (ref[...].astype(jnp.float32) + value.astype(jnp.float32)).astype(ref.dtype)


class Scatter:
    def __init__(self, copies, parts, far, near, row, row_far, row_near):
        y, x, a, b, self.device = place()
        self.a, self.b = a, b
        self.copies, self.parts, self.far, self.near = copies, parts, far, near
        self.ring = RingSum(
            copies, row, row_far, row_near, b, lambda j: tensor(self.device(a, j))
        )
        self.above, self.below = tensor(self.device(a + 1, b)), tensor(self.device(a + 3, b))
        self.ups, self.downs = (b + 2, b + 1), (b + 3, b)

    def part(self, i, j):
        return self.parts.at[lax.rem(i, SIDE), lax.rem(j, SIDE)]

    def landing(self, side, j):
        return self.near.at[side, lax.rem(j, SIDE)]

    def send_far(self):
        self.far_up, self.far_down = [], []
        for k in range(2):
            self.far_up.append(
                self.copies.start(self.part(self.a + 2, self.ups[k]), self.far.at[0, k], self.above)
            )
            self.far_down.append(
                self.copies.start(
                    self.part(self.a + 2, self.downs[k]), self.far.at[1, k], self.below
                )
            )

    def send_near(self):
        self.near_up, self.near_down = [], []
        for k in range(2):
            self.near_up.append(
                self.copies.start(
                    self.part(self.a + 1, self.downs[k]),
                    self.landing(0, self.downs[k]),
                    self.above,
                )
            )
            self.near_down.append(
                self.copies.start(
                    self.part(self.a + 3, self.ups[k]), self.landing(1, self.ups[k]), self.below
                )
            )

    def pass_on(self):
        self.sum_up, self.sum_down = [], []
        for k in range(2):
            self.far_up[k].wait_recv()
            add_into(self.part(self.a + 1, self.ups[k]), self.far[0, k])
            self.sum_up.append(
                self.copies.start(
                    self.part(self.a + 1, self.ups[k]), self.landing(0, self.ups[k]), self.above
                )
            )
            self.far_down[k].wait_recv()
            add_into(self.part(self.a + 3, self.downs[k]), self.far[1, k])
            self.sum_down.append(
                self.copies.start(
                    self.part(self.a + 3, self.downs[k]),
                    self.landing(1, self.downs[k]),
                    self.below,
                )
            )

    def total(self, j):
        at = lax.rem(j, SIDE)
        return (
            self.parts[self.a, at].astype(jnp.float32)
            + self.near[0, at].astype(jnp.float32)
            + self.near[1, at].astype(jnp.float32)
        )

    def finish(self):
        ring, b = self.ring, self.b
        self.sum_up[0].wait_recv()
        self.near_down[0].wait_recv()
        ring.row(2)[...] = self.total(b + 2).astype(jnp.bfloat16)
        ring.send_far()
        self.near_up[0].wait_recv()
        self.sum_down[0].wait_recv()
        ring.row(3)[...] = self.total(b + 3).astype(jnp.bfloat16)
        ring.send_prev()
        self.sum_up[1].wait_recv()
        self.near_down[1].wait_recv()
        ring.row(1)[...] = self.total(b + 1).astype(jnp.bfloat16)
        ring.send_next()
        ring.pass_on()
        self.near_up[1].wait_recv()
        self.sum_down[1].wait_recv()
        return ring.finish(self.total(b))


class SmallSum:
    def __init__(self, copies, over_x, over_y):
        t = lax.axis_index("tensor")
        self.y, self.x = lax.div(t, SIDE), lax.rem(t, SIDE)
        self.copies, self.over_x, self.over_y = copies, over_x, over_y

    def begin(self, value):
        self.over_x[self.x] = value.astype(jnp.bfloat16)
        mine = self.over_x.at[self.x]
        self.sent = [
            self.copies.start(
                mine, mine, tensor(SIDE * self.y + lax.rem(self.x + k, SIDE))
            )
            for k in (1, 2, 3)
        ]

    def middle(self):
        for copy in self.sent:
            copy.wait_recv()
        self.over_y[self.y] = sum(
            self.over_x[k].astype(jnp.float32) for k in range(SIDE)
        ).astype(jnp.bfloat16)
        mine = self.over_y.at[self.y]
        self.sent = [
            self.copies.start(
                mine, mine, tensor(SIDE * lax.rem(self.y + k, SIDE) + self.x)
            )
            for k in (1, 2, 3)
        ]

    def finish(self):
        for copy in self.sent:
            copy.wait_recv()
        return sum(self.over_y[k].astype(jnp.float32) for k in range(SIDE))


def layer_norm(values, gain_row, shift_row):
    average = jnp.mean(values, axis=-1, keepdims=True)
    centred = values - average
    spread = jnp.mean(centred * centred, axis=-1, keepdims=True)
    return centred * lax.rsqrt(spread + 1e-05) * gain_row + shift_row


def project_kernel(
    reps,
    scale,
    len_ref,
    dec_ref,
    x_hbm,
    w_hbm,
    cache_hbm,
    w_out_hbm,
    out_ref,
    attn_ref,
    w_row_hbm,
    rows,
    dec_rows,
    w_ref,
    cache_ref,
    states,
    local_sem,
    send_sem,
    recv_sem,
):
    y, x, a, b, device = place()
    load_x = pltpu.make_async_copy(x_hbm, rows.at[device(a, b)], local_sem.at[2])
    load_x.start()
    load_w = pltpu.make_async_copy(w_hbm, w_ref, local_sem.at[0])
    load_w.start()
    load_cache = pltpu.make_async_copy(cache_hbm, cache_ref, local_sem.at[1])
    load_cache.start()
    keep_w = pltpu.make_async_copy(w_out_hbm, w_row_hbm.at[b], local_sem.at[3])
    keep_w.start()
    rep = lax.axis_index("rep")
    copies = Copies(send_sem, recv_sem)
    greet(
        [device(a, b + k) for k in (1, 2, 3)] + [device(a + 1, b), device(a + 3, b)],
        [lax.rem(rep + k, reps) for k in range(1, reps)],
    )
    gather = Gather(copies, lambda i, j: rows.at[device(i, j)])
    mine = quarter(w_out_hbm.shape[1], lax.div(rep, 2), reps // 2)
    shards = RowRing(
        copies, w_row_hbm, w_out_hbm, mine, b, lambda j: tensor(device(a, j))
    )
    dec_rows[...] = jnp.zeros_like(dec_rows)
    dec_rows[: dec_ref.shape[0]] = dec_ref[...]
    load_x.wait()
    levels = Levels(copies, rep, reps)
    shards.pass_on()
    shards.finish()
    for k in (1, 2, 3):
        levels.spread(w_row_hbm.at[lax.rem(b + k, SIDE)])
    gather.begin()
    load_w.wait()
    dec = (
        lax.dot_general(w_ref[...], dec_rows[...], NT, preferred_element_type=jnp.float32)
        .astype(jnp.bfloat16)
        .astype(jnp.float32)
    )
    gather.first()
    load_cache.wait()
    hd = cache_ref.shape[2] // 2
    heads = cache_ref.shape[1]
    span = cache_ref.shape[3]
    lanes = dec.shape[1]
    lane = lax.broadcasted_iota(jnp.int32, (1, lanes), 1)
    position = rep * span + lax.broadcasted_iota(jnp.int32, (1, span), 1)

    def request(r, state):
        pick = lane == r
        column = jnp.sum(jnp.where(pick, dec, 0.0), axis=1, keepdims=True)
        valid = position < len_ref[r]
        out = []
        for h in range(heads):
            query = column[3 * hd * h : 3 * hd * h + hd]
            key = cache_ref[r, h, :hd].astype(jnp.float32)
            value = cache_ref[r, h, hd:].astype(jnp.float32)
            score = jnp.sum(key * query, axis=0, keepdims=True) * scale
            score = jnp.where(valid, score, NEG)
            high = jnp.max(score, axis=1, keepdims=True)
            weight = jnp.where(valid, jnp.exp(score - high), 0.0)
            total = jnp.sum(weight, axis=1, keepdims=True)
            mixed = jnp.sum(value * weight, axis=1, keepdims=True)
            highs, totals, mixes = state[h]
            out.append(
                (
                    jnp.where(pick, high, highs),
                    jnp.where(pick, total, totals),
                    jnp.where(pick, mixed, mixes),
                )
            )
        return tuple(out)

    empty = tuple(
        (
            jnp.full((1, lanes), NEG, jnp.float32),
            jnp.zeros((1, lanes), jnp.float32),
            jnp.zeros((hd, lanes), jnp.float32),
        )
        for _ in range(heads)
    )
    state = lax.fori_loop(0, cache_ref.shape[0], request, empty)
    for h in range(heads):
        states[rep, h, :hd] = state[h][2]
        states[rep, h, hd : hd + 8] = jnp.broadcast_to(state[h][0], (8, lanes))
        states[rep, h, hd + 8 : hd + 16] = jnp.broadcast_to(state[h][1], (8, lanes))
    sent = [
        copies.start(states.at[rep], states.at[rep], {"rep": lax.rem(rep + k, reps)})
        for k in range(1, reps)
    ]
    levels.pass_on()
    gather.middle()

    def tiles(start):
        core = lax.rem(rep, 2)
        for k in (0, 2):
            at = []
            for n in (k, k + 1):
                row_at = (1 - core) * lax.rem(a + start + n // 2, SIDE) + core * n
                side = (1 - core) * (n % 2) + core * lax.rem(lax.div(a, 2) + start // 2, 2)
                at.append(2 * row_at + side)
            block = jnp.concatenate(
                [rows[pl.ds(2 * t, 2)].reshape(2 * ROWS, rows.shape[2]) for t in at], axis=0
            )
            result = lax.dot_general(
                w_ref[...], block, NT, preferred_element_type=jnp.float32
            ).astype(out_ref.dtype)
            for n, t in enumerate(at):
                out_ref[:, pl.ds(pl.multiple_of(t * 2 * ROWS, 2 * ROWS), 2 * ROWS)] = result[
                    :, n * 2 * ROWS : (n + 1) * 2 * ROWS
                ]

    tiles(0)
    for copy in sent:
        copy.wait_recv()
    for h in range(heads):
        base = 3 * hd * h
        query, key, value = (dec[base + hd * k : base + hd * (k + 1)] for k in range(3))
        own = jnp.sum(query * key, axis=0, keepdims=True) * scale
        highest = own
        for k in range(reps):
            highest = jnp.maximum(highest, states[k, h, hd : hd + 1])
        own_weight = jnp.exp(own - highest)
        total, mixed = own_weight, own_weight * value
        for k in range(reps):
            factor = jnp.exp(states[k, h, hd : hd + 1] - highest)
            total = total + factor * states[k, h, hd + 8 : hd + 9]
            mixed = mixed + factor * states[k, h, :hd]
        attn_ref[:, hd * h : hd * (h + 1)] = (mixed / total).T[: attn_ref.shape[0]].astype(
            attn_ref.dtype
        )
    gather.last()
    tiles(2)
    levels.finish()
    keep_w.wait()
    copies.drain()


def attend(head, scale, offset, qkv_ref, kv_ref, seg_row, out_ref, q_ref, state):
    hd = q_ref.shape[1]
    span = seg_row.shape[1]
    block, key_block = 256, 2048
    early = span // 2 // block
    factor = scale * LOG2E
    q_ref[...] = qkv_ref[head, 0].astype(jnp.float32).T.astype(jnp.bfloat16)
    seg_keys = seg_row[...].astype(jnp.float32)
    seg_rows = jnp.broadcast_to(seg_keys, (8, span)).T[:, :1]
    states = [state[2 * i : 2 * i + 2] for i in range(early)]

    def rows(i):
        return slice(i * block, (i + 1) * block)

    def mix(weight, values):
        ones = jnp.ones((16, values.shape[1]), jnp.bfloat16)
        return lax.dot_general(
            weight.astype(jnp.bfloat16),
            jnp.concatenate([values, ones], axis=0),
            NT,
            preferred_element_type=jnp.float32,
        )

    for m_ref, acc_ref in states:
        m_ref[...] = jnp.full(m_ref.shape, NEG, jnp.float32)
        acc_ref[...] = jnp.zeros(acc_ref.shape, jnp.float32)

    @pl.loop(0, kv_ref.shape[2] // key_block)
    def _(j):
        at = pl.multiple_of(j * key_block, key_block)
        keys = kv_ref[head, :hd, pl.ds(at, key_block)]
        values = kv_ref[head, hd:, pl.ds(at, key_block)]
        seen = at + lax.broadcasted_iota(jnp.int32, (1, key_block), 1) < offset
        scores = [
            jnp.dot(q_ref[rows(i)], keys, preferred_element_type=jnp.float32)
            for i in range(early)
        ]
        for score, (m_ref, acc_ref) in zip(scores, states):
            score = jnp.where(seen, score, NEG)
            high = jnp.maximum(m_ref[...], jnp.max(score, axis=1, keepdims=True))
            decay = jnp.exp2((m_ref[...] - high) * factor)
            weight = jnp.exp2((score - high) * factor)
            m_ref[...] = high
            acc_ref[...] = acc_ref[...] * decay + mix(weight, values)

    for i in range(span // block):
        low = max(0, (i - early) * block)
        high = (i + 1) * block
        seg_q = seg_rows[rows(i)]
        score = jnp.dot(
            q_ref[rows(i)], qkv_ref[head, 1, :, low:high], preferred_element_type=jnp.float32
        )
        shape = (block, high - low)
        query_at = i * block + lax.broadcasted_iota(jnp.int32, shape, 0)
        key_at = low + lax.broadcasted_iota(jnp.int32, shape, 1)
        seen = (seg_keys[:, low:high] == seg_q) & (key_at <= query_at)
        score = jnp.where(seen, score, NEG)
        values = qkv_ref[head, 2, :, low:high]
        peak = jnp.max(score, axis=1, keepdims=True)
        if i < early:
            m_ref, acc_ref = states[i]
            keep = (seg_q == 0) & (offset > 0)
            before = jnp.where(keep, m_ref[...], NEG)
            peak = jnp.maximum(peak, before)
            decay = jnp.where(keep, jnp.exp2((before - peak) * factor), 0.0)
        weight = jnp.exp2((score - peak) * factor)
        mixed = mix(weight, values)
        if i < early:
            mixed = mixed + acc_ref[...] * decay
        out_ref[rows(i), head * hd : (head + 1) * hd] = (
            mixed[:, :hd] / mixed[:, hd : hd + 1]
        ).astype(out_ref.dtype)


def tail_kernel(
    scale,
    reps,
    offset_ref,
    seg_row,
    dec_attn_ref,
    x_dec_ref,
    up_bias_ref,
    biases_ref,
    gains_ref,
    shifts_ref,
    qkv_hbm,
    kv_hbm,
    x_hbm,
    w_row_hbm,
    w_up_hbm,
    w_down_hbm,
    w_next_hbm,
    result_hbm,
    out_ref,
    dec_out_ref,
    dec_next_ref,
    qkv_ref,
    kv_ref,
    x_ref,
    w_row_ref,
    w_up_ref,
    w_down_ref,
    w_next_ref,
    attn_ref,
    heads_ref,
    columns_ref,
    result_ref,
    slabs,
    parts,
    far,
    near,
    row,
    row_far,
    row_near,
    over_x,
    over_y,
    q_ref,
    m0_ref,
    acc0_ref,
    m1_ref,
    acc1_ref,
    local_sem,
    send_sem,
    recv_sem,
):
    y, x, a, b, device = place()
    loads = []
    for k, (source, target) in enumerate(
        (
            (qkv_hbm, qkv_ref),
            (kv_hbm, kv_ref),
            (w_row_hbm, w_row_ref),
            (x_hbm, x_ref),
            (w_next_hbm, w_next_ref.at[b]),
            (w_up_hbm, w_up_ref),
            (w_down_hbm, w_down_ref),
        )
    ):
        loads.append(pltpu.make_async_copy(source, target, local_sem.at[k]))
        loads[-1].start()
    load_qkv, load_kv, load_row, load_x, load_next, load_up, load_down = loads
    copies = Copies(send_sem, recv_sem)
    rep = lax.axis_index("rep")
    plane, planes = lax.div(rep, 2), reps // 2
    columns, width = w_next_hbm.shape

    greet(
        [SIDE * y + lax.rem(x + k, SIDE) for k in (1, 2, 3)]
        + [SIDE * lax.rem(y + k, SIDE) + x for k in (1, 2, 3)],
        [lax.rem(rep + 2 * k, reps) for k in (1, planes - 1)],
    )
    chunk = (SIDE, ROWS, width)
    load_row.wait()
    dec_sum = SmallSum(copies, over_x.at[0], over_y.at[0])
    dec_sum.begin(
        jnp.dot(dec_attn_ref[...], w_row_ref[b], preferred_element_type=jnp.float32)
    )
    shards = RowRing(
        copies,
        w_next_ref,
        w_next_hbm,
        quarter(width, plane, planes),
        b,
        lambda j: tensor(device(a, j)),
    )
    attn_ref[...] = jnp.zeros_like(attn_ref)
    result_ref[...] = jnp.zeros_like(result_ref)
    load_qkv.wait()
    load_kv.wait()
    state = (m0_ref, acc0_ref, m1_ref, acc1_ref)
    offset = offset_ref[0]
    heads = qkv_ref.shape[0]
    for head in range(heads):
        attend(head, scale, offset, qkv_ref, kv_ref, seg_row, attn_ref, q_ref, state)
        if head == 0:
            dec_sum.middle()
            shards.pass_on()

    def tokens(i, j):
        return attn_ref.at[pl.ds(pl.multiple_of(device(i, j) * ROWS, ROWS), ROWS)]

    swaps = [
        copies.start(tokens(i, b + k), heads_ref.at[b, i], tensor(device(a, b + k)))
        for k in (2, 1, 3)
        for i in range(SIDE)
    ]
    for i in range(SIDE):
        heads_ref[b, i] = tokens(i, b)[...]
    for swap in swaps:
        swap.wait_recv()
    ring = RingSum(
        copies, row.at[0], row_far.at[0], row_near.at[0], a, lambda i: tensor(device(i, b))
    )
    depth = w_row_ref.shape[1]
    step = width // 5
    for n in range(0, width, step):
        total = sum(
            jnp.dot(
                heads_ref[j].reshape(SIDE * ROWS, heads_ref.shape[3])[:, :depth],
                w_row_ref[j, :, n : n + step],
                preferred_element_type=jnp.float32,
            )
            for j in range(SIDE)
        )
        row[0, :, :, n : n + step] = total.astype(jnp.bfloat16).reshape(SIDE, ROWS, step)
    ring.send_far()
    ring.send_next()
    ring.send_prev()
    ring.pass_on()
    shards.finish()
    levels = Levels(copies, rep, reps)
    for k in (1, 2, 3):
        levels.spread(w_next_ref.at[lax.rem(b + k, SIDE)])
    dec_first = layer_norm(
        x_dec_ref[...].astype(jnp.float32) + dec_sum.finish() + biases_ref[0:1],
        gains_ref[0:1],
        shifts_ref[0:1],
    ).astype(jnp.bfloat16)
    own = row[0, a].astype(jnp.float32)
    load_x.wait()
    attn_sum = ring.finish(own)
    first = layer_norm(
        x_ref[...].astype(jnp.float32) + attn_sum + biases_ref[0:1], gains_ref[0:1], shifts_ref[0:1]
    ).astype(jnp.bfloat16)

    def slab(i, j):
        return slabs.at[lax.rem(i, SIDE), lax.rem(j, SIDE)]

    slab(a, b)[...] = first
    gather = Gather(copies, slab)
    gather.begin()
    load_up.wait()
    load_down.wait()

    def mlp(value):
        inner = jnp.dot(value, w_up_ref[...], preferred_element_type=jnp.float32)
        inner = inner + up_bias_ref[...][None, :]
        hidden = (0.5 * inner * (1.0 + lax.erf(inner * 0.7071067811865476))).astype(jnp.bfloat16)
        return jnp.dot(hidden, w_down_ref[...], preferred_element_type=jnp.float32)

    def mlp_share(i):
        at = lax.rem(i, SIDE)
        parts[at] = (
            mlp(slabs[at].reshape(SIDE * ROWS, width)).astype(jnp.bfloat16).reshape(chunk)
        )

    scatter = Scatter(copies, parts, far, near, row.at[1], row_far.at[1], row_near.at[1])
    gather.first()
    mlp_share(a)
    dec_sum = SmallSum(copies, over_x.at[1], over_y.at[1])
    dec_sum.begin(mlp(dec_first))
    gather.middle()
    mlp_share(a + 1)
    mlp_share(a + 3)
    scatter.send_near()
    gather.last()
    mlp_share(a + 2)
    scatter.send_far()
    levels.pass_on()
    scatter.pass_on()
    dec_sum.middle()
    mlp_sum = scatter.finish()
    second = layer_norm(
        first.astype(jnp.float32) + mlp_sum + biases_ref[1:2], gains_ref[1:2], shifts_ref[1:2]
    ).astype(jnp.bfloat16)
    out_ref[...] = second
    columns_ref[a] = second
    RingGather(copies, columns_ref, a, lambda i: tensor(device(i, b))).run()
    levels.finish()
    load_next.wait()
    keeps = []
    for k in (2, 1, 3, 0):
        j = lax.rem(b + k, SIDE)
        result_ref[j, :, :, :columns] = (
            lax.dot_general(
                columns_ref[...].reshape(SIDE * ROWS, width),
                w_next_ref[j],
                NT,
                preferred_element_type=jnp.float32,
            )
            .astype(jnp.bfloat16)
            .reshape(SIDE, ROWS, columns)
        )
        for i in range(SIDE):
            source, target = result_ref.at[j, i], result_hbm.at[device(i, b)]
            if k:
                keeps.append(copies.start(source, target, tensor(device(a, j))))
            else:
                local = pltpu.make_async_copy(source, target, local_sem.at[i])
                local.start()
                loads.append(local)
    dec_out = layer_norm(
        dec_first.astype(jnp.float32) + dec_sum.finish() + biases_ref[1:2],
        gains_ref[1:2],
        shifts_ref[1:2],
    ).astype(jnp.bfloat16)
    dec_out_ref[...] = dec_out
    dec_next_ref[...] = lax.dot_general(
        dec_out, w_next_ref[b], NT, preferred_element_type=jnp.float32
    ).astype(jnp.bfloat16)
    for copy in keeps:
        copy.wait_recv()
    for local in loads[-SIDE:]:
        local.wait()
    copies.drain()


def layout_kernel(
    result_ref, own_ref, dec_ref, dec_result_ref, next_ref, out_ref, dec_out_ref, dec_next_ref
):
    columns, lanes = next_ref.shape[0], result_ref.shape[2]
    same = lax.broadcasted_iota(jnp.int32, (columns, lanes), 0) == lax.broadcasted_iota(
        jnp.int32, (columns, lanes), 1
    )
    next_ref[...] = lax.dot_general(
        same.astype(jnp.float32).astype(jnp.bfloat16),
        result_ref[...].reshape(SIDE * ROWS, lanes),
        NT,
        preferred_element_type=jnp.float32,
    ).astype(next_ref.dtype)

    @pl.when(pl.program_id(0) == 0)
    def _():
        out_ref[...] = own_ref[...]
        dec_out_ref[...] = dec_ref[...]
        dec_next_ref[...] = dec_result_ref[...]


def per_device(
    reps,
    x_pre,
    x_dec,
    prefix_kv,
    cache_kv,
    dec_len,
    offsets,
    segments,
    w_qkv,
    w_out,
    w_up,
    up_bias,
    w_down,
    biases,
    gains,
    shifts,
    w_next,
):
    heads = prefix_kv.shape[2]
    hd = prefix_kv.shape[3] // 2
    span = segments.shape[1]
    width = x_pre.shape[1]
    decodes = x_dec.shape[0]
    columns = w_qkv.shape[1]
    units = w_up.shape[1]
    scale = hd ** (-0.5)
    bf16, f32 = jnp.bfloat16, jnp.float32
    shape = jax.ShapeDtypeStruct
    whole = pl.BlockSpec(memory_space=VMEM)
    scalars = pl.BlockSpec(memory_space=pltpu.SMEM)
    anywhere = pl.BlockSpec(memory_space=pltpu.HBM)
    group = SIDE * SIDE

    cache_t = cache_kv.transpose(0, 2, 3, 1)
    n_copies = 16 + reps - 1 + 6 + (SIDE - 1) * 4
    qkv_t, dec_attn, w_row = pl.pallas_call(
        functools.partial(project_kernel, reps, scale),
        out_shape=(
            shape((columns, span), bf16),
            shape((decodes, heads * hd), bf16),
            shape((SIDE,) + w_out.shape, bf16),
        ),
        in_specs=[scalars, whole] + [anywhere] * 4,
        out_specs=(whole, whole, anywhere),
        scratch_shapes=[
            VMEM((group, ROWS, width), bf16),
            VMEM((128, width), bf16),
            VMEM((columns, width), bf16),
            VMEM(cache_t.shape, bf16),
            VMEM((reps, heads, hd + 16, 128), f32),
            pltpu.SemaphoreType.DMA((4,)),
            pltpu.SemaphoreType.DMA((n_copies,)),
            pltpu.SemaphoreType.DMA((n_copies,)),
        ],
        compiler_params=pltpu.CompilerParams(
            collective_id=0, has_side_effects=True, vmem_limit_bytes=62 << 20
        ),
        name="project",
    )(dec_len, x_dec, x_pre, w_qkv.T, cache_t, w_out)

    n_copies = 100
    lanes = 512
    result, own, dec_own, dec_result = pl.pallas_call(
        functools.partial(tail_kernel, scale, reps),
        out_shape=(
            shape((group, ROWS, lanes), bf16),
            shape((ROWS, width), bf16),
            shape((decodes, width), bf16),
            shape((decodes, columns), bf16),
        ),
        in_specs=[scalars] + [whole] * 7 + [anywhere] * 7,
        out_specs=(anywhere, whole, whole, whole),
        scratch_shapes=[
            VMEM((heads, 3, hd, span), bf16),
            VMEM((heads, 2 * hd, prefix_kv.shape[1]), bf16),
            VMEM((ROWS, width), bf16),
            VMEM((SIDE,) + w_out.shape, bf16),
            VMEM((width, units), bf16),
            VMEM((units, width), bf16),
            VMEM((SIDE, columns, width), bf16),
            VMEM((span, 256), bf16),
            VMEM((SIDE, SIDE, ROWS, 256), bf16),
            VMEM((SIDE, ROWS, width), bf16),
            VMEM((SIDE, SIDE, ROWS, lanes), bf16),
            VMEM((SIDE, SIDE, ROWS, width), bf16),
            VMEM((SIDE, SIDE, ROWS, width), bf16),
            VMEM((2, 2, ROWS, width), bf16),
            VMEM((2, SIDE, ROWS, width), bf16),
            VMEM((2, SIDE, ROWS, width), bf16),
            VMEM((2, 2, ROWS // 2, width), bf16),
            VMEM((2, 2, ROWS, width), bf16),
            VMEM((2, SIDE, decodes, width), bf16),
            VMEM((2, SIDE, decodes, width), bf16),
            VMEM((span, hd), bf16),
            *([VMEM((256, 1), f32), VMEM((256, hd + 16), f32)] * 2),
            pltpu.SemaphoreType.DMA((8,)),
            pltpu.SemaphoreType.DMA((n_copies,)),
            pltpu.SemaphoreType.DMA((n_copies,)),
        ],
        compiler_params=pltpu.CompilerParams(
            collective_id=1, has_side_effects=True, vmem_limit_bytes=62 << 20
        ),
        name="tail",
    )(
        offsets,
        segments,
        dec_attn,
        x_dec,
        up_bias,
        biases,
        gains,
        shifts,
        qkv_t.reshape(heads, 3, hd, span),
        prefix_kv[0].transpose(1, 2, 0),
        x_pre,
        w_row,
        w_up,
        w_down,
        w_next.T,
    )

    next_t, layer_out, dec_out, dec_next = pl.pallas_call(
        layout_kernel,
        grid=(SIDE,),
        out_shape=(
            shape((columns, span), bf16),
            shape((ROWS, width), bf16),
            shape((decodes, width), bf16),
            shape((decodes, columns), bf16),
        ),
        in_specs=[
            pl.BlockSpec((SIDE, ROWS, lanes), lambda i: (i, 0, 0)),
            pl.BlockSpec((ROWS, width), lambda i: (0, 0)),
            pl.BlockSpec((decodes, width), lambda i: (0, 0)),
            pl.BlockSpec((decodes, columns), lambda i: (0, 0)),
        ],
        out_specs=(
            pl.BlockSpec((columns, SIDE * ROWS), lambda i: (0, i)),
            pl.BlockSpec((ROWS, width), lambda i: (0, 0)),
            pl.BlockSpec((decodes, width), lambda i: (0, 0)),
            pl.BlockSpec((decodes, columns), lambda i: (0, 0)),
        ),
        compiler_params=pltpu.CompilerParams(
            dimension_semantics=("arbitrary",), vmem_limit_bytes=62 << 20
        ),
        name="layout",
    )(result, own, dec_own, dec_result)
    return layer_out, next_t.T, dec_out, dec_next


def solution(mesh):
    placed = (
        P(("rep", "tensor"), None),
        P(),
        P("rep", None, "tensor", None),
        P(None, "rep", "tensor", None),
        P(),
        P("rep"),
        P("rep", None),
        P(None, "tensor"),
        P("tensor", None),
        P(None, "tensor"),
        P("tensor"),
        P("tensor", None),
        P(),
        P(),
        P(),
        P(None, "tensor"),
    )
    return jax.shard_map(
        functools.partial(per_device, mesh.shape["rep"]),
        mesh=mesh,
        in_specs=placed,
        out_specs=(P(("rep", "tensor"), None), P("rep", "tensor"), P(), P(None, "tensor")),
        check_vma=False,
    )
```
